256 devices in a mesh: gx: 4 (over x), gy: 4 (over y), gz: 16 (over z, core).
Axes of the slice: x: 4, y: 4, z: 8, core: 2. Of those that a mesh axis runs over, the one named last changes fastest.
Arguments:
- incidence: int32 [4, 4, 16, 16, 16, 8, 128], P('gx', 'gy', 'gz'), may hold values from 0 to 1, as said below
- live_counts: int32 [4, 4, 16, 16], P('gx', 'gy', 'gz'), may hold values from 1 to 16, as said below
- lame_first: float32 [4, 4, 16, 16, 16], P('gx', 'gy', 'gz'), may hold values from 0.5 to 2
- shear_modulus: float32 [4, 4, 16, 16, 16], P('gx', 'gy', 'gz'), may hold values from 0.5 to 4.5
- stretch: float32 [3, 4, 4, 16, 16, 16], P(None, 'gx', 'gy', 'gz'), may hold values from 0.5 to 2
Outputs:
- stiffness: float32 [4, 4, 16, 3, 128, 3, 128], P('gx', 'gy', 'gz')
The draws below stay inside these ranges and needn't reach their ends.
Inputs may be any that keep to these rules, and one draw needn't show every extreme that they name: `incidence`: each element slot names 8 distinct nodes of the tile, some corners replaced by all-zero rows; corner 0 of every slot is always present. `live_counts`: among the 16 tiles of one element block and one node block, at least one has exactly 16 live slots.
All inputs are finite; a program needn't handle non-finite values.
Results may differ from the reference program's by a relative error of at most 0.000059.
Values sent between devices are 32-bit elements; how exact they have to be, the bound alone decides.
A program may use at most 64 MiB of HBM per device.

```python
import math
import jax
import jax.numpy as jnp
import numpy as np
from jax import lax

TILE = 128
CAP = 16
NTB = 16
N_GX = 4
N_GY = 4
N_GZ = 16


def draw_incidence(key, part):
    base_shape = (N_GX, N_GY, N_GZ, NTB, CAP)
    key_order = jax.random.fold_in(key, 11)
    key_keep = jax.random.fold_in(key, 12)
    scores = jax.random.randint(key_order, base_shape + (TILE,), 0, 2 ** 20) * TILE + lax.broadcasted_iota(jnp.int32, base_shape + (TILE,), 5)
    node_ids = jnp.argsort(scores, axis=5)[..., :8].astype(jnp.int32)
    keeping = jax.random.randint(key_keep, base_shape + (8,), 0, 4) > 0
    corner_iota = lax.broadcasted_iota(jnp.int32, base_shape + (8,), 5)
    keeping = keeping | (corner_iota == 0)
    chosen = jnp.where(keeping, node_ids, -1)
    node_range = lax.broadcasted_iota(jnp.int32, base_shape + (8, TILE), 6)
    return (chosen[..., None] == node_range).astype(jnp.int32)


def draw_live_counts(key, part):
    shape_counts = (N_GX, N_GY, N_GZ, NTB)
    drawn = jax.random.randint(jax.random.fold_in(key, 21), shape_counts, 1, CAP // 2 + 1)
    summed = lax.broadcasted_iota(jnp.int32, shape_counts, 0) + lax.broadcasted_iota(jnp.int32, shape_counts, 1) + lax.broadcasted_iota(jnp.int32, shape_counts, 2)
    full_tile = lax.broadcasted_iota(jnp.int32, shape_counts, 3) == summed % NTB
    return jnp.where(full_tile, CAP, drawn).astype(jnp.int32)


def draw_shear_modulus(key, part):
    shape_values = (N_GX, N_GY, N_GZ, NTB, CAP)
    uniform_draw = jax.random.uniform(jax.random.fold_in(key, 31), shape_values, jnp.float32)
    base_values = jnp.exp(jnp.log(0.5) + uniform_draw * (jnp.log(1.5) - jnp.log(0.5)))
    ranking = (lax.broadcasted_iota(jnp.int32, shape_values, 0) * N_GY + lax.broadcasted_iota(jnp.int32, shape_values, 1)) * N_GZ + lax.broadcasted_iota(jnp.int32, shape_values, 2)
    rising = 1.0 + 2.0 * ranking.astype(jnp.float32) / max(N_GX * N_GY * N_GZ - 1, 1)
    return (base_values * rising).astype(jnp.float32)


def levels(stream_key, extent, shards, low, largest):
    loudness, own = 1.0, jax.random.fold_in(stream_key, 6)
    for axis_at, parts in shards:
        heights = jnp.exp(jax.random.uniform(jax.random.fold_in(own, axis_at), (parts,), jnp.float32, low / len(shards), largest / len(shards)))
        loudness = loudness * jnp.repeat(heights, extent[axis_at] // parts).reshape([-1 if axis == axis_at else 1 for axis in range(len(extent))])
    return loudness


def setup_inputs(seed: int = 0) -> dict:
    splits = jax.random.split(jax.random.key(seed), 6)
    return {
        "incidence": draw_incidence(jax.random.fold_in(splits[5], 71), 0),
        "live_counts": draw_live_counts(jax.random.fold_in(splits[5], 71), 0),
        "lame_first": jnp.clip(jnp.exp(math.log(2.0) - 1.3862944 * jax.random.uniform(splits[2], (N_GX, N_GY, N_GZ, NTB, CAP), jnp.float32) ** levels(splits[2], (N_GX, N_GY, N_GZ, NTB, CAP), ((0, 4), (1, 4), (2, 16)), -0.2, 0.2)), 0.5, 2.0),
        "shear_modulus": draw_shear_modulus(jax.random.fold_in(splits[5], 71), 0),
        "stretch": jnp.clip(jnp.exp(math.log(2.0) - 1.3862944 * jax.random.uniform(splits[4], (3, N_GX, N_GY, N_GZ, NTB, CAP), jnp.float32) ** levels(splits[4], (3, N_GX, N_GY, N_GZ, NTB, CAP), ((1, 4), (2, 4), (3, 16)), -0.2, 0.2)), 0.5, 2.0),
    }


def corner_table():
    corner_signs = np.array([[sign_x, sign_y, sign_z] for sign_z in (-1.0, 1.0) for sign_y in (-1.0, 1.0) for sign_x in (-1.0, 1.0)])
    gauss_points = corner_signs / math.sqrt(3.0)
    shape_grads = np.zeros((8, 8, 3))
    for gauss_index in range(8):
        for corner_index in range(8):
            for axis_index in range(3):
                product_value = corner_signs[corner_index, axis_index] / 8.0
                for other_axis in range(3):
                    if other_axis != axis_index:
                        product_value = product_value * (1.0 + corner_signs[corner_index, other_axis] * gauss_points[gauss_index, other_axis])
                shape_grads[gauss_index, corner_index, axis_index] = product_value
    table_values = np.zeros((8, 3, 8, 3))
    for gauss_index in range(8):
        for first_corner in range(8):
            for first_axis in range(3):
                for second_corner in range(8):
                    for second_axis in range(3):
                        table_values[first_corner, first_axis, second_corner, second_axis] += shape_grads[gauss_index, first_corner, first_axis] * shape_grads[gauss_index, second_corner, second_axis]
    return table_values

def element_matrices(first_param, shear_values, lengths):
    inverse = 2.0 / lengths
    scaling = inverse[:, None, :] * inverse[None, :, :]
    volume = lengths[0] * lengths[1] * lengths[2] / 8.0
    ref_table = jnp.asarray(corner_table(), jnp.float32)
    coupled = ref_table[None] * jnp.transpose(scaling, (2, 0, 1))[:, None, :, None, :]
    contracted = coupled[:, :, 0, :, 0] + coupled[:, :, 1, :, 1] + coupled[:, :, 2, :, 2]
    unit_matrix = jnp.eye(3, dtype=jnp.float32)
    matrices = first_param[:, None, None, None, None] * coupled + shear_values[:, None, None, None, None] * (contracted[:, :, None, :, None] * unit_matrix[None, None, :, None, :] + jnp.transpose(coupled, (0, 1, 4, 3, 2)))
    return matrices * volume[:, None, None, None, None]

def assemble_block(matrices, onehot):
    spread = jnp.einsum('epiqj,eqb->epijb', matrices, onehot, precision=lax.Precision.HIGHEST)
    return jnp.einsum('epa,epijb->iajb', onehot, spread, precision=lax.Precision.HIGHEST)

def reference(incidence, live_counts, lame_first, shear_modulus, stretch):
    tile_total = N_GX * N_GY * NTB
    slot_total = N_GZ * CAP
    onehot_all = jnp.transpose(incidence, (0, 1, 3, 2, 4, 5, 6)).reshape(tile_total, slot_total, 8, TILE)
    live_mask = (jnp.arange(CAP, dtype=jnp.int32)[None, None, None, None, :] < live_counts[..., None]).astype(jnp.float32)

    def regroup(values):
        return jnp.transpose(values, (0, 1, 3, 2, 4)).reshape(tile_total, slot_total)
    stretch_all = jnp.transpose(stretch, (1, 2, 4, 3, 5, 0)).reshape(tile_total, slot_total, 3)

    def one_tile(packed):
        onehot, alive_mask, first_param, shear_values, lengths = packed
        matrices = element_matrices(first_param, shear_values, lengths.T) * alive_mask[:, None, None, None, None]
        return assemble_block(matrices, onehot.astype(jnp.float32))
    blocks = lax.map(one_tile, (onehot_all, regroup(live_mask), regroup(lame_first), regroup(shear_modulus), stretch_all))
    flattened = blocks.reshape(tile_total, 3 * TILE, 3 * TILE)
    grand_total = jnp.sum(jnp.trace(flattened, axis1=1, axis2=2))
    mean_diag = grand_total / (3 * TILE * tile_total)
    return (blocks / mean_diag).reshape(N_GX, N_GY, NTB, 3, TILE, 3, TILE)
```

```python
import functools

import jax
import jax.numpy as jnp
from jax import lax
from jax.experimental import pallas as pl
from jax.experimental.pallas import tpu as pltpu
from jax.sharding import PartitionSpec as P

MESH = pl.DeviceIdType.MESH
F32, BF16 = jnp.float32, jnp.bfloat16
TILE, CAP, CORNERS = 128, 16, 8

ALL_MODES = (1, 2, 4, 3, 5, 6, 7)


def split(value):
    high = value.astype(BF16)
    return high, (value - high.astype(F32)).astype(BF16)


def swap_groups(values):
    sub = lax.broadcasted_iota(jnp.int32, (8, 128), 0)
    group = lax.broadcasted_iota(jnp.int32, (8, 128), 1) // CAP
    for bit in (1, 2, 4):
        upper_sub = (sub & bit) != 0
        upper_group = (group & bit) != 0
        below = pltpu.roll(pltpu.roll(values, 8 - bit, 0), CAP * bit, 1)
        above = pltpu.roll(pltpu.roll(values, bit, 0), 128 - CAP * bit, 1)
        values = jnp.where(
            upper_sub == upper_group, values, jnp.where(upper_sub, above, below)
        )
    return values


def kernel(
    n_x, n_y, n_z,
    live_hbm, inc_hbm, lame_hbm, shear_hbm, stretch_hbm,
    block_ref, scale_ref,
    live, inc, lame, shear, stretch, nodes, params, send, recv, plane, plane_recv, line, line_recv,
    in_sem, small_sem, send_sem, recv_sem, plane_send_sem, plane_sem, line_send_sem, line_sem,
):
    n_tiles = send.shape[0]
    my_x, my_y, my_z = lax.axis_index("gx"), lax.axis_index("gy"), lax.axis_index("gz")
    n_xy = n_x * n_y
    my_xy = my_x * n_y + my_y

    chunks = in_sem.shape[0]
    rows = inc.shape[0] // chunks
    loads = [
        pltpu.make_async_copy(
            inc_hbm.at[pl.ds(c * rows, rows)], inc.at[pl.ds(c * rows, rows)], in_sem.at[c]
        )
        for c in range(chunks)
    ]
    small = [
        pltpu.make_async_copy(source, target, small_sem.at[k])
        for k, (source, target) in enumerate(
            ((live_hbm, live), (lame_hbm, lame), (shear_hbm, shear), (stretch_hbm, stretch))
        )
    ]
    for copy in small + loads:
        copy.start()

    barrier = pltpu.get_barrier_semaphore()

    @pl.loop(1, n_z)
    def _(step):
        pl.semaphore_signal(
            barrier, inc=1, device_id={"gz": lax.rem(my_z + step, n_z)}, device_id_type=MESH
        )

    @pl.loop(1, n_xy)
    def _(step):
        other = lax.rem(my_xy + step, n_xy)
        pl.semaphore_signal(
            barrier,
            inc=1,
            device_id={"gx": other // n_y, "gy": lax.rem(other, n_y)},
            device_id_type=MESH,
        )

    for copy in small:
        copy.wait()
    params[...] = jnp.zeros_like(params)
    first, second = lame[...], shear[...]
    lengths = [stretch[k] for k in range(3)]
    for k, value in enumerate([first, second] + lengths):
        params[:, k * CAP : (k + 1) * CAP] = value
    send[:, 1, :] = params[...]
    inverse = [1.0 / value for value in lengths]
    trace = (
        (lengths[0] * lengths[1] * lengths[2] / 9.0)
        * (first + 4.0 * second)
        * (inverse[0] * inverse[0] + inverse[1] * inverse[1] + inverse[2] * inverse[2])
    )
    trace = jnp.concatenate([trace] * CORNERS, axis=1)

    number = (lax.broadcasted_iota(jnp.int32, (TILE, TILE), 0) + 1).astype(F32).astype(BF16)
    row = lax.broadcasted_iota(jnp.int32, (TILE, TILE), 0)
    lane = lax.broadcasted_iota(jnp.int32, (TILE, TILE), 1)
    place = lane == (row % CORNERS) * CAP + row // CORNERS
    slot = lax.broadcasted_iota(jnp.int32, (1, TILE), 1) % CAP
    per_chunk = n_tiles // chunks
    for t in range(n_tiles):
        if t % per_chunk == 0:
            loads[t // per_chunk].wait()
        onehot = inc[t * TILE : (t + 1) * TILE, :].astype(F32).astype(BF16)
        spread = jnp.dot(onehot, number, preferred_element_type=F32)
        ids = jnp.sum(jnp.where(place, spread, 0.0), axis=0, keepdims=True)
        ids = jnp.where(slot < live[0, t], ids, 0.0)
        send[t, 0:1, :] = ids
        nodes[t : t + 1, :] = ids
    partial = jnp.sum(jnp.where(nodes[...] > 0.0, trace, 0.0), axis=0, keepdims=True)
    plane[...] = jnp.broadcast_to(jnp.sum(partial, axis=1, keepdims=True), (1, TILE))

    pl.semaphore_wait(barrier, (n_z - 1) + (n_xy - 1))

    def to_plane(step):
        other = lax.rem(my_xy + step, n_xy)
        return pltpu.make_async_remote_copy(
            src_ref=plane,
            dst_ref=plane_recv.at[my_xy],
            send_sem=plane_send_sem.at[step],
            recv_sem=plane_sem.at[my_xy],
            device_id={"gx": other // n_y, "gy": lax.rem(other, n_y)},
            device_id_type=MESH,
        )

    def to_tile(step):
        other = lax.rem(my_z + step, n_z)
        return pltpu.make_async_remote_copy(
            src_ref=send.at[other],
            dst_ref=recv.at[my_z],
            send_sem=send_sem.at[step],
            recv_sem=recv_sem.at[my_z],
            device_id={"gz": other},
            device_id_type=MESH,
        )

    def to_line(step):
        other = lax.rem(my_z + step, n_z)
        return pltpu.make_async_remote_copy(
            src_ref=line,
            dst_ref=line_recv.at[my_z],
            send_sem=line_send_sem.at[step],
            recv_sem=line_sem.at[my_z],
            device_id={"gz": other},
            device_id_type=MESH,
        )

    def await_from(target, sems, source, device):
        pltpu.make_async_remote_copy(
            src_ref=target.at[source],
            dst_ref=target.at[source],
            send_sem=sems.at[source],
            recv_sem=sems.at[source],
            device_id=device,
            device_id_type=MESH,
        ).wait_recv()

    @pl.loop(1, n_xy)
    def _(step):
        to_plane(step).start()

    @pl.loop(1, n_z)
    def _(step):
        to_tile(step).start()

    recv[my_z] = send[my_z]
    plane_recv[my_xy] = plane[...]

    @pl.loop(1, n_xy)
    def _(step):
        other = lax.rem(my_xy + step, n_xy)
        await_from(plane_recv, plane_sem, other, {"gx": other // n_y, "gy": lax.rem(other, n_y)})

    total = plane_recv[0]
    for k in range(1, n_xy):
        total = total + plane_recv[k]
    line[...] = total
    line_recv[my_z] = total

    @pl.loop(1, n_z)
    def _(step):
        to_line(step).start()

    @pl.loop(1, n_z)
    def _(step):
        other = lax.rem(my_z + step, n_z)
        await_from(recv, recv_sem, other, {"gz": other})

    halves = range(n_z // 8)
    ids = jnp.concatenate([swap_groups(recv[8 * h : 8 * h + 8, 0, :]) for h in halves], axis=1)
    material = jnp.concatenate(
        [swap_groups(recv[8 * h : 8 * h + 8, 1, :]) for h in halves], axis=1
    )
    wide = ids.shape[1]
    first, second = material[0:1], material[1:2]
    h = [material[2 + k : 3 + k] for k in range(3)]

    node = (lax.broadcasted_iota(jnp.int32, (TILE, wide), 0) + 1).astype(F32)
    corner = [
        jnp.where(node == ids[p : p + 1], 1.0, 0.0).astype(BF16) for p in range(CORNERS)
    ]
    mode = corner
    for bit in (1, 2, 4):
        mode = [
            mode[k] - mode[k ^ bit] if k & bit else mode[k] + mode[k ^ bit]
            for k in range(CORNERS)
        ]

    def scaled(wave, coefficient):
        wide_row = jnp.broadcast_to(coefficient, (16, wide)).astype(BF16)
        return (wave.reshape(TILE // 16, 16, wide) * wide_row[None]).reshape(TILE, wide)

    def product(left, right):
        return lax.dot_general(
            left, right, (((1,), (1,)), ((), ())), preferred_element_type=F32
        )

    def assemble(pairs):
        high, low, other = [], [], []
        for left, right, coefficient in pairs:
            top = coefficient.astype(BF16).astype(F32)
            high.append(scaled(mode[left], top))
            low.append(scaled(mode[left], coefficient - top))
            other.append(mode[right])
        right = jnp.concatenate(other, axis=1)
        left = jnp.concatenate(
            [jnp.concatenate(high, axis=1), jnp.concatenate(low, axis=1)], axis=0
        )
        result = product(left, right)
        return result[:TILE] + result[TILE:]

    area = [h[1] * h[2] / (16.0 * h[0]), h[0] * h[2] / (16.0 * h[1]), h[0] * h[1] / (16.0 * h[2])]
    strong = first + 2.0 * second
    for i in range(3):
        alpha = [(strong if k == i else second) * area[k] for k in range(3)]
        coefficients = {
            1: alpha[0],
            2: alpha[1],
            4: alpha[2],
            3: (alpha[0] + alpha[1]) / 3.0,
            5: (alpha[0] + alpha[2]) / 3.0,
            6: (alpha[1] + alpha[2]) / 3.0,
            7: (alpha[0] + alpha[1] + alpha[2]) / 9.0,
        }
        block_ref[i, i] = assemble([(m, m, coefficients[m]) for m in ALL_MODES])
    for i, j, k in ((0, 1, 2), (0, 2, 1), (1, 2, 0)):
        a, b, c = 1 << i, 1 << j, 1 << k
        la, mu = h[k] * first / 16.0, h[k] * second / 16.0
        result = assemble(
            [
                (a, b, la),
                (a | c, b | c, la / 3.0),
                (b, a, mu),
                (b | c, a | c, mu / 3.0),
            ]
        )
        block_ref[i, j] = result
        block_ref[j, i] = result.T

    @pl.loop(1, n_z)
    def _(step):
        other = lax.rem(my_z + step, n_z)
        await_from(line_recv, line_sem, other, {"gz": other})

    total = line_recv[0]
    for k in range(1, n_z):
        total = total + line_recv[k]
    scale_ref[...] = (3.0 * TILE * n_xy * n_z) / total

    @pl.loop(1, n_xy)
    def _(step):
        to_plane(step).wait_send()

    @pl.loop(1, n_z)
    def _(step):
        to_tile(step).wait_send()
        to_line(step).wait_send()


def solution(mesh):
    n_x, n_y, n_z = mesh.shape["gx"], mesh.shape["gy"], mesh.shape["gz"]
    n_xy = n_x * n_y

    def on_device(incidence, live_counts, lame_first, shear_modulus, stretch):
        n_tiles = incidence.shape[3]
        hbm = pl.BlockSpec(memory_space=pl.ANY)
        vmem = pl.BlockSpec(memory_space=pltpu.VMEM)
        block, scale = pl.pallas_call(
            functools.partial(kernel, n_x, n_y, n_z),
            out_shape=(
                jax.ShapeDtypeStruct((3, 3, TILE, TILE), F32),
                jax.ShapeDtypeStruct((1, TILE), F32),
            ),
            in_specs=[hbm] * 5,
            out_specs=(vmem, vmem),
            scratch_shapes=[
                pltpu.SMEM((1, n_tiles), jnp.int32),
                pltpu.VMEM((n_tiles * CAP * CORNERS, TILE), jnp.int32),
                pltpu.VMEM((n_tiles, CAP), F32),
                pltpu.VMEM((n_tiles, CAP), F32),
                pltpu.VMEM((3, n_tiles, CAP), F32),
                pltpu.VMEM((n_tiles, TILE), F32),
                pltpu.VMEM((n_tiles, TILE), F32),
                pltpu.VMEM((n_z, 2, TILE), F32),
                pltpu.VMEM((n_z, 2, TILE), F32),
                pltpu.VMEM((1, TILE), F32),
                pltpu.VMEM((n_xy, 1, TILE), F32),
                pltpu.VMEM((1, TILE), F32),
                pltpu.VMEM((n_z, 1, TILE), F32),
                pltpu.SemaphoreType.DMA((4,)),
                pltpu.SemaphoreType.DMA((4,)),
                pltpu.SemaphoreType.DMA((n_z,)),
                pltpu.SemaphoreType.DMA((n_z,)),
                pltpu.SemaphoreType.DMA((n_xy,)),
                pltpu.SemaphoreType.DMA((n_xy,)),
                pltpu.SemaphoreType.DMA((n_z,)),
                pltpu.SemaphoreType.DMA((n_z,)),
            ],
            compiler_params=pltpu.CompilerParams(collective_id=0, has_side_effects=True),
        )(
            live_counts.reshape(1, n_tiles),
            incidence.reshape(n_tiles * CAP * CORNERS, TILE),
            lame_first.reshape(n_tiles, CAP),
            shear_modulus.reshape(n_tiles, CAP),
            stretch.reshape(3, n_tiles, CAP),
        )
        block = block * scale.reshape(1, 1, 1, TILE)
        return block.transpose(0, 2, 1, 3).reshape(1, 1, 1, 3, TILE, 3, TILE)

    return jax.shard_map(
        on_device,
        mesh=mesh,
        in_specs=(
            P("gx", "gy", "gz", None, None, None, None),
            P("gx", "gy", "gz", None),
            P("gx", "gy", "gz", None, None),
            P("gx", "gy", "gz", None, None),
            P(None, "gx", "gy", "gz", None, None),
        ),
        out_specs=P("gx", "gy", "gz", None, None, None, None),
        check_vma=False,
    )
```

```python
import functools

import jax
import jax.numpy as jnp
from jax import lax
from jax.experimental import pallas as pl
from jax.experimental.pallas import tpu as pltpu
from jax.sharding import PartitionSpec as P

MESH = pl.DeviceIdType.MESH
F32, BF16 = jnp.float32, jnp.bfloat16
TILE, CAP, CORNERS = 128, 16, 8

ALL_MODES = (1, 2, 4, 3, 5, 6, 7)


def split(value):
    high = value.astype(BF16)
    return high, (value - high.astype(F32)).astype(BF16)


def swap_groups(values):
    sub = lax.broadcasted_iota(jnp.int32, (8, 128), 0)
    group = lax.broadcasted_iota(jnp.int32, (8, 128), 1) // CAP
    for bit in (1, 2, 4):
        upper_sub = (sub & bit) != 0
        upper_group = (group & bit) != 0
        below = pltpu.roll(pltpu.roll(values, 8 - bit, 0), CAP * bit, 1)
        above = pltpu.roll(pltpu.roll(values, bit, 0), 128 - CAP * bit, 1)
        values = jnp.where(
            upper_sub == upper_group, values, jnp.where(upper_sub, above, below)
        )
    return values


def kernel(
    n_x, n_y, n_z,
    live_hbm, inc_hbm, lame_hbm, shear_hbm, stretch_hbm,
    block_ref, scale_ref,
    live, inc, lame, shear, stretch, nodes, params, send, recv, plane_recv, line_recv,
    in_sem, small_sem, send_sem, recv_sem,
):
    n_tiles = send.shape[0]
    my_x, my_y, my_z = lax.axis_index("gx"), lax.axis_index("gy"), lax.axis_index("gz")
    n_xy = n_x * n_y

    chunks = in_sem.shape[0]
    rows = inc.shape[0] // chunks
    loads = [
        pltpu.make_async_copy(
            inc_hbm.at[pl.ds(c * rows, rows)], inc.at[pl.ds(c * rows, rows)], in_sem.at[c]
        )
        for c in range(chunks)
    ]
    small = [
        pltpu.make_async_copy(source, target, small_sem.at[k])
        for k, (source, target) in enumerate(
            ((live_hbm, live), (lame_hbm, lame), (shear_hbm, shear), (stretch_hbm, stretch))
        )
    ]
    for copy in small + loads:
        copy.start()

    at_x = [lax.rem(my_x + k, n_x) for k in range(n_x)]
    at_y = [lax.rem(my_y + k, n_y) for k in range(n_y)]
    at_z = [lax.rem(my_z + k, n_z) for k in range(n_z)]

    def hops(step, size):
        return min(step, size - step)

    plane_steps = sorted(
        ((i, j) for i in range(n_x) for j in range(n_y) if i or j),
        key=lambda step: -hops(step[0], n_x) - hops(step[1], n_y),
    )
    line_steps = sorted(range(1, n_z), key=lambda step: -hops(step, n_z))

    barrier = pltpu.get_barrier_semaphore()
    for i, j in plane_steps:
        pl.semaphore_signal(
            barrier, inc=1, device_id={"gx": at_x[i], "gy": at_y[j]}, device_id_type=MESH
        )
    for step in line_steps:
        pl.semaphore_signal(barrier, inc=1, device_id={"gz": at_z[step]}, device_id_type=MESH)

    for copy in small:
        copy.wait()
    params[...] = jnp.zeros_like(params)
    first, second = lame[...], shear[...]
    lengths = [stretch[k] for k in range(3)]
    for k, value in enumerate([first, second] + lengths):
        params[:, k * CAP : (k + 1) * CAP] = value
    send[:, 1, :] = params[...]
    inverse = [1.0 / value for value in lengths]
    trace = (
        (lengths[0] * lengths[1] * lengths[2] / 9.0)
        * (first + 4.0 * second)
        * (inverse[0] * inverse[0] + inverse[1] * inverse[1] + inverse[2] * inverse[2])
    )
    trace = jnp.concatenate([trace] * CORNERS, axis=1)

    number = (lax.broadcasted_iota(jnp.int32, (TILE, TILE), 0) + 1).astype(F32).astype(BF16)
    row = lax.broadcasted_iota(jnp.int32, (TILE, TILE), 0)
    lane = lax.broadcasted_iota(jnp.int32, (TILE, TILE), 1)
    place = lane == (row % CORNERS) * CAP + row // CORNERS
    slot = lax.broadcasted_iota(jnp.int32, (1, TILE), 1) % CAP
    per_chunk = n_tiles // chunks
    for t in range(n_tiles):
        if t % per_chunk == 0:
            loads[t // per_chunk].wait()
        onehot = inc[t * TILE : (t + 1) * TILE, :].astype(F32).astype(BF16)
        spread = jnp.dot(onehot, number, preferred_element_type=F32)
        ids = jnp.sum(jnp.where(place, spread, 0.0), axis=0, keepdims=True)
        ids = jnp.where(slot < live[0, t], ids, 0.0)
        send[t, 0:1, :] = ids
        nodes[t : t + 1, :] = ids
    partial = jnp.sum(jnp.where(nodes[...] > 0.0, trace, 0.0), axis=0, keepdims=True)
    plane_recv[0] = jnp.broadcast_to(jnp.sum(partial, axis=1, keepdims=True), (1, TILE))

    pl.semaphore_wait(barrier, (n_z - 1) + (n_xy - 1))

    for i, j in plane_steps:
        pltpu.make_async_remote_copy(
            src_ref=plane_recv.at[0],
            dst_ref=plane_recv.at[i * n_y + j],
            send_sem=send_sem.at[0],
            recv_sem=recv_sem.at[0],
            device_id={"gx": at_x[i], "gy": at_y[j]},
            device_id_type=MESH,
        ).start()
    for step in line_steps:
        pltpu.make_async_remote_copy(
            src_ref=send.at[at_z[step]],
            dst_ref=recv.at[step],
            send_sem=send_sem.at[1],
            recv_sem=recv_sem.at[1],
            device_id={"gz": at_z[step]},
            device_id_type=MESH,
        ).start()
    recv[0] = send[my_z]

    def whole(target, kind, device):
        return pltpu.make_async_remote_copy(
            src_ref=target.at[pl.ds(1, target.shape[0] - 1)],
            dst_ref=target.at[pl.ds(1, target.shape[0] - 1)],
            send_sem=send_sem.at[kind],
            recv_sem=recv_sem.at[kind],
            device_id=device,
            device_id_type=MESH,
        )

    plane_all = whole(plane_recv, 0, {"gx": at_x[n_x - 1], "gy": at_y[n_y - 1]})
    tile_all = whole(recv, 1, {"gz": at_z[1]})
    line_all = whole(line_recv, 2, {"gz": at_z[1]})

    plane_all.wait_recv()
    total = plane_recv[0]
    for k in range(1, n_xy):
        total = total + plane_recv[k]
    line_recv[0] = total
    for step in line_steps:
        pltpu.make_async_remote_copy(
            src_ref=line_recv.at[0],
            dst_ref=line_recv.at[step],
            send_sem=send_sem.at[2],
            recv_sem=recv_sem.at[2],
            device_id={"gz": at_z[step]},
            device_id_type=MESH,
        ).start()
    tile_all.wait_recv()

    halves = range(n_z // 8)
    ids = jnp.concatenate([swap_groups(recv[8 * h : 8 * h + 8, 0, :]) for h in halves], axis=1)
    material = jnp.concatenate(
        [swap_groups(recv[8 * h : 8 * h + 8, 1, :]) for h in halves], axis=1
    )
    wide = ids.shape[1]
    first, second = material[0:1], material[1:2]
    h = [material[2 + k : 3 + k] for k in range(3)]

    node = (lax.broadcasted_iota(jnp.int32, (TILE, wide), 0) + 1).astype(F32)
    corner = [
        jnp.where(node == ids[p : p + 1], 1.0, 0.0).astype(BF16) for p in range(CORNERS)
    ]
    mode = corner
    for bit in (1, 2, 4):
        mode = [
            mode[k] - mode[k ^ bit] if k & bit else mode[k] + mode[k ^ bit]
            for k in range(CORNERS)
        ]

    def scaled(wave, coefficient):
        wide_row = jnp.broadcast_to(coefficient, (16, wide)).astype(BF16)
        return (wave.reshape(TILE // 16, 16, wide) * wide_row[None]).reshape(TILE, wide)

    def product(left, right):
        return lax.dot_general(
            left, right, (((1,), (1,)), ((), ())), preferred_element_type=F32
        )

    def assemble(pairs):
        high, low, other = [], [], []
        for left, right, coefficient in pairs:
            top = coefficient.astype(BF16).astype(F32)
            high.append(scaled(mode[left], top))
            low.append(scaled(mode[left], coefficient - top))
            other.append(mode[right])
        right = jnp.concatenate(other, axis=1)
        left = jnp.concatenate(
            [jnp.concatenate(high, axis=1), jnp.concatenate(low, axis=1)], axis=0
        )
        result = product(left, right)
        return result[:TILE] + result[TILE:]

    area = [h[1] * h[2] / (16.0 * h[0]), h[0] * h[2] / (16.0 * h[1]), h[0] * h[1] / (16.0 * h[2])]
    strong = first + 2.0 * second
    for i in range(3):
        alpha = [(strong if k == i else second) * area[k] for k in range(3)]
        coefficients = {
            1: alpha[0],
            2: alpha[1],
            4: alpha[2],
            3: (alpha[0] + alpha[1]) / 3.0,
            5: (alpha[0] + alpha[2]) / 3.0,
            6: (alpha[1] + alpha[2]) / 3.0,
            7: (alpha[0] + alpha[1] + alpha[2]) / 9.0,
        }
        block_ref[i, i] = assemble([(m, m, coefficients[m]) for m in ALL_MODES])
    for i, j, k in ((0, 1, 2), (0, 2, 1), (1, 2, 0)):
        a, b, c = 1 << i, 1 << j, 1 << k
        la, mu = h[k] * first / 16.0, h[k] * second / 16.0
        result = assemble(
            [
                (a, b, la),
                (a | c, b | c, la / 3.0),
                (b, a, mu),
                (b | c, a | c, mu / 3.0),
            ]
        )
        block_ref[i, j] = result
        block_ref[j, i] = result.T

    line_all.wait_recv()
    total = line_recv[0]
    for k in range(1, n_z):
        total = total + line_recv[k]
    scale_ref[...] = (3.0 * TILE * n_xy * n_z) / total
    for copies in (plane_all, tile_all, line_all):
        copies.wait_send()


def solution(mesh):
    n_x, n_y, n_z = mesh.shape["gx"], mesh.shape["gy"], mesh.shape["gz"]
    n_xy = n_x * n_y

    def on_device(incidence, live_counts, lame_first, shear_modulus, stretch):
        n_tiles = incidence.shape[3]
        hbm = pl.BlockSpec(memory_space=pltpu.HBM)
        vmem = pl.BlockSpec(memory_space=pltpu.VMEM)
        block, scale = pl.pallas_call(
            functools.partial(kernel, n_x, n_y, n_z),
            out_shape=(
                jax.ShapeDtypeStruct((3, 3, TILE, TILE), F32),
                jax.ShapeDtypeStruct((1, TILE), F32),
            ),
            in_specs=[hbm] * 5,
            out_specs=(vmem, vmem),
            scratch_shapes=[
                pltpu.SMEM((1, n_tiles), jnp.int32),
                pltpu.VMEM((n_tiles * CAP * CORNERS, TILE), jnp.int32),
                pltpu.VMEM((n_tiles, CAP), F32),
                pltpu.VMEM((n_tiles, CAP), F32),
                pltpu.VMEM((3, n_tiles, CAP), F32),
                pltpu.VMEM((n_tiles, TILE), F32),
                pltpu.VMEM((n_tiles, TILE), F32),
                pltpu.VMEM((n_z, 2, TILE), F32),
                pltpu.VMEM((n_z, 2, TILE), F32),
                pltpu.VMEM((n_xy, 1, TILE), F32),
                pltpu.VMEM((n_z, 1, TILE), F32),
                pltpu.SemaphoreType.DMA((8,)),
                pltpu.SemaphoreType.DMA((4,)),
                pltpu.SemaphoreType.DMA((3,)),
                pltpu.SemaphoreType.DMA((3,)),
            ],
            compiler_params=pltpu.CompilerParams(
                collective_id=0, has_side_effects=True, vmem_limit_bytes=24 << 20
            ),
        )(
            *(
                pltpu.with_memory_space_constraint(value, pltpu.HBM)
                for value in (
                    live_counts.reshape(1, n_tiles),
                    incidence.reshape(n_tiles * CAP * CORNERS, TILE),
                    lame_first.reshape(n_tiles, CAP),
                    shear_modulus.reshape(n_tiles, CAP),
                    stretch.reshape(3, n_tiles, CAP),
                )
            )
        )
        block = block * scale.reshape(1, 1, 1, TILE)
        return block.transpose(0, 2, 1, 3).reshape(1, 1, 1, 3, TILE, 3, TILE)

    return jax.shard_map(
        on_device,
        mesh=mesh,
        in_specs=(
            P("gx", "gy", "gz", None, None, None, None),
            P("gx", "gy", "gz", None),
            P("gx", "gy", "gz", None, None),
            P("gx", "gy", "gz", None, None),
            P(None, "gx", "gy", "gz", None, None),
        ),
        out_specs=P("gx", "gy", "gz", None, None, None, None),
        check_vma=False,
    )
```

```python
import functools

import jax
import jax.numpy as jnp
from jax import lax
from jax.experimental import pallas as pl
from jax.experimental.pallas import tpu as pltpu
from jax.sharding import PartitionSpec as P

MESH = pl.DeviceIdType.MESH
F32, BF16 = jnp.float32, jnp.bfloat16
TILE, CAP, CORNERS = 128, 16, 8

HUB = (0, 0, 1)

ALL_MODES = (1, 2, 4, 3, 5, 6, 7)


def split(value):
    high = value.astype(BF16)
    return high, (value - high.astype(F32)).astype(BF16)


def swap_groups(values):
    sub = lax.broadcasted_iota(jnp.int32, (8, 128), 0)
    group = lax.broadcasted_iota(jnp.int32, (8, 128), 1) // CAP
    for bit in (1, 2, 4):
        upper_sub = (sub & bit) != 0
        upper_group = (group & bit) != 0
        below = pltpu.roll(pltpu.roll(values, 8 - bit, 0), CAP * bit, 1)
        above = pltpu.roll(pltpu.roll(values, bit, 0), 128 - CAP * bit, 1)
        values = jnp.where(
            upper_sub == upper_group, values, jnp.where(upper_sub, above, below)
        )
    return values


def kernel(
    n_x, n_y, n_z,
    live_hbm, inc_hbm, lame_hbm, shear_hbm, stretch_hbm,
    block_ref, scale_ref,
    live, inc, lame, shear, stretch, nodes, params, send, recv, plane_recv, line_recv,
    hub_recv,
    in_sem, small_sem, send_sem, recv_sem,
):
    n_tiles = send.shape[0]
    my_x, my_y, my_z = lax.axis_index("gx"), lax.axis_index("gy"), lax.axis_index("gz")
    n_xy = n_x * n_y

    chunks = in_sem.shape[0]
    rows = inc.shape[0] // chunks
    loads = [
        pltpu.make_async_copy(
            inc_hbm.at[pl.ds(c * rows, rows)], inc.at[pl.ds(c * rows, rows)], in_sem.at[c]
        )
        for c in range(chunks)
    ]
    small = [
        pltpu.make_async_copy(source, target, small_sem.at[k])
        for k, (source, target) in enumerate(
            ((live_hbm, live), (lame_hbm, lame), (shear_hbm, shear), (stretch_hbm, stretch))
        )
    ]
    for copy in small + loads:
        copy.start()

    at_x = [lax.rem(my_x + k, n_x) for k in range(n_x)]
    at_y = [lax.rem(my_y + k, n_y) for k in range(n_y)]
    at_z = [lax.rem(my_z + k, n_z) for k in range(n_z)]

    def hops(step, size):
        return min(step, size - step)

    plane_steps = sorted(
        ((i, j) for i in range(n_x) for j in range(n_y) if i or j),
        key=lambda step: -hops(step[0], n_x) - hops(step[1], n_y),
    )
    line_steps = sorted(range(1, n_z), key=lambda step: -hops(step, n_z))

    barrier = pltpu.get_barrier_semaphore()
    for i, j in plane_steps:
        pl.semaphore_signal(
            barrier, inc=1, device_id={"gx": at_x[i], "gy": at_y[j]}, device_id_type=MESH
        )
    for step in line_steps:
        pl.semaphore_signal(barrier, inc=1, device_id={"gz": at_z[step]}, device_id_type=MESH)

    hub_x, hub_y, hub_z = HUB
    hub_line = jnp.logical_and(my_x == hub_x, my_y == hub_y)
    is_hub = jnp.logical_and(hub_line, my_z == hub_z)

    @pl.when(is_hub)
    def _():
        @pl.loop(0, n_xy)
        def _(step):
            far = lax.rem(step + n_xy // 2 + n_y // 2, n_xy)
            target = {"gx": lax.rem(hub_x + far // n_y, n_x), "gy": lax.rem(hub_y + far, n_y)}
            for k in line_steps:
                pl.semaphore_signal(
                    barrier,
                    inc=1,
                    device_id=target | {"gz": (hub_z + k) % n_z},
                    device_id_type=MESH,
                )

            @pl.when(far > 0)
            def _():
                pl.semaphore_signal(
                    barrier, inc=1, device_id=target | {"gz": hub_z}, device_id_type=MESH
                )

    for copy in small:
        copy.wait()
    params[...] = jnp.zeros_like(params)
    first, second = lame[...], shear[...]
    lengths = [stretch[k] for k in range(3)]
    for k, value in enumerate([first, second] + lengths):
        params[:, k * CAP : (k + 1) * CAP] = value
    send[:, 1, :] = params[...]
    inverse = [1.0 / value for value in lengths]
    trace = (
        (lengths[0] * lengths[1] * lengths[2] / 9.0)
        * (first + 4.0 * second)
        * (inverse[0] * inverse[0] + inverse[1] * inverse[1] + inverse[2] * inverse[2])
    )
    trace = jnp.concatenate([trace] * CORNERS, axis=1)

    number = (lax.broadcasted_iota(jnp.int32, (TILE, TILE), 0) + 1).astype(F32).astype(BF16)
    row = lax.broadcasted_iota(jnp.int32, (TILE, TILE), 0)
    lane = lax.broadcasted_iota(jnp.int32, (TILE, TILE), 1)
    place = lane == (row % CORNERS) * CAP + row // CORNERS
    slot = lax.broadcasted_iota(jnp.int32, (1, TILE), 1) % CAP
    per_chunk = n_tiles // chunks
    for t in range(n_tiles):
        if t % per_chunk == 0:
            loads[t // per_chunk].wait()
        onehot = inc[t * TILE : (t + 1) * TILE, :].astype(F32).astype(BF16)
        spread = jnp.dot(onehot, number, preferred_element_type=F32)
        ids = jnp.sum(jnp.where(place, spread, 0.0), axis=0, keepdims=True)
        ids = jnp.where(slot < live[0, t], ids, 0.0)
        send[t, 0:1, :] = ids
        nodes[t : t + 1, :] = ids
    partial = jnp.sum(jnp.where(nodes[...] > 0.0, trace, 0.0), axis=0, keepdims=True)
    plane_recv[0] = jnp.broadcast_to(jnp.sum(partial, axis=1, keepdims=True), (1, TILE))

    pl.semaphore_wait(barrier, jnp.where(is_hub, n_z + n_xy - 2, n_z + n_xy - 1))

    hub_slot = (
        lax.rem(my_x - hub_x + n_x, n_x) * n_y + lax.rem(my_y - hub_y + n_y, n_y)
    ) * n_z + lax.rem(my_z - hub_z + n_z, n_z)
    to_hub = pltpu.make_async_remote_copy(
        src_ref=plane_recv.at[0],
        dst_ref=hub_recv.at[hub_slot],
        send_sem=send_sem.at[3],
        recv_sem=recv_sem.at[3],
        device_id={"gx": hub_x, "gy": hub_y, "gz": hub_z},
        device_id_type=MESH,
    )

    @pl.when(jnp.logical_not(is_hub))
    def _():
        to_hub.start()

    @pl.when(is_hub)
    def _():
        hub_recv[0] = plane_recv[0]

    for i, j in plane_steps:
        pltpu.make_async_remote_copy(
            src_ref=plane_recv.at[0],
            dst_ref=plane_recv.at[i * n_y + j],
            send_sem=send_sem.at[0],
            recv_sem=recv_sem.at[0],
            device_id={"gx": at_x[i], "gy": at_y[j]},
            device_id_type=MESH,
        ).start()
    for step in line_steps:
        pltpu.make_async_remote_copy(
            src_ref=send.at[at_z[step]],
            dst_ref=recv.at[step],
            send_sem=send_sem.at[1],
            recv_sem=recv_sem.at[1],
            device_id={"gz": at_z[step]},
            device_id_type=MESH,
        ).start()
    recv[0] = send[my_z]

    def whole(target, kind, device, fewer=0):
        return pltpu.make_async_remote_copy(
            src_ref=target.at[pl.ds(1, target.shape[0] - 1 - fewer)],
            dst_ref=target.at[pl.ds(1, target.shape[0] - 1 - fewer)],
            send_sem=send_sem.at[kind],
            recv_sem=recv_sem.at[kind],
            device_id=device,
            device_id_type=MESH,
        )

    plane_all = whole(plane_recv, 0, {"gx": at_x[n_x - 1], "gy": at_y[n_y - 1]})
    tile_all = whole(recv, 1, {"gz": at_z[1]})
    line_all = whole(line_recv, 2, {"gz": at_z[1]})
    line_some = whole(line_recv, 2, {"gz": at_z[1]}, fewer=1)
    hub_all = whole(hub_recv, 3, {"gz": at_z[1]})

    plane_all.wait_recv()
    total = plane_recv[0]
    for k in range(1, n_xy):
        total = total + plane_recv[k]
    line_recv[0] = total
    for step in line_steps:

        @pl.when(jnp.logical_not(jnp.logical_and(hub_line, at_z[step] == hub_z)))
        def _():
            pltpu.make_async_remote_copy(
                src_ref=line_recv.at[0],
                dst_ref=line_recv.at[step],
                send_sem=send_sem.at[2],
                recv_sem=recv_sem.at[2],
                device_id={"gz": at_z[step]},
                device_id_type=MESH,
            ).start()

    tile_all.wait_recv()

    halves = range(n_z // 8)
    ids = jnp.concatenate([swap_groups(recv[8 * h : 8 * h + 8, 0, :]) for h in halves], axis=1)
    material = jnp.concatenate(
        [swap_groups(recv[8 * h : 8 * h + 8, 1, :]) for h in halves], axis=1
    )
    wide = ids.shape[1]
    first, second = material[0:1], material[1:2]
    h = [material[2 + k : 3 + k] for k in range(3)]

    node = (lax.broadcasted_iota(jnp.int32, (TILE, wide), 0) + 1).astype(F32)
    corner = [
        jnp.where(node == ids[p : p + 1], 1.0, 0.0).astype(BF16) for p in range(CORNERS)
    ]
    mode = corner
    for bit in (1, 2, 4):
        mode = [
            mode[k] - mode[k ^ bit] if k & bit else mode[k] + mode[k ^ bit]
            for k in range(CORNERS)
        ]

    def scaled(wave, coefficient):
        wide_row = jnp.broadcast_to(coefficient, (16, wide)).astype(BF16)
        return (wave.reshape(TILE // 16, 16, wide) * wide_row[None]).reshape(TILE, wide)

    def product(left, right):
        return lax.dot_general(
            left, right, (((1,), (1,)), ((), ())), preferred_element_type=F32
        )

    def assemble(pairs):
        high, low, other = [], [], []
        for left, right, coefficient in pairs:
            top = coefficient.astype(BF16).astype(F32)
            high.append(scaled(mode[left], top))
            low.append(scaled(mode[left], coefficient - top))
            other.append(mode[right])
        right = jnp.concatenate(other, axis=1)
        left = jnp.concatenate(
            [jnp.concatenate(high, axis=1), jnp.concatenate(low, axis=1)], axis=0
        )
        result = product(left, right)
        return result[:TILE] + result[TILE:]

    area = [h[1] * h[2] / (16.0 * h[0]), h[0] * h[2] / (16.0 * h[1]), h[0] * h[1] / (16.0 * h[2])]
    strong = first + 2.0 * second
    for i in range(3):
        alpha = [(strong if k == i else second) * area[k] for k in range(3)]
        coefficients = {
            1: alpha[0],
            2: alpha[1],
            4: alpha[2],
            3: (alpha[0] + alpha[1]) / 3.0,
            5: (alpha[0] + alpha[2]) / 3.0,
            6: (alpha[1] + alpha[2]) / 3.0,
            7: (alpha[0] + alpha[1] + alpha[2]) / 9.0,
        }
        block_ref[i, i] = assemble([(m, m, coefficients[m]) for m in ALL_MODES])
    for i, j, k in ((0, 1, 2), (0, 2, 1), (1, 2, 0)):
        a, b, c = 1 << i, 1 << j, 1 << k
        la, mu = h[k] * first / 16.0, h[k] * second / 16.0
        result = assemble(
            [
                (a, b, la),
                (a | c, b | c, la / 3.0),
                (b, a, mu),
                (b | c, a | c, mu / 3.0),
            ]
        )
        block_ref[i, j] = result
        block_ref[j, i] = result.T

    def sum_rows(rows, count):
        lanes = min(8, count)
        sums = [rows[k] for k in range(lanes)]
        for k in range(lanes, count):
            sums[k % lanes] = sums[k % lanes] + rows[k]
        while len(sums) > 1:
            sums = [sums[k] + sums[k + 1] for k in range(0, len(sums), 2)]
        return sums[0]

    entries = 3.0 * TILE * n_xy * n_z

    @pl.when(is_hub)
    def _():
        hub_all.wait_recv()
        scale_ref[...] = entries / sum_rows(hub_recv, n_xy * n_z)

    @pl.when(jnp.logical_not(is_hub))
    def _():
        line_all.wait_recv()
        scale_ref[...] = entries / sum_rows(line_recv, n_z)
        to_hub.wait_send()

    plane_all.wait_send()
    tile_all.wait_send()
    in_between = jnp.logical_and(hub_line, my_z != hub_z)

    @pl.when(in_between)
    def _():
        line_some.wait_send()

    @pl.when(jnp.logical_not(in_between))
    def _():
        line_all.wait_send()


def solution(mesh):
    n_x, n_y, n_z = mesh.shape["gx"], mesh.shape["gy"], mesh.shape["gz"]
    n_xy = n_x * n_y

    def on_device(incidence, live_counts, lame_first, shear_modulus, stretch):
        n_tiles = incidence.shape[3]
        hbm = pl.BlockSpec(memory_space=pltpu.HBM)
        vmem = pl.BlockSpec(memory_space=pltpu.VMEM)
        block, scale = pl.pallas_call(
            functools.partial(kernel, n_x, n_y, n_z),
            out_shape=(
                jax.ShapeDtypeStruct((3, 3, TILE, TILE), F32),
                jax.ShapeDtypeStruct((1, TILE), F32),
            ),
            in_specs=[hbm] * 5,
            out_specs=(vmem, vmem),
            scratch_shapes=[
                pltpu.SMEM((1, n_tiles), jnp.int32),
                pltpu.VMEM((n_tiles * CAP * CORNERS, TILE), jnp.int32),
                pltpu.VMEM((n_tiles, CAP), F32),
                pltpu.VMEM((n_tiles, CAP), F32),
                pltpu.VMEM((3, n_tiles, CAP), F32),
                pltpu.VMEM((n_tiles, TILE), F32),
                pltpu.VMEM((n_tiles, TILE), F32),
                pltpu.VMEM((n_z, 2, TILE), F32),
                pltpu.VMEM((n_z, 2, TILE), F32),
                pltpu.VMEM((n_xy, 1, TILE), F32),
                pltpu.VMEM((n_z, 1, TILE), F32),
                pltpu.VMEM((n_xy * n_z, 1, TILE), F32),
                pltpu.SemaphoreType.DMA((4,)),
                pltpu.SemaphoreType.DMA((4,)),
                pltpu.SemaphoreType.DMA((4,)),
                pltpu.SemaphoreType.DMA((4,)),
            ],
            compiler_params=pltpu.CompilerParams(
                collective_id=0, has_side_effects=True, vmem_limit_bytes=24 << 20
            ),
        )(
            *(
                pltpu.with_memory_space_constraint(value, pltpu.HBM)
                for value in (
                    live_counts.reshape(1, n_tiles),
                    incidence.reshape(n_tiles * CAP * CORNERS, TILE),
                    lame_first.reshape(n_tiles, CAP),
                    shear_modulus.reshape(n_tiles, CAP),
                    stretch.reshape(3, n_tiles, CAP),
                )
            )
        )
        block = block * scale.reshape(1, 1, 1, TILE)
        return block.transpose(0, 2, 1, 3).reshape(1, 1, 1, 3, TILE, 3, TILE)

    return jax.shard_map(
        on_device,
        mesh=mesh,
        in_specs=(
            P("gx", "gy", "gz", None, None, None, None),
            P("gx", "gy", "gz", None),
            P("gx", "gy", "gz", None, None),
            P("gx", "gy", "gz", None, None),
            P(None, "gx", "gy", "gz", None, None),
        ),
        out_specs=P("gx", "gy", "gz", None, None, None, None),
        check_vma=False,
    )
```

```python
import functools

import jax
import jax.numpy as jnp
from jax import lax
from jax.experimental import pallas as pl
from jax.experimental.pallas import tpu as pltpu
from jax.sharding import PartitionSpec as P

MESH = pl.DeviceIdType.MESH
F32, BF16 = jnp.float32, jnp.bfloat16
TILE, CAP, CORNERS = 128, 16, 8

LEAD = 1
CAST = 3
EARLY = 4

ALL_MODES = (1, 2, 4, 3, 5, 6, 7)


def split(value):
    high = value.astype(BF16)
    return high, (value - high.astype(F32)).astype(BF16)


def swap_groups(values):
    sub = lax.broadcasted_iota(jnp.int32, (8, 128), 0)
    group = lax.broadcasted_iota(jnp.int32, (8, 128), 1) // CAP
    for bit in (1, 2, 4):
        upper_sub = (sub & bit) != 0
        upper_group = (group & bit) != 0
        below = pltpu.roll(pltpu.roll(values, 8 - bit, 0), CAP * bit, 1)
        above = pltpu.roll(pltpu.roll(values, bit, 0), 128 - CAP * bit, 1)
        values = jnp.where(
            upper_sub == upper_group, values, jnp.where(upper_sub, above, below)
        )
    return values


def kernel(
    n_x, n_y, n_z,
    live_hbm, inc_hbm, lame_hbm, shear_hbm, stretch_hbm,
    block_ref, scale_ref,
    live, inc, lame, shear, stretch, nodes, params, send, recv, row, row_recv, hub_recv,
    in_sem, small_sem, send_sem, recv_sem, cast_sem, here, ready,
):
    n_tiles = send.shape[0]
    my_x, my_y, my_z = lax.axis_index("gx"), lax.axis_index("gy"), lax.axis_index("gz")
    n_xy = n_x * n_y

    chunks = in_sem.shape[0]
    rows = inc.shape[0] // chunks
    loads = [
        pltpu.make_async_copy(
            inc_hbm.at[pl.ds(c * rows, rows)], inc.at[pl.ds(c * rows, rows)], in_sem.at[c]
        )
        for c in range(chunks)
    ]
    small = [
        pltpu.make_async_copy(source, target, small_sem.at[k])
        for k, (source, target) in enumerate(
            ((live_hbm, live), (lame_hbm, lame), (shear_hbm, shear), (stretch_hbm, stretch))
        )
    ]
    for copy in loads + small:
        copy.start()

    def hops(step, size):
        return min(step, size - step)

    hubs = [(0, 0, LEAD), (0, 0, CAST)]
    hubs += [(i, 0, LEAD) for i in range(1, n_x)] + [(0, j, LEAD) for j in range(1, n_y)]

    def is_at(x, y, z):
        return jnp.logical_and(jnp.logical_and(my_x == x, my_y == y), my_z == z)

    in_corner = jnp.logical_and(my_x == 0, my_y == 0)
    on_edge = jnp.logical_or(my_x == 0, my_y == 0)
    is_lead = my_z == LEAD
    is_early = my_z < EARLY
    is_hub = jnp.logical_or(jnp.logical_and(on_edge, is_lead), is_at(0, 0, CAST))
    plane_steps = sorted(
        ((i, j) for i in range(n_x) for j in range(n_y)),
        key=lambda step: -hops(step[0], n_x) - hops(step[1], n_y),
    )
    line_steps = sorted(range(1, n_z), key=lambda step: -hops(step, n_z))

    barrier = pltpu.get_barrier_semaphore()

    def greet(x, y, z):
        pl.semaphore_signal(
            barrier, inc=1, device_id={"gx": x, "gy": y, "gz": z}, device_id_type=MESH
        )

    @pl.when(is_early)
    def _():
        for step in line_steps:
            greet(my_x, my_y, lax.rem(my_z + step, n_z))

    @pl.when(is_hub)
    def _():
        half = n_z // 2

        @pl.loop(0, half)
        def _(near):
            ahead = lax.rem(my_z + half + near, n_z)
            behind = lax.rem(my_z + jnp.where(near == 0, 0, half - near), n_z)
            for i, j in plane_steps:
                x, y = lax.rem(my_x + i, n_x), lax.rem(my_y + j, n_y)
                greet(x, y, ahead)
                if i or j:
                    greet(x, y, behind)
                else:

                    @pl.when(near > 0)
                    def _():
                        greet(x, y, behind)

    for copy in small:
        copy.wait()
    params[...] = jnp.zeros_like(params)
    first, second = lame[...], shear[...]
    lengths = [stretch[k] for k in range(3)]
    for k, value in enumerate([first, second] + lengths):
        params[:, k * CAP : (k + 1) * CAP] = value
    send[:, 1, :] = params[...]
    inverse = [1.0 / value for value in lengths]
    trace = (
        (lengths[0] * lengths[1] * lengths[2] / 9.0)
        * (first + 4.0 * second)
        * (inverse[0] * inverse[0] + inverse[1] * inverse[1] + inverse[2] * inverse[2])
    )
    trace = jnp.concatenate([trace] * CORNERS, axis=1)

    number = (lax.broadcasted_iota(jnp.int32, (TILE, TILE), 0) + 1).astype(F32).astype(BF16)
    down = lax.broadcasted_iota(jnp.int32, (TILE, TILE), 0)
    lane = lax.broadcasted_iota(jnp.int32, (TILE, TILE), 1)
    place = lane == (down % CORNERS) * CAP + down // CORNERS
    slot = lax.broadcasted_iota(jnp.int32, (1, TILE), 1) % CAP
    per_chunk = n_tiles // chunks
    for t in range(n_tiles):
        if t % per_chunk == 0:
            loads[t // per_chunk].wait()
        onehot = inc[t * TILE : (t + 1) * TILE, :].astype(F32).astype(BF16)
        spread = jnp.dot(onehot, number, preferred_element_type=F32)
        ids = jnp.sum(jnp.where(place, spread, 0.0), axis=0, keepdims=True)
        ids = jnp.where(slot < live[0, t], ids, 0.0)
        send[t, 0:1, :] = ids
        nodes[t : t + 1, :] = ids
    partial = jnp.sum(jnp.where(nodes[...] > 0.0, trace, 0.0), axis=0, keepdims=True)
    row[...] = jnp.broadcast_to(jnp.sum(partial, axis=1, keepdims=True), (1, TILE))

    pl.semaphore_wait(
        barrier,
        len(hubs) + EARLY - jnp.where(is_hub, 1, 0) - jnp.where(is_early, 1, 0),
    )

    for x, y, z in hubs:
        source = lax.rem(my_x - x + n_x, n_x) * n_y + lax.rem(my_y - y + n_y, n_y)

        @pl.when(jnp.logical_not(is_at(x, y, z)))
        def _():
            pltpu.make_async_remote_copy(
                src_ref=row,
                dst_ref=hub_recv.at[source * n_z + lax.rem(my_z - z + n_z, n_z)],
                send_sem=send_sem.at[0],
                recv_sem=recv_sem.at[0],
                device_id={"gx": x, "gy": y, "gz": z},
                device_id_type=MESH,
            ).start()

    hub_recv[0] = row[...]

    @pl.when(jnp.logical_not(is_lead))
    def _():
        pl.semaphore_signal(here, inc=1, device_id={"gz": LEAD}, device_id_type=MESH)

    def send_tile(z):
        @pl.when(my_z != z)
        def _():
            pltpu.make_async_remote_copy(
                src_ref=send.at[z],
                dst_ref=recv.at[lax.rem(my_z - z + n_z, n_z)],
                send_sem=send_sem.at[1],
                recv_sem=recv_sem.at[1],
                device_id={"gz": z},
                device_id_type=MESH,
            ).start()

    for z in range(EARLY):
        send_tile(z)
    recv[0] = send[my_z]

    @pl.when(is_lead)
    def _():
        pl.semaphore_wait(here, n_z - 1)
        for step in line_steps:
            pl.semaphore_signal(
                ready, inc=1, device_id={"gz": (LEAD + step) % n_z}, device_id_type=MESH
            )

    @pl.when(jnp.logical_not(is_lead))
    def _():
        pl.semaphore_wait(ready, 1)

    for z in range(EARLY, n_z):
        send_tile(z)

    def rows(target, count, send_with, recv_with):
        return pltpu.make_async_remote_copy(
            src_ref=target.at[pl.ds(1, count)],
            dst_ref=target.at[pl.ds(1, count)],
            send_sem=send_with,
            recv_sem=recv_with,
            device_id={"gz": lax.rem(my_z + 1, n_z)},
            device_id_type=MESH,
        )

    tiles = rows(recv, n_z - 1, send_sem.at[1], recv_sem.at[1])
    tiles.wait_recv()

    halves = range(n_z // 8)
    ids = jnp.concatenate([swap_groups(recv[8 * h : 8 * h + 8, 0, :]) for h in halves], axis=1)
    material = jnp.concatenate(
        [swap_groups(recv[8 * h : 8 * h + 8, 1, :]) for h in halves], axis=1
    )
    wide = ids.shape[1]
    first, second = material[0:1], material[1:2]
    h = [material[2 + k : 3 + k] for k in range(3)]

    node = (lax.broadcasted_iota(jnp.int32, (TILE, wide), 0) + 1).astype(F32)
    corner = [
        jnp.where(node == ids[p : p + 1], 1.0, 0.0).astype(BF16) for p in range(CORNERS)
    ]
    mode = corner
    for bit in (1, 2, 4):
        mode = [
            mode[k] - mode[k ^ bit] if k & bit else mode[k] + mode[k ^ bit]
            for k in range(CORNERS)
        ]

    def scaled(wave, coefficient):
        wide_row = jnp.broadcast_to(coefficient, (16, wide)).astype(BF16)
        return (wave.reshape(TILE // 16, 16, wide) * wide_row[None]).reshape(TILE, wide)

    def product(left, right):
        return lax.dot_general(
            left, right, (((1,), (1,)), ((), ())), preferred_element_type=F32
        )

    def assemble(pairs):
        high, low, other = [], [], []
        for left, right, coefficient in pairs:
            top = coefficient.astype(BF16).astype(F32)
            high.append(scaled(mode[left], top))
            low.append(scaled(mode[left], coefficient - top))
            other.append(mode[right])
        right = jnp.concatenate(other, axis=1)
        left = jnp.concatenate(
            [jnp.concatenate(high, axis=1), jnp.concatenate(low, axis=1)], axis=0
        )
        result = product(left, right)
        return result[:TILE] + result[TILE:]

    area = [h[1] * h[2] / (16.0 * h[0]), h[0] * h[2] / (16.0 * h[1]), h[0] * h[1] / (16.0 * h[2])]
    strong = first + 2.0 * second
    for i in range(3):
        alpha = [(strong if k == i else second) * area[k] for k in range(3)]
        coefficients = {
            1: alpha[0],
            2: alpha[1],
            4: alpha[2],
            3: (alpha[0] + alpha[1]) / 3.0,
            5: (alpha[0] + alpha[2]) / 3.0,
            6: (alpha[1] + alpha[2]) / 3.0,
            7: (alpha[0] + alpha[1] + alpha[2]) / 9.0,
        }
        block_ref[i, i] = assemble([(m, m, coefficients[m]) for m in ALL_MODES])
    for i, j, k in ((0, 1, 2), (0, 2, 1), (1, 2, 0)):
        a, b, c = 1 << i, 1 << j, 1 << k
        la, mu = h[k] * first / 16.0, h[k] * second / 16.0
        result = assemble(
            [
                (a, b, la),
                (a | c, b | c, la / 3.0),
                (b, a, mu),
                (b | c, a | c, mu / 3.0),
            ]
        )
        block_ref[i, j] = result
        block_ref[j, i] = result.T

    def sum_rows(values, count):
        lanes = min(8, count)
        sums = [values[k] for k in range(lanes)]
        for k in range(lanes, count):
            sums[k % lanes] = sums[k % lanes] + values[k]
        while len(sums) > 1:
            sums = [sums[k] + sums[k + 1] for k in range(0, len(sums), 2)]
        return sums[0]

    from_x, from_y = jnp.minimum(my_x, n_x - my_x), jnp.minimum(my_y, n_y - my_y)
    lead_x = jnp.logical_and(is_lead, jnp.logical_and(my_y == 0, my_x != 0))
    lead_y = jnp.logical_and(is_lead, jnp.logical_and(my_x == 0, my_y != 0))
    lines = [(0, 0, jnp.logical_and(is_hub, jnp.logical_not(is_at(0, 0, LEAD))))]
    lines += [
        (0, j, jnp.logical_and(lead_x, hops(j, n_y) <= from_x)) for j in range(1, n_y)
    ]
    lines += [(i, 0, jnp.logical_and(lead_y, from_y > hops(i, n_x))) for i in range(1, n_x)]

    @pl.when(is_hub)
    def _():
        rows(hub_recv, n_xy * n_z - 1, send_sem.at[0], recv_sem.at[0]).wait_recv()
        scale = (3.0 * TILE * n_xy * n_z) / sum_rows(hub_recv, n_xy * n_z)
        scale_ref[...] = scale
        row_recv[...] = scale
        for which, (i, j, casts) in enumerate(lines):

            @pl.when(casts)
            def _():
                for z in range(n_z):
                    copy = pltpu.make_async_remote_copy(
                        src_ref=row_recv,
                        dst_ref=row_recv,
                        send_sem=cast_sem.at[which],
                        recv_sem=recv_sem.at[2],
                        device_id={
                            "gx": lax.rem(my_x + i, n_x),
                            "gy": lax.rem(my_y + j, n_y),
                            "gz": z,
                        },
                        device_id_type=MESH,
                    )
                    if i or j:
                        copy.start()
                    else:
                        first_hub = jnp.logical_and(in_corner, z == LEAD)

                        @pl.when(jnp.logical_not(jnp.logical_or(my_z == z, first_hub)))
                        def _():
                            copy.start()

        for which, (i, j, casts) in enumerate(lines):
            if i or j:

                @pl.when(casts)
                def _():
                    rows(hub_recv, n_z, cast_sem.at[which], recv_sem.at[2]).wait_send()

        @pl.when(jnp.logical_and(is_lead, jnp.logical_not(in_corner)))
        def _():
            rows(hub_recv, n_z - 1, cast_sem.at[0], recv_sem.at[2]).wait_send()

        @pl.when(jnp.logical_not(is_lead))
        def _():
            rows(hub_recv, n_z - 2, cast_sem.at[0], recv_sem.at[2]).wait_send()

        rows(hub_recv, len(hubs) - 1, send_sem.at[0], recv_sem.at[0]).wait_send()

    @pl.when(jnp.logical_not(is_hub))
    def _():
        rows(hub_recv, 1, send_sem.at[2], recv_sem.at[2]).wait_recv()
        scale_ref[...] = row_recv[...]
        rows(hub_recv, len(hubs), send_sem.at[0], recv_sem.at[0]).wait_send()

    tiles.wait_send()


def solution(mesh):
    n_x, n_y, n_z = mesh.shape["gx"], mesh.shape["gy"], mesh.shape["gz"]
    n_xy = n_x * n_y

    def on_device(incidence, live_counts, lame_first, shear_modulus, stretch):
        n_tiles = incidence.shape[3]
        hbm = pl.BlockSpec(memory_space=pltpu.HBM)
        vmem = pl.BlockSpec(memory_space=pltpu.VMEM)
        block, scale = pl.pallas_call(
            functools.partial(kernel, n_x, n_y, n_z),
            out_shape=(
                jax.ShapeDtypeStruct((3, 3, TILE, TILE), F32),
                jax.ShapeDtypeStruct((1, TILE), F32),
            ),
            in_specs=[hbm] * 5,
            out_specs=(vmem, vmem),
            scratch_shapes=[
                pltpu.SMEM((1, n_tiles), jnp.int32),
                pltpu.VMEM((n_tiles * CAP * CORNERS, TILE), jnp.int32),
                pltpu.VMEM((n_tiles, CAP), F32),
                pltpu.VMEM((n_tiles, CAP), F32),
                pltpu.VMEM((3, n_tiles, CAP), F32),
                pltpu.VMEM((n_tiles, TILE), F32),
                pltpu.VMEM((n_tiles, TILE), F32),
                pltpu.VMEM((n_z, 2, TILE), F32),
                pltpu.VMEM((n_z, 2, TILE), F32),
                pltpu.VMEM((1, TILE), F32),
                pltpu.VMEM((1, TILE), F32),
                pltpu.VMEM((n_xy * n_z, 1, TILE), F32),
                pltpu.SemaphoreType.DMA((4,)),
                pltpu.SemaphoreType.DMA((4,)),
                pltpu.SemaphoreType.DMA((3,)),
                pltpu.SemaphoreType.DMA((3,)),
                pltpu.SemaphoreType.DMA((n_x + n_y - 1,)),
                pltpu.SemaphoreType.REGULAR,
                pltpu.SemaphoreType.REGULAR,
            ],
            compiler_params=pltpu.CompilerParams(
                collective_id=0, has_side_effects=True, vmem_limit_bytes=24 << 20
            ),
        )(
            *(
                pltpu.with_memory_space_constraint(value, pltpu.HBM)
                for value in (
                    live_counts.reshape(1, n_tiles),
                    incidence.reshape(n_tiles * CAP * CORNERS, TILE),
                    lame_first.reshape(n_tiles, CAP),
                    shear_modulus.reshape(n_tiles, CAP),
                    stretch.reshape(3, n_tiles, CAP),
                )
            )
        )
        block = block * scale.reshape(1, 1, 1, TILE)
        return block.transpose(0, 2, 1, 3).reshape(1, 1, 1, 3, TILE, 3, TILE)

    return jax.shard_map(
        on_device,
        mesh=mesh,
        in_specs=(
            P("gx", "gy", "gz", None, None, None, None),
            P("gx", "gy", "gz", None),
            P("gx", "gy", "gz", None, None),
            P("gx", "gy", "gz", None, None),
            P(None, "gx", "gy", "gz", None, None),
        ),
        out_specs=P("gx", "gy", "gz", None, None, None, None),
        check_vma=False,
    )
```

```python
import functools

import jax
import jax.numpy as jnp
from jax import lax
from jax.experimental import pallas as pl
from jax.experimental.pallas import tpu as pltpu
from jax.sharding import PartitionSpec as P

MESH = pl.DeviceIdType.MESH
F32, BF16 = jnp.float32, jnp.bfloat16
TILE, CAP, CORNERS = 128, 16, 8

LEAD = 1
CAST = 3
EARLY = 4

ALL_MODES = (1, 2, 4, 3, 5, 6, 7)


def split(value):
    high = value.astype(BF16)
    return high, (value - high.astype(F32)).astype(BF16)


def swap_groups(values):
    sub = lax.broadcasted_iota(jnp.int32, (8, 128), 0)
    group = lax.broadcasted_iota(jnp.int32, (8, 128), 1) // CAP
    for bit in (1, 2, 4):
        upper_sub = (sub & bit) != 0
        upper_group = (group & bit) != 0
        below = pltpu.roll(pltpu.roll(values, 8 - bit, 0), CAP * bit, 1)
        above = pltpu.roll(pltpu.roll(values, bit, 0), 128 - CAP * bit, 1)
        values = jnp.where(
            upper_sub == upper_group, values, jnp.where(upper_sub, above, below)
        )
    return values


def kernel(
    n_x, n_y, n_z,
    live_hbm, inc_hbm, lame_hbm, shear_hbm, stretch_hbm,
    block_ref, scale_ref,
    live, inc, lame, shear, stretch, weight, number, place, params, send, recv, row, row_recv, hub_recv,
    in_sem, small_sem, send_sem, recv_sem, cast_sem, here, ready,
):
    n_tiles = send.shape[0]
    my_x, my_y, my_z = lax.axis_index("gx"), lax.axis_index("gy"), lax.axis_index("gz")
    n_xy = n_x * n_y

    load = pltpu.make_async_copy(inc_hbm, inc, in_sem)
    small = [
        pltpu.make_async_copy(source, target, small_sem.at[k])
        for k, (source, target) in enumerate(
            ((live_hbm, live), (lame_hbm, lame), (shear_hbm, shear), (stretch_hbm, stretch))
        )
    ]
    for copy in [load] + small:
        copy.start()

    def hops(step, size):
        return min(step, size - step)

    hubs = [(0, 0, LEAD), (0, 0, CAST)]
    hubs += [(i, 0, LEAD) for i in range(1, n_x)] + [(0, j, LEAD) for j in range(1, n_y)]

    def is_at(x, y, z):
        return jnp.logical_and(jnp.logical_and(my_x == x, my_y == y), my_z == z)

    in_corner = jnp.logical_and(my_x == 0, my_y == 0)
    on_edge = jnp.logical_or(my_x == 0, my_y == 0)
    is_lead = my_z == LEAD
    is_early = my_z < EARLY
    is_hub = jnp.logical_or(jnp.logical_and(on_edge, is_lead), is_at(0, 0, CAST))
    plane_steps = sorted(
        ((i, j) for i in range(n_x) for j in range(n_y)),
        key=lambda step: -hops(step[0], n_x) - hops(step[1], n_y),
    )
    line_steps = sorted(range(1, n_z), key=lambda step: -hops(step, n_z))

    barrier = pltpu.get_barrier_semaphore()

    def greet(x, y, z):
        pl.semaphore_signal(
            barrier, inc=1, device_id={"gx": x, "gy": y, "gz": z}, device_id_type=MESH
        )

    @pl.when(is_early)
    def _():
        for step in line_steps:
            greet(my_x, my_y, lax.rem(my_z + step, n_z))

    @pl.when(is_hub)
    def _():
        half = n_z // 2

        @pl.loop(0, half)
        def _(near):
            ahead = lax.rem(my_z + half + near, n_z)
            behind = lax.rem(my_z + jnp.where(near == 0, 0, half - near), n_z)
            for i, j in plane_steps:
                x, y = lax.rem(my_x + i, n_x), lax.rem(my_y + j, n_y)
                greet(x, y, ahead)
                if i or j:
                    greet(x, y, behind)
                else:

                    @pl.when(near > 0)
                    def _():
                        greet(x, y, behind)

    for copy in small:
        copy.wait()
    params[...] = jnp.zeros_like(params)
    first, second = lame[...], shear[...]
    lengths = [stretch[k] for k in range(3)]
    for k, value in enumerate([first, second] + lengths):
        params[:, k * CAP : (k + 1) * CAP] = value
    send[:, 1, :] = params[...]
    inverse = [1.0 / value for value in lengths]
    trace = (
        (lengths[0] * lengths[1] * lengths[2] / 9.0)
        * (first + 4.0 * second)
        * (inverse[0] * inverse[0] + inverse[1] * inverse[1] + inverse[2] * inverse[2])
    )
    diagonal = lax.broadcasted_iota(jnp.int32, (CAP, CAP), 0) == lax.broadcasted_iota(
        jnp.int32, (CAP, CAP), 1
    )
    slot_down = lax.broadcasted_iota(jnp.int32, (CAP, 1), 0)
    for t in range(n_tiles):
        column = jnp.sum(jnp.where(diagonal, trace[t : t + 1, :], 0.0), axis=1, keepdims=True)
        column = jnp.where(slot_down < live[0, t], column, 0.0)
        weight[t * CAP : (t + 1) * CAP, :] = jnp.broadcast_to(column, (CAP, TILE))

    down = lax.broadcasted_iota(jnp.int32, (TILE, TILE), 0)
    lane = lax.broadcasted_iota(jnp.int32, (TILE, TILE), 1)
    number[...] = (down + 1).astype(F32).astype(BF16)
    place[...] = jnp.where(lane == (down % CORNERS) * CAP + down // CORNERS, 1.0, 0.0)
    slot = lax.broadcasted_iota(jnp.int32, (1, TILE), 1) % CAP

    load.wait()
    sums = [jnp.zeros((CORNERS, TILE), F32) for _ in range(8)]
    for e in range(n_tiles * CAP):
        onehot = inc[e * CORNERS : (e + 1) * CORNERS, :].astype(F32)
        sums[e % 8] = sums[e % 8] + onehot * weight[e : e + 1, :]
    while len(sums) > 1:
        sums = [sums[k] + sums[k + 1] for k in range(0, len(sums), 2)]
    partial = jnp.sum(sums[0], axis=0, keepdims=True)
    row[...] = jnp.broadcast_to(jnp.sum(partial, axis=1, keepdims=True), (1, TILE))

    pl.semaphore_wait(
        barrier,
        len(hubs) + EARLY - jnp.where(is_hub, 1, 0) - jnp.where(is_early, 1, 0),
    )

    for x, y, z in hubs:
        source = lax.rem(my_x - x + n_x, n_x) * n_y + lax.rem(my_y - y + n_y, n_y)

        @pl.when(jnp.logical_not(is_at(x, y, z)))
        def _():
            pltpu.make_async_remote_copy(
                src_ref=row,
                dst_ref=hub_recv.at[source * n_z + lax.rem(my_z - z + n_z, n_z)],
                send_sem=send_sem.at[0],
                recv_sem=recv_sem.at[0],
                device_id={"gx": x, "gy": y, "gz": z},
                device_id_type=MESH,
            ).start()

    hub_recv[0] = row[...]

    @pl.when(jnp.logical_not(is_lead))
    def _():
        pl.semaphore_signal(here, inc=1, device_id={"gz": LEAD}, device_id_type=MESH)

    for t in range(n_tiles):
        onehot = inc[t * TILE : (t + 1) * TILE, :].astype(F32).astype(BF16)
        spread = jnp.dot(onehot, number[...], preferred_element_type=F32)
        ids = jnp.sum(spread * place[...], axis=0, keepdims=True)
        send[t, 0:1, :] = jnp.where(slot < live[0, t], ids, 0.0)

    def send_tile(z):
        @pl.when(my_z != z)
        def _():
            pltpu.make_async_remote_copy(
                src_ref=send.at[z],
                dst_ref=recv.at[lax.rem(my_z - z + n_z, n_z)],
                send_sem=send_sem.at[1],
                recv_sem=recv_sem.at[1],
                device_id={"gz": z},
                device_id_type=MESH,
            ).start()

    for z in range(EARLY):
        send_tile(z)
    recv[0] = send[my_z]

    @pl.when(is_lead)
    def _():
        pl.semaphore_wait(here, n_z - 1)
        for step in line_steps:
            pl.semaphore_signal(
                ready, inc=1, device_id={"gz": (LEAD + step) % n_z}, device_id_type=MESH
            )

    @pl.when(jnp.logical_not(is_lead))
    def _():
        pl.semaphore_wait(ready, 1)

    for z in range(EARLY, n_z):
        send_tile(z)

    def rows(target, count, send_with, recv_with):
        return pltpu.make_async_remote_copy(
            src_ref=target.at[pl.ds(1, count)],
            dst_ref=target.at[pl.ds(1, count)],
            send_sem=send_with,
            recv_sem=recv_with,
            device_id={"gz": lax.rem(my_z + 1, n_z)},
            device_id_type=MESH,
        )

    tiles = rows(recv, n_z - 1, send_sem.at[1], recv_sem.at[1])
    tiles.wait_recv()

    halves = range(n_z // 8)
    ids = jnp.concatenate([swap_groups(recv[8 * h : 8 * h + 8, 0, :]) for h in halves], axis=1)
    material = jnp.concatenate(
        [swap_groups(recv[8 * h : 8 * h + 8, 1, :]) for h in halves], axis=1
    )
    wide = ids.shape[1]
    first, second = material[0:1], material[1:2]
    h = [material[2 + k : 3 + k] for k in range(3)]

    node = (lax.broadcasted_iota(jnp.int32, (TILE, wide), 0) + 1).astype(F32)
    corner = [
        jnp.where(node == ids[p : p + 1], 1.0, 0.0).astype(BF16) for p in range(CORNERS)
    ]
    mode = corner
    for bit in (1, 2, 4):
        mode = [
            mode[k] - mode[k ^ bit] if k & bit else mode[k] + mode[k ^ bit]
            for k in range(CORNERS)
        ]

    def scaled(wave, coefficient):
        wide_row = jnp.broadcast_to(coefficient, (16, wide)).astype(BF16)
        return (wave.reshape(TILE // 16, 16, wide) * wide_row[None]).reshape(TILE, wide)

    def product(left, right):
        return lax.dot_general(
            left, right, (((1,), (1,)), ((), ())), preferred_element_type=F32
        )

    def assemble(pairs):
        high, low, other = [], [], []
        for left, right, coefficient in pairs:
            top = coefficient.astype(BF16).astype(F32)
            high.append(scaled(mode[left], top))
            low.append(scaled(mode[left], coefficient - top))
            other.append(mode[right])
        right = jnp.concatenate(other, axis=1)
        left = jnp.concatenate(
            [jnp.concatenate(high, axis=1), jnp.concatenate(low, axis=1)], axis=0
        )
        result = product(left, right)
        return result[:TILE] + result[TILE:]

    area = [h[1] * h[2] / (16.0 * h[0]), h[0] * h[2] / (16.0 * h[1]), h[0] * h[1] / (16.0 * h[2])]
    strong = first + 2.0 * second
    for i in range(3):
        alpha = [(strong if k == i else second) * area[k] for k in range(3)]
        coefficients = {
            1: alpha[0],
            2: alpha[1],
            4: alpha[2],
            3: (alpha[0] + alpha[1]) / 3.0,
            5: (alpha[0] + alpha[2]) / 3.0,
            6: (alpha[1] + alpha[2]) / 3.0,
            7: (alpha[0] + alpha[1] + alpha[2]) / 9.0,
        }
        block_ref[i, i] = assemble([(m, m, coefficients[m]) for m in ALL_MODES])
    for i, j, k in ((0, 1, 2), (0, 2, 1), (1, 2, 0)):
        a, b, c = 1 << i, 1 << j, 1 << k
        la, mu = h[k] * first / 16.0, h[k] * second / 16.0
        result = assemble(
            [
                (a, b, la),
                (a | c, b | c, la / 3.0),
                (b, a, mu),
                (b | c, a | c, mu / 3.0),
            ]
        )
        block_ref[i, j] = result
        block_ref[j, i] = result.T

    def sum_rows(values, count):
        lanes = min(8, count)
        sums = [values[k] for k in range(lanes)]
        for k in range(lanes, count):
            sums[k % lanes] = sums[k % lanes] + values[k]
        while len(sums) > 1:
            sums = [sums[k] + sums[k + 1] for k in range(0, len(sums), 2)]
        return sums[0]

    from_x, from_y = jnp.minimum(my_x, n_x - my_x), jnp.minimum(my_y, n_y - my_y)
    lead_x = jnp.logical_and(is_lead, jnp.logical_and(my_y == 0, my_x != 0))
    lead_y = jnp.logical_and(is_lead, jnp.logical_and(my_x == 0, my_y != 0))
    lines = [(0, 0, jnp.logical_and(is_hub, jnp.logical_not(is_at(0, 0, LEAD))))]
    lines += [
        (0, j, jnp.logical_and(lead_x, hops(j, n_y) <= from_x)) for j in range(1, n_y)
    ]
    lines += [(i, 0, jnp.logical_and(lead_y, from_y > hops(i, n_x))) for i in range(1, n_x)]

    @pl.when(is_hub)
    def _():
        rows(hub_recv, n_xy * n_z - 1, send_sem.at[0], recv_sem.at[0]).wait_recv()
        scale = (3.0 * TILE * n_xy * n_z) / sum_rows(hub_recv, n_xy * n_z)
        scale_ref[...] = scale
        row_recv[...] = scale
        for which, (i, j, casts) in enumerate(lines):

            @pl.when(casts)
            def _():
                for z in range(n_z):
                    copy = pltpu.make_async_remote_copy(
                        src_ref=row_recv,
                        dst_ref=row_recv,
                        send_sem=cast_sem.at[which],
                        recv_sem=recv_sem.at[2],
                        device_id={
                            "gx": lax.rem(my_x + i, n_x),
                            "gy": lax.rem(my_y + j, n_y),
                            "gz": z,
                        },
                        device_id_type=MESH,
                    )
                    if i or j:
                        copy.start()
                    else:
                        first_hub = jnp.logical_and(in_corner, z == LEAD)

                        @pl.when(jnp.logical_not(jnp.logical_or(my_z == z, first_hub)))
                        def _():
                            copy.start()

        for which, (i, j, casts) in enumerate(lines):
            if i or j:

                @pl.when(casts)
                def _():
                    rows(hub_recv, n_z, cast_sem.at[which], recv_sem.at[2]).wait_send()

        @pl.when(jnp.logical_and(is_lead, jnp.logical_not(in_corner)))
        def _():
            rows(hub_recv, n_z - 1, cast_sem.at[0], recv_sem.at[2]).wait_send()

        @pl.when(jnp.logical_not(is_lead))
        def _():
            rows(hub_recv, n_z - 2, cast_sem.at[0], recv_sem.at[2]).wait_send()

        rows(hub_recv, len(hubs) - 1, send_sem.at[0], recv_sem.at[0]).wait_send()

    @pl.when(jnp.logical_not(is_hub))
    def _():
        rows(hub_recv, 1, send_sem.at[2], recv_sem.at[2]).wait_recv()
        scale_ref[...] = row_recv[...]
        rows(hub_recv, len(hubs), send_sem.at[0], recv_sem.at[0]).wait_send()

    tiles.wait_send()


def solution(mesh):
    n_x, n_y, n_z = mesh.shape["gx"], mesh.shape["gy"], mesh.shape["gz"]
    n_xy = n_x * n_y

    def on_device(incidence, live_counts, lame_first, shear_modulus, stretch):
        n_tiles = incidence.shape[3]
        hbm = pl.BlockSpec(memory_space=pltpu.HBM)
        vmem = pl.BlockSpec(memory_space=pltpu.VMEM)
        block, scale = pl.pallas_call(
            functools.partial(kernel, n_x, n_y, n_z),
            out_shape=(
                jax.ShapeDtypeStruct((3, 3, TILE, TILE), F32),
                jax.ShapeDtypeStruct((1, TILE), F32),
            ),
            in_specs=[hbm] * 5,
            out_specs=(vmem, vmem),
            scratch_shapes=[
                pltpu.SMEM((1, n_tiles), jnp.int32),
                pltpu.VMEM((n_tiles * CAP * CORNERS, TILE), jnp.int32),
                pltpu.VMEM((n_tiles, CAP), F32),
                pltpu.VMEM((n_tiles, CAP), F32),
                pltpu.VMEM((3, n_tiles, CAP), F32),
                pltpu.VMEM((n_tiles * CAP, TILE), F32),
                pltpu.VMEM((TILE, TILE), BF16),
                pltpu.VMEM((TILE, TILE), F32),
                pltpu.VMEM((n_tiles, TILE), F32),
                pltpu.VMEM((n_z, 2, TILE), F32),
                pltpu.VMEM((n_z, 2, TILE), F32),
                pltpu.VMEM((1, TILE), F32),
                pltpu.VMEM((1, TILE), F32),
                pltpu.VMEM((n_xy * n_z, 1, TILE), F32),
                pltpu.SemaphoreType.DMA,
                pltpu.SemaphoreType.DMA((4,)),
                pltpu.SemaphoreType.DMA((3,)),
                pltpu.SemaphoreType.DMA((3,)),
                pltpu.SemaphoreType.DMA((n_x + n_y - 1,)),
                pltpu.SemaphoreType.REGULAR,
                pltpu.SemaphoreType.REGULAR,
            ],
            compiler_params=pltpu.CompilerParams(
                collective_id=0, has_side_effects=True, vmem_limit_bytes=24 << 20
            ),
        )(
            *(
                pltpu.with_memory_space_constraint(value, pltpu.HBM)
                for value in (
                    live_counts.reshape(1, n_tiles),
                    incidence.reshape(n_tiles * CAP * CORNERS, TILE),
                    lame_first.reshape(n_tiles, CAP),
                    shear_modulus.reshape(n_tiles, CAP),
                    stretch.reshape(3, n_tiles, CAP),
                )
            )
        )
        block = block * scale.reshape(1, 1, 1, TILE)
        return block.transpose(0, 2, 1, 3).reshape(1, 1, 1, 3, TILE, 3, TILE)

    return jax.shard_map(
        on_device,
        mesh=mesh,
        in_specs=(
            P("gx", "gy", "gz", None, None, None, None),
            P("gx", "gy", "gz", None),
            P("gx", "gy", "gz", None, None),
            P("gx", "gy", "gz", None, None),
            P(None, "gx", "gy", "gz", None, None),
        ),
        out_specs=P("gx", "gy", "gz", None, None, None, None),
        check_vma=False,
    )
```

```python
import functools

import jax
import jax.numpy as jnp
from jax import lax
from jax.experimental import pallas as pl
from jax.experimental.pallas import tpu as pltpu
from jax.sharding import PartitionSpec as P

MESH = pl.DeviceIdType.MESH
F32, BF16 = jnp.float32, jnp.bfloat16
TILE, CAP, CORNERS = 128, 16, 8

LEAD = 1
CAST = 3
EARLY = 4

ALL_MODES = (1, 2, 4, 3, 5, 6, 7)


def split(value):
    high = value.astype(BF16)
    return high, (value - high.astype(F32)).astype(BF16)


def swap_groups(values):
    sub = lax.broadcasted_iota(jnp.int32, (8, 128), 0)
    group = lax.broadcasted_iota(jnp.int32, (8, 128), 1) // CAP
    for bit in (1, 2, 4):
        upper_sub = (sub & bit) != 0
        upper_group = (group & bit) != 0
        below = pltpu.roll(pltpu.roll(values, 8 - bit, 0), CAP * bit, 1)
        above = pltpu.roll(pltpu.roll(values, bit, 0), 128 - CAP * bit, 1)
        values = jnp.where(
            upper_sub == upper_group, values, jnp.where(upper_sub, above, below)
        )
    return values


def kernel(
    n_x, n_y, n_z,
    live_hbm, inc_hbm, lame_hbm, shear_hbm, stretch_hbm,
    block_ref, scale_ref,
    live, inc, lame, shear, stretch, weight, number, place, params, send, recv, row, row_recv, hub_recv,
    in_sem, small_sem, send_sem, recv_sem, cast_sem, here, ready,
):
    n_tiles = send.shape[0]
    my_x, my_y, my_z = lax.axis_index("gx"), lax.axis_index("gy"), lax.axis_index("gz")
    n_xy = n_x * n_y

    last = 4
    short = 2 * CORNERS
    ends = [(inc.shape[0] - last * short) * k // last for k in range(last + 1)]
    ends += [inc.shape[0] - short * k for k in range(last - 1, -1, -1)]
    loads = [
        pltpu.make_async_copy(
            inc_hbm.at[pl.ds(first, end - first)], inc.at[pl.ds(first, end - first)], in_sem
        )
        for first, end in zip(ends, ends[1:])
    ]
    load = pltpu.make_async_copy(inc_hbm, inc, in_sem)
    small = [
        pltpu.make_async_copy(source, target, small_sem.at[k])
        for k, (source, target) in enumerate(
            ((live_hbm, live), (lame_hbm, lame), (shear_hbm, shear), (stretch_hbm, stretch))
        )
    ]
    for copy in small + loads:
        copy.start()

    def hops(step, size):
        return min(step, size - step)

    hubs = [(0, 0, LEAD), (0, 0, CAST)]
    hubs += [(i, 0, LEAD) for i in range(1, n_x)] + [(0, j, LEAD) for j in range(1, n_y)]

    def is_at(x, y, z):
        return jnp.logical_and(jnp.logical_and(my_x == x, my_y == y), my_z == z)

    in_corner = jnp.logical_and(my_x == 0, my_y == 0)
    on_edge = jnp.logical_or(my_x == 0, my_y == 0)
    is_lead = my_z == LEAD
    is_early = my_z < EARLY
    is_hub = jnp.logical_or(jnp.logical_and(on_edge, is_lead), is_at(0, 0, CAST))
    plane_steps = sorted(
        ((i, j) for i in range(n_x) for j in range(n_y)),
        key=lambda step: -hops(step[0], n_x) - hops(step[1], n_y),
    )
    line_steps = sorted(range(1, n_z), key=lambda step: -hops(step, n_z))

    barrier = pltpu.get_barrier_semaphore()

    def greet(x, y, z):
        pl.semaphore_signal(
            barrier, inc=1, device_id={"gx": x, "gy": y, "gz": z}, device_id_type=MESH
        )

    @pl.when(is_early)
    def _():
        for step in line_steps:
            greet(my_x, my_y, lax.rem(my_z + step, n_z))

    @pl.when(is_hub)
    def _():
        half = n_z // 2

        @pl.loop(0, half)
        def _(near):
            ahead = lax.rem(my_z + half + near, n_z)
            behind = lax.rem(my_z + jnp.where(near == 0, 0, half - near), n_z)
            for i, j in plane_steps:
                x, y = lax.rem(my_x + i, n_x), lax.rem(my_y + j, n_y)
                greet(x, y, ahead)
                if i or j:
                    greet(x, y, behind)
                else:

                    @pl.when(near > 0)
                    def _():
                        greet(x, y, behind)

    for copy in small:
        copy.wait()
    params[...] = jnp.zeros_like(params)
    first, second = lame[...], shear[...]
    lengths = [stretch[k] for k in range(3)]
    for k, value in enumerate([first, second] + lengths):
        params[:, k * CAP : (k + 1) * CAP] = value
    send[:, 1, :] = params[...]
    inverse = [1.0 / value for value in lengths]
    trace = (
        (lengths[0] * lengths[1] * lengths[2] / 9.0)
        * (first + 4.0 * second)
        * (inverse[0] * inverse[0] + inverse[1] * inverse[1] + inverse[2] * inverse[2])
    )
    diagonal = lax.broadcasted_iota(jnp.int32, (CAP, CAP), 0) == lax.broadcasted_iota(
        jnp.int32, (CAP, CAP), 1
    )
    slot_down = lax.broadcasted_iota(jnp.int32, (CAP, 1), 0)
    for t in range(n_tiles):
        column = jnp.sum(jnp.where(diagonal, trace[t : t + 1, :], 0.0), axis=1, keepdims=True)
        column = jnp.where(slot_down < live[0, t], column, 0.0)
        weight[t * CAP : (t + 1) * CAP, :] = jnp.broadcast_to(column, (CAP, TILE))

    down = lax.broadcasted_iota(jnp.int32, (TILE, TILE), 0)
    lane = lax.broadcasted_iota(jnp.int32, (TILE, TILE), 1)
    number[...] = (down + 1).astype(F32).astype(BF16)
    place[...] = jnp.where(lane == (down % CORNERS) * CAP + down // CORNERS, 1.0, 0.0)
    slot = lax.broadcasted_iota(jnp.int32, (1, TILE), 1) % CAP

    load.wait()
    sums = [jnp.zeros((CORNERS, TILE), F32) for _ in range(8)]
    for e in range(n_tiles * CAP):
        onehot = inc[e * CORNERS : (e + 1) * CORNERS, :].astype(F32)
        sums[e % 8] = sums[e % 8] + onehot * weight[e : e + 1, :]
    while len(sums) > 1:
        sums = [sums[k] + sums[k + 1] for k in range(0, len(sums), 2)]
    partial = jnp.sum(sums[0], axis=0, keepdims=True)
    row[...] = jnp.broadcast_to(jnp.sum(partial, axis=1, keepdims=True), (1, TILE))

    pl.semaphore_wait(
        barrier,
        len(hubs) + EARLY - jnp.where(is_hub, 1, 0) - jnp.where(is_early, 1, 0),
    )

    for x, y, z in hubs:
        source = lax.rem(my_x - x + n_x, n_x) * n_y + lax.rem(my_y - y + n_y, n_y)

        @pl.when(jnp.logical_not(is_at(x, y, z)))
        def _():
            pltpu.make_async_remote_copy(
                src_ref=row,
                dst_ref=hub_recv.at[source * n_z + lax.rem(my_z - z + n_z, n_z)],
                send_sem=send_sem.at[0],
                recv_sem=recv_sem.at[0],
                device_id={"gx": x, "gy": y, "gz": z},
                device_id_type=MESH,
            ).start()

    hub_recv[0] = row[...]

    @pl.when(jnp.logical_not(is_lead))
    def _():
        pl.semaphore_signal(here, inc=1, device_id={"gz": LEAD}, device_id_type=MESH)

    for t in range(n_tiles):
        onehot = inc[t * TILE : (t + 1) * TILE, :].astype(F32).astype(BF16)
        spread = jnp.dot(onehot, number[...], preferred_element_type=F32)
        ids = jnp.sum(spread * place[...], axis=0, keepdims=True)
        send[t, 0:1, :] = jnp.where(slot < live[0, t], ids, 0.0)

    def send_tile(z):
        @pl.when(my_z != z)
        def _():
            pltpu.make_async_remote_copy(
                src_ref=send.at[z],
                dst_ref=recv.at[lax.rem(my_z - z + n_z, n_z)],
                send_sem=send_sem.at[1],
                recv_sem=recv_sem.at[1],
                device_id={"gz": z},
                device_id_type=MESH,
            ).start()

    for z in range(EARLY):
        send_tile(z)
    recv[0] = send[my_z]

    @pl.when(is_lead)
    def _():
        pl.semaphore_wait(here, n_z - 1)
        for step in line_steps:
            pl.semaphore_signal(
                ready, inc=1, device_id={"gz": (LEAD + step) % n_z}, device_id_type=MESH
            )

    @pl.when(jnp.logical_not(is_lead))
    def _():
        pl.semaphore_wait(ready, 1)

    for z in range(EARLY, n_z):
        send_tile(z)

    def rows(target, count, send_with, recv_with):
        return pltpu.make_async_remote_copy(
            src_ref=target.at[pl.ds(1, count)],
            dst_ref=target.at[pl.ds(1, count)],
            send_sem=send_with,
            recv_sem=recv_with,
            device_id={"gz": lax.rem(my_z + 1, n_z)},
            device_id_type=MESH,
        )

    tiles = rows(recv, n_z - 1, send_sem.at[1], recv_sem.at[1])
    tiles.wait_recv()

    halves = range(n_z // 8)
    ids = jnp.concatenate([swap_groups(recv[8 * h : 8 * h + 8, 0, :]) for h in halves], axis=1)
    material = jnp.concatenate(
        [swap_groups(recv[8 * h : 8 * h + 8, 1, :]) for h in halves], axis=1
    )
    wide = ids.shape[1]
    first, second = material[0:1], material[1:2]
    h = [material[2 + k : 3 + k] for k in range(3)]

    node = (lax.broadcasted_iota(jnp.int32, (TILE, wide), 0) + 1).astype(F32)
    corner = [
        jnp.where(node == ids[p : p + 1], 1.0, 0.0).astype(BF16) for p in range(CORNERS)
    ]
    mode = corner
    for bit in (1, 2, 4):
        mode = [
            mode[k] - mode[k ^ bit] if k & bit else mode[k] + mode[k ^ bit]
            for k in range(CORNERS)
        ]

    def scaled(wave, coefficient):
        wide_row = jnp.broadcast_to(coefficient, (16, wide)).astype(BF16)
        return (wave.reshape(TILE // 16, 16, wide) * wide_row[None]).reshape(TILE, wide)

    def product(left, right):
        return lax.dot_general(
            left, right, (((1,), (1,)), ((), ())), preferred_element_type=F32
        )

    def assemble(pairs):
        high, low, other = [], [], []
        for left, right, coefficient in pairs:
            top = coefficient.astype(BF16).astype(F32)
            high.append(scaled(mode[left], top))
            low.append(scaled(mode[left], coefficient - top))
            other.append(mode[right])
        right = jnp.concatenate(other, axis=1)
        left = jnp.concatenate(
            [jnp.concatenate(high, axis=1), jnp.concatenate(low, axis=1)], axis=0
        )
        result = product(left, right)
        return result[:TILE] + result[TILE:]

    area = [h[1] * h[2] / (16.0 * h[0]), h[0] * h[2] / (16.0 * h[1]), h[0] * h[1] / (16.0 * h[2])]
    strong = first + 2.0 * second
    for i in range(3):
        alpha = [(strong if k == i else second) * area[k] for k in range(3)]
        coefficients = {
            1: alpha[0],
            2: alpha[1],
            4: alpha[2],
            3: (alpha[0] + alpha[1]) / 3.0,
            5: (alpha[0] + alpha[2]) / 3.0,
            6: (alpha[1] + alpha[2]) / 3.0,
            7: (alpha[0] + alpha[1] + alpha[2]) / 9.0,
        }
        block_ref[i, i] = assemble([(m, m, coefficients[m]) for m in ALL_MODES])
    for i, j, k in ((0, 1, 2), (0, 2, 1), (1, 2, 0)):
        a, b, c = 1 << i, 1 << j, 1 << k
        la, mu = h[k] * first / 16.0, h[k] * second / 16.0
        result = assemble(
            [
                (a, b, la),
                (a | c, b | c, la / 3.0),
                (b, a, mu),
                (b | c, a | c, mu / 3.0),
            ]
        )
        block_ref[i, j] = result
        block_ref[j, i] = result.T

    def sum_rows(values, count):
        lanes = min(8, count)
        sums = [values[k] for k in range(lanes)]
        for k in range(lanes, count):
            sums[k % lanes] = sums[k % lanes] + values[k]
        while len(sums) > 1:
            sums = [sums[k] + sums[k + 1] for k in range(0, len(sums), 2)]
        return sums[0]

    from_x, from_y = jnp.minimum(my_x, n_x - my_x), jnp.minimum(my_y, n_y - my_y)
    lead_x = jnp.logical_and(is_lead, jnp.logical_and(my_y == 0, my_x != 0))
    lead_y = jnp.logical_and(is_lead, jnp.logical_and(my_x == 0, my_y != 0))
    lines = [(0, 0, jnp.logical_and(is_hub, jnp.logical_not(is_at(0, 0, LEAD))))]
    lines += [
        (0, j, jnp.logical_and(lead_x, hops(j, n_y) <= from_x)) for j in range(1, n_y)
    ]
    lines += [(i, 0, jnp.logical_and(lead_y, from_y > hops(i, n_x))) for i in range(1, n_x)]

    @pl.when(is_hub)
    def _():
        rows(hub_recv, n_xy * n_z - 1, send_sem.at[0], recv_sem.at[0]).wait_recv()
        scale = (3.0 * TILE * n_xy * n_z) / sum_rows(hub_recv, n_xy * n_z)
        scale_ref[...] = scale
        row_recv[...] = scale
        @pl.when(jnp.logical_not(is_at(0, 0, LEAD)))
        def _():
            for which, (i, j, casts) in enumerate(lines):

                @pl.when(casts)
                def _():
                    for z in range(n_z):
                        copy = pltpu.make_async_remote_copy(
                            src_ref=row_recv,
                            dst_ref=row_recv,
                            send_sem=cast_sem.at[which],
                            recv_sem=recv_sem.at[2],
                            device_id={
                                "gx": lax.rem(my_x + i, n_x),
                                "gy": lax.rem(my_y + j, n_y),
                                "gz": z,
                            },
                            device_id_type=MESH,
                        )
                        if i or j:
                            copy.start()
                        else:
                            first_hub = jnp.logical_and(in_corner, z == LEAD)

                            @pl.when(jnp.logical_not(jnp.logical_or(my_z == z, first_hub)))
                            def _():
                                copy.start()

            for which, (i, j, casts) in enumerate(lines):
                if i or j:

                    @pl.when(casts)
                    def _():
                        rows(hub_recv, n_z, cast_sem.at[which], recv_sem.at[2]).wait_send()

            @pl.when(jnp.logical_and(is_lead, jnp.logical_not(in_corner)))
            def _():
                rows(hub_recv, n_z - 1, cast_sem.at[0], recv_sem.at[2]).wait_send()

            @pl.when(jnp.logical_not(is_lead))
            def _():
                rows(hub_recv, n_z - 2, cast_sem.at[0], recv_sem.at[2]).wait_send()

        rows(hub_recv, len(hubs) - 1, send_sem.at[0], recv_sem.at[0]).wait_send()

    @pl.when(jnp.logical_not(is_hub))
    def _():
        rows(hub_recv, 1, send_sem.at[2], recv_sem.at[2]).wait_recv()
        scale_ref[...] = row_recv[...]
        rows(hub_recv, len(hubs), send_sem.at[0], recv_sem.at[0]).wait_send()

    tiles.wait_send()


def solution(mesh):
    n_x, n_y, n_z = mesh.shape["gx"], mesh.shape["gy"], mesh.shape["gz"]
    n_xy = n_x * n_y

    def on_device(incidence, live_counts, lame_first, shear_modulus, stretch):
        n_tiles = incidence.shape[3]
        hbm = pl.BlockSpec(memory_space=pltpu.HBM)
        vmem = pl.BlockSpec(memory_space=pltpu.VMEM)
        block, scale = pl.pallas_call(
            functools.partial(kernel, n_x, n_y, n_z),
            out_shape=(
                jax.ShapeDtypeStruct((3, 3, TILE, TILE), F32),
                jax.ShapeDtypeStruct((1, TILE), F32),
            ),
            in_specs=[hbm] * 5,
            out_specs=(vmem, vmem),
            scratch_shapes=[
                pltpu.SMEM((1, n_tiles), jnp.int32),
                pltpu.VMEM((n_tiles * CAP * CORNERS, TILE), jnp.int32),
                pltpu.VMEM((n_tiles, CAP), F32),
                pltpu.VMEM((n_tiles, CAP), F32),
                pltpu.VMEM((3, n_tiles, CAP), F32),
                pltpu.VMEM((n_tiles * CAP, TILE), F32),
                pltpu.VMEM((TILE, TILE), BF16),
                pltpu.VMEM((TILE, TILE), F32),
                pltpu.VMEM((n_tiles, TILE), F32),
                pltpu.VMEM((n_z, 2, TILE), F32),
                pltpu.VMEM((n_z, 2, TILE), F32),
                pltpu.VMEM((1, TILE), F32),
                pltpu.VMEM((1, TILE), F32),
                pltpu.VMEM((n_xy * n_z, 1, TILE), F32),
                pltpu.SemaphoreType.DMA,
                pltpu.SemaphoreType.DMA((4,)),
                pltpu.SemaphoreType.DMA((3,)),
                pltpu.SemaphoreType.DMA((3,)),
                pltpu.SemaphoreType.DMA((n_x + n_y - 1,)),
                pltpu.SemaphoreType.REGULAR,
                pltpu.SemaphoreType.REGULAR,
            ],
            compiler_params=pltpu.CompilerParams(
                collective_id=0, has_side_effects=True, vmem_limit_bytes=24 << 20
            ),
        )(
            *(
                pltpu.with_memory_space_constraint(value, pltpu.HBM)
                for value in (
                    live_counts.reshape(1, n_tiles),
                    incidence.reshape(n_tiles * CAP * CORNERS, TILE),
                    lame_first.reshape(n_tiles, CAP),
                    shear_modulus.reshape(n_tiles, CAP),
                    stretch.reshape(3, n_tiles, CAP),
                )
            )
        )
        block = block * scale.reshape(1, 1, 1, TILE)
        return block.transpose(0, 2, 1, 3).reshape(1, 1, 1, 3, TILE, 3, TILE)

    return jax.shard_map(
        on_device,
        mesh=mesh,
        in_specs=(
            P("gx", "gy", "gz", None, None, None, None),
            P("gx", "gy", "gz", None),
            P("gx", "gy", "gz", None, None),
            P("gx", "gy", "gz", None, None),
            P(None, "gx", "gy", "gz", None, None),
        ),
        out_specs=P("gx", "gy", "gz", None, None, None, None),
        check_vma=False,
    )
```

```python
import functools

import jax
import jax.numpy as jnp
from jax import lax
from jax.experimental import pallas as pl
from jax.experimental.pallas import tpu as pltpu
from jax.sharding import PartitionSpec as P

MESH = pl.DeviceIdType.MESH
F32, BF16 = jnp.float32, jnp.bfloat16
TILE, CAP, CORNERS = 128, 16, 8

LEAD = 1
CAST = 3
EARLY = 4

ALL_MODES = (1, 2, 4, 3, 5, 6, 7)


def split(value):
    high = value.astype(BF16)
    return high, (value - high.astype(F32)).astype(BF16)


def swap_groups(values):
    sub = lax.broadcasted_iota(jnp.int32, (8, 128), 0)
    group = lax.broadcasted_iota(jnp.int32, (8, 128), 1) // CAP
    for bit in (1, 2, 4):
        upper_sub = (sub & bit) != 0
        upper_group = (group & bit) != 0
        below = pltpu.roll(pltpu.roll(values, 8 - bit, 0), CAP * bit, 1)
        above = pltpu.roll(pltpu.roll(values, bit, 0), 128 - CAP * bit, 1)
        values = jnp.where(
            upper_sub == upper_group, values, jnp.where(upper_sub, above, below)
        )
    return values


def kernel(
    n_x, n_y, n_z,
    live_hbm, inc_hbm, lame_hbm, shear_hbm, stretch_hbm,
    block_ref, scale_ref,
    live, inc, lame, shear, stretch, weight, number, place, params, send, recv, row, row_recv, hub_recv,
    in_sem, small_sem, send_sem, recv_sem, cast_sem, here, ready,
):
    n_tiles = send.shape[0]
    my_x, my_y, my_z = lax.axis_index("gx"), lax.axis_index("gy"), lax.axis_index("gz")
    n_xy = n_x * n_y

    last = 4
    short = 2 * CORNERS
    main = inc.shape[0] - last * short
    ends = [main // CORNERS * k // last * CORNERS for k in range(last + 1)]
    ends += [main + short * (k + 1) for k in range(last)]
    loads = [
        pltpu.make_async_copy(
            inc_hbm.at[pl.ds(first, end - first)],
            inc.at[pl.ds(first, end - first)],
            in_sem.at[min(k, last)],
        )
        for k, (first, end) in enumerate(zip(ends, ends[1:]))
    ]
    rest = pl.ds(main, last * short)
    arrivals = loads[:last] + [
        pltpu.make_async_copy(inc_hbm.at[rest], inc.at[rest], in_sem.at[last])
    ]
    starts = {end // CORNERS: copy for end, copy in zip(ends, arrivals)}
    small = [
        pltpu.make_async_copy(source, target, small_sem.at[k])
        for k, (source, target) in enumerate(
            ((live_hbm, live), (lame_hbm, lame), (shear_hbm, shear), (stretch_hbm, stretch))
        )
    ]
    for copy in small + loads:
        copy.start()

    def hops(step, size):
        return min(step, size - step)

    hubs = [(0, 0, LEAD), (0, 0, CAST)]
    hubs += [(i, 0, LEAD) for i in range(1, n_x)] + [(0, j, LEAD) for j in range(1, n_y)]

    def is_at(x, y, z):
        return jnp.logical_and(jnp.logical_and(my_x == x, my_y == y), my_z == z)

    in_corner = jnp.logical_and(my_x == 0, my_y == 0)
    on_edge = jnp.logical_or(my_x == 0, my_y == 0)
    is_lead = my_z == LEAD
    is_early = my_z < EARLY
    is_hub = jnp.logical_or(jnp.logical_and(on_edge, is_lead), is_at(0, 0, CAST))
    plane_steps = sorted(
        ((i, j) for i in range(n_x) for j in range(n_y)),
        key=lambda step: -hops(step[0], n_x) - hops(step[1], n_y),
    )
    line_steps = sorted(range(1, n_z), key=lambda step: -hops(step, n_z))

    barrier = pltpu.get_barrier_semaphore()

    def greet(x, y, z):
        pl.semaphore_signal(
            barrier, inc=1, device_id={"gx": x, "gy": y, "gz": z}, device_id_type=MESH
        )

    @pl.when(is_early)
    def _():
        for step in line_steps:
            greet(my_x, my_y, lax.rem(my_z + step, n_z))

    @pl.when(is_hub)
    def _():
        half = n_z // 2

        @pl.loop(0, half)
        def _(near):
            ahead = lax.rem(my_z + half + near, n_z)
            behind = lax.rem(my_z + jnp.where(near == 0, 0, half - near), n_z)
            for i, j in plane_steps:
                x, y = lax.rem(my_x + i, n_x), lax.rem(my_y + j, n_y)
                greet(x, y, ahead)
                if i or j:
                    greet(x, y, behind)
                else:

                    @pl.when(near > 0)
                    def _():
                        greet(x, y, behind)

    for copy in small:
        copy.wait()
    params[...] = jnp.zeros_like(params)
    first, second = lame[...], shear[...]
    lengths = [stretch[k] for k in range(3)]
    for k, value in enumerate([first, second] + lengths):
        params[:, k * CAP : (k + 1) * CAP] = value
    send[:, 1, :] = params[...]
    inverse = [1.0 / value for value in lengths]
    trace = (
        (lengths[0] * lengths[1] * lengths[2] / 9.0)
        * (first + 4.0 * second)
        * (inverse[0] * inverse[0] + inverse[1] * inverse[1] + inverse[2] * inverse[2])
    )
    diagonal = lax.broadcasted_iota(jnp.int32, (CAP, CAP), 0) == lax.broadcasted_iota(
        jnp.int32, (CAP, CAP), 1
    )
    slot_down = lax.broadcasted_iota(jnp.int32, (CAP, 1), 0)
    for t in range(n_tiles):
        column = jnp.sum(jnp.where(diagonal, trace[t : t + 1, :], 0.0), axis=1, keepdims=True)
        column = jnp.where(slot_down < live[0, t], column, 0.0)
        weight[t * CAP : (t + 1) * CAP, :] = jnp.broadcast_to(column, (CAP, TILE))

    down = lax.broadcasted_iota(jnp.int32, (TILE, TILE), 0)
    lane = lax.broadcasted_iota(jnp.int32, (TILE, TILE), 1)
    number[...] = (down + 1).astype(F32).astype(BF16)
    place[...] = jnp.where(lane == (down % CORNERS) * CAP + down // CORNERS, 1.0, 0.0)
    slot = lax.broadcasted_iota(jnp.int32, (1, TILE), 1) % CAP

    sums = [jnp.zeros((CORNERS, TILE), F32) for _ in range(8)]
    for e in range(n_tiles * CAP):
        if e in starts:
            starts[e].wait()
        onehot = inc[e * CORNERS : (e + 1) * CORNERS, :].astype(F32)
        sums[e % 8] = sums[e % 8] + onehot * weight[e : e + 1, :]
    while len(sums) > 1:
        sums = [sums[k] + sums[k + 1] for k in range(0, len(sums), 2)]
    partial = jnp.sum(sums[0], axis=0, keepdims=True)
    row[...] = jnp.broadcast_to(jnp.sum(partial, axis=1, keepdims=True), (1, TILE))

    pl.semaphore_wait(
        barrier,
        len(hubs) + EARLY - jnp.where(is_hub, 1, 0) - jnp.where(is_early, 1, 0),
    )

    for x, y, z in hubs:
        source = lax.rem(my_x - x + n_x, n_x) * n_y + lax.rem(my_y - y + n_y, n_y)

        @pl.when(jnp.logical_not(is_at(x, y, z)))
        def _():
            pltpu.make_async_remote_copy(
                src_ref=row,
                dst_ref=hub_recv.at[source * n_z + lax.rem(my_z - z + n_z, n_z)],
                send_sem=send_sem.at[0],
                recv_sem=recv_sem.at[0],
                device_id={"gx": x, "gy": y, "gz": z},
                device_id_type=MESH,
            ).start()

    hub_recv[0] = row[...]

    @pl.when(jnp.logical_not(is_lead))
    def _():
        pl.semaphore_signal(here, inc=1, device_id={"gz": LEAD}, device_id_type=MESH)

    for t in range(n_tiles):
        onehot = inc[t * TILE : (t + 1) * TILE, :].astype(F32).astype(BF16)
        spread = jnp.dot(onehot, number[...], preferred_element_type=F32)
        ids = jnp.sum(spread * place[...], axis=0, keepdims=True)
        send[t, 0:1, :] = jnp.where(slot < live[0, t], ids, 0.0)

    def send_tile(z):
        @pl.when(my_z != z)
        def _():
            pltpu.make_async_remote_copy(
                src_ref=send.at[z],
                dst_ref=recv.at[lax.rem(my_z - z + n_z, n_z)],
                send_sem=send_sem.at[1],
                recv_sem=recv_sem.at[1],
                device_id={"gz": z},
                device_id_type=MESH,
            ).start()

    for z in range(EARLY):
        send_tile(z)
    recv[0] = send[my_z]

    @pl.when(is_lead)
    def _():
        pl.semaphore_wait(here, n_z - 1)
        for step in line_steps:
            pl.semaphore_signal(
                ready, inc=1, device_id={"gz": (LEAD + step) % n_z}, device_id_type=MESH
            )

    @pl.when(jnp.logical_not(is_lead))
    def _():
        pl.semaphore_wait(ready, 1)

    for z in range(EARLY, n_z):
        send_tile(z)

    def rows(target, count, send_with, recv_with):
        return pltpu.make_async_remote_copy(
            src_ref=target.at[pl.ds(1, count)],
            dst_ref=target.at[pl.ds(1, count)],
            send_sem=send_with,
            recv_sem=recv_with,
            device_id={"gz": lax.rem(my_z + 1, n_z)},
            device_id_type=MESH,
        )

    tiles = rows(recv, n_z - 1, send_sem.at[1], recv_sem.at[1])
    tiles.wait_recv()

    halves = range(n_z // 8)
    ids = jnp.concatenate([swap_groups(recv[8 * h : 8 * h + 8, 0, :]) for h in halves], axis=1)
    material = jnp.concatenate(
        [swap_groups(recv[8 * h : 8 * h + 8, 1, :]) for h in halves], axis=1
    )
    wide = ids.shape[1]
    first, second = material[0:1], material[1:2]
    h = [material[2 + k : 3 + k] for k in range(3)]

    node = (lax.broadcasted_iota(jnp.int32, (TILE, wide), 0) + 1).astype(F32)
    corner = [
        jnp.where(node == ids[p : p + 1], 1.0, 0.0).astype(BF16) for p in range(CORNERS)
    ]
    mode = corner
    for bit in (1, 2, 4):
        mode = [
            mode[k] - mode[k ^ bit] if k & bit else mode[k] + mode[k ^ bit]
            for k in range(CORNERS)
        ]

    def scaled(wave, coefficient):
        wide_row = jnp.broadcast_to(coefficient, (16, wide)).astype(BF16)
        return (wave.reshape(TILE // 16, 16, wide) * wide_row[None]).reshape(TILE, wide)

    def product(left, right):
        return lax.dot_general(
            left, right, (((1,), (1,)), ((), ())), preferred_element_type=F32
        )

    def assemble(pairs):
        high, low, other = [], [], []
        for left, right, coefficient in pairs:
            top = coefficient.astype(BF16).astype(F32)
            high.append(scaled(mode[left], top))
            low.append(scaled(mode[left], coefficient - top))
            other.append(mode[right])
        right = jnp.concatenate(other, axis=1)
        left = jnp.concatenate(
            [jnp.concatenate(high, axis=1), jnp.concatenate(low, axis=1)], axis=0
        )
        result = product(left, right)
        return result[:TILE] + result[TILE:]

    area = [h[1] * h[2] / (16.0 * h[0]), h[0] * h[2] / (16.0 * h[1]), h[0] * h[1] / (16.0 * h[2])]
    strong = first + 2.0 * second
    for i in range(3):
        alpha = [(strong if k == i else second) * area[k] for k in range(3)]
        coefficients = {
            1: alpha[0],
            2: alpha[1],
            4: alpha[2],
            3: (alpha[0] + alpha[1]) / 3.0,
            5: (alpha[0] + alpha[2]) / 3.0,
            6: (alpha[1] + alpha[2]) / 3.0,
            7: (alpha[0] + alpha[1] + alpha[2]) / 9.0,
        }
        block_ref[i, i] = assemble([(m, m, coefficients[m]) for m in ALL_MODES])
    for i, j, k in ((0, 1, 2), (0, 2, 1), (1, 2, 0)):
        a, b, c = 1 << i, 1 << j, 1 << k
        la, mu = h[k] * first / 16.0, h[k] * second / 16.0
        result = assemble(
            [
                (a, b, la),
                (a | c, b | c, la / 3.0),
                (b, a, mu),
                (b | c, a | c, mu / 3.0),
            ]
        )
        block_ref[i, j] = result
        block_ref[j, i] = result.T

    def sum_rows(values, count):
        lanes = min(8, count)
        sums = [values[k] for k in range(lanes)]
        for k in range(lanes, count):
            sums[k % lanes] = sums[k % lanes] + values[k]
        while len(sums) > 1:
            sums = [sums[k] + sums[k + 1] for k in range(0, len(sums), 2)]
        return sums[0]

    from_x, from_y = jnp.minimum(my_x, n_x - my_x), jnp.minimum(my_y, n_y - my_y)
    lead_x = jnp.logical_and(is_lead, jnp.logical_and(my_y == 0, my_x != 0))
    lead_y = jnp.logical_and(is_lead, jnp.logical_and(my_x == 0, my_y != 0))
    lines = [(0, 0, jnp.logical_and(is_hub, jnp.logical_not(is_at(0, 0, LEAD))))]
    lines += [
        (0, j, jnp.logical_and(lead_x, hops(j, n_y) <= from_x)) for j in range(1, n_y)
    ]
    lines += [(i, 0, jnp.logical_and(lead_y, from_y > hops(i, n_x))) for i in range(1, n_x)]

    owned_at_x = {
        i: 1 + sum(hops(j, n_y) <= hops(i, n_x) for j in range(1, n_y)) for i in range(1, n_x)
    }
    owned_at_y = {
        j: 1 + sum(hops(j, n_y) > hops(i, n_x) for i in range(1, n_x)) for j in range(1, n_y)
    }

    @pl.when(is_hub)
    def _():
        rows(hub_recv, n_xy * n_z - 1, send_sem.at[0], recv_sem.at[0]).wait_recv()
        scale = (3.0 * TILE * n_xy * n_z) / sum_rows(hub_recv, n_xy * n_z)
        scale_ref[...] = scale
        row_recv[...] = scale
        @pl.when(jnp.logical_not(is_at(0, 0, LEAD)))
        def _():
            for i, j, casts in lines:

                @pl.when(casts)
                def _():
                    for z in range(n_z):
                        copy = pltpu.make_async_remote_copy(
                            src_ref=row_recv,
                            dst_ref=row_recv,
                            send_sem=cast_sem,
                            recv_sem=recv_sem.at[2],
                            device_id={
                                "gx": lax.rem(my_x + i, n_x),
                                "gy": lax.rem(my_y + j, n_y),
                                "gz": z,
                            },
                            device_id_type=MESH,
                        )
                        if i or j:
                            copy.start()
                        else:
                            first_hub = jnp.logical_and(in_corner, z == LEAD)

                            @pl.when(jnp.logical_not(jnp.logical_or(my_z == z, first_hub)))
                            def _():
                                copy.start()

            for owned in sorted({0} | set(owned_at_x.values()) | set(owned_at_y.values())):
                own = n_z - 1 if owned else n_z - 2
                is_so = is_at(0, 0, CAST) if owned == 0 else False
                for i, count in owned_at_x.items():
                    if count == owned:
                        is_so = jnp.logical_or(is_so, is_at(i, 0, LEAD))
                for j, count in owned_at_y.items():
                    if count == owned:
                        is_so = jnp.logical_or(is_so, is_at(0, j, LEAD))

                @pl.when(is_so)
                def _():
                    rows(hub_recv, max(owned - 1, 0) * n_z + own, cast_sem, recv_sem.at[2]).wait_send()

        rows(hub_recv, len(hubs) - 1, send_sem.at[0], recv_sem.at[0]).wait_send()

    @pl.when(jnp.logical_not(is_hub))
    def _():
        rows(hub_recv, 1, send_sem.at[2], recv_sem.at[2]).wait_recv()
        scale_ref[...] = row_recv[...]
        rows(hub_recv, len(hubs), send_sem.at[0], recv_sem.at[0]).wait_send()

    tiles.wait_send()


def solution(mesh):
    n_x, n_y, n_z = mesh.shape["gx"], mesh.shape["gy"], mesh.shape["gz"]
    n_xy = n_x * n_y

    def on_device(incidence, live_counts, lame_first, shear_modulus, stretch):
        n_tiles = incidence.shape[3]
        hbm = pl.BlockSpec(memory_space=pltpu.HBM)
        vmem = pl.BlockSpec(memory_space=pltpu.VMEM)
        block, scale = pl.pallas_call(
            functools.partial(kernel, n_x, n_y, n_z),
            out_shape=(
                jax.ShapeDtypeStruct((3, 3, TILE, TILE), F32),
                jax.ShapeDtypeStruct((1, TILE), F32),
            ),
            in_specs=[hbm] * 5,
            out_specs=(vmem, vmem),
            scratch_shapes=[
                pltpu.SMEM((1, n_tiles), jnp.int32),
                pltpu.VMEM((n_tiles * CAP * CORNERS, TILE), jnp.int32),
                pltpu.VMEM((n_tiles, CAP), F32),
                pltpu.VMEM((n_tiles, CAP), F32),
                pltpu.VMEM((3, n_tiles, CAP), F32),
                pltpu.VMEM((n_tiles * CAP, TILE), F32),
                pltpu.VMEM((TILE, TILE), BF16),
                pltpu.VMEM((TILE, TILE), F32),
                pltpu.VMEM((n_tiles, TILE), F32),
                pltpu.VMEM((n_z, 2, TILE), F32),
                pltpu.VMEM((n_z, 2, TILE), F32),
                pltpu.VMEM((1, TILE), F32),
                pltpu.VMEM((1, TILE), F32),
                pltpu.VMEM((n_xy * n_z, 1, TILE), F32),
                pltpu.SemaphoreType.DMA((5,)),
                pltpu.SemaphoreType.DMA((4,)),
                pltpu.SemaphoreType.DMA((3,)),
                pltpu.SemaphoreType.DMA((3,)),
                pltpu.SemaphoreType.DMA,
                pltpu.SemaphoreType.REGULAR,
                pltpu.SemaphoreType.REGULAR,
            ],
            compiler_params=pltpu.CompilerParams(
                collective_id=0, has_side_effects=True, vmem_limit_bytes=24 << 20
            ),
        )(
            *(
                pltpu.with_memory_space_constraint(value, pltpu.HBM)
                for value in (
                    live_counts.reshape(1, n_tiles),
                    incidence.reshape(n_tiles * CAP * CORNERS, TILE),
                    lame_first.reshape(n_tiles, CAP),
                    shear_modulus.reshape(n_tiles, CAP),
                    stretch.reshape(3, n_tiles, CAP),
                )
            )
        )
        block = block * scale.reshape(1, 1, 1, TILE)
        return block.transpose(0, 2, 1, 3).reshape(1, 1, 1, 3, TILE, 3, TILE)

    return jax.shard_map(
        on_device,
        mesh=mesh,
        in_specs=(
            P("gx", "gy", "gz", None, None, None, None),
            P("gx", "gy", "gz", None),
            P("gx", "gy", "gz", None, None),
            P("gx", "gy", "gz", None, None),
            P(None, "gx", "gy", "gz", None, None),
        ),
        out_specs=P("gx", "gy", "gz", None, None, None, None),
        check_vma=False,
    )
```

```python
import functools

import jax
import jax.numpy as jnp
from jax import lax
from jax.experimental import pallas as pl
from jax.experimental.pallas import tpu as pltpu
from jax.sharding import PartitionSpec as P

MESH = pl.DeviceIdType.MESH
F32, BF16 = jnp.float32, jnp.bfloat16
TILE, CAP, CORNERS = 128, 16, 8

LEAD = 1
CAST = 3
EARLY = 4

ALL_MODES = (1, 2, 4, 3, 5, 6, 7)


def split(value):
    high = value.astype(BF16)
    return high, (value - high.astype(F32)).astype(BF16)


def swap_groups(values):
    sub = lax.broadcasted_iota(jnp.int32, (8, 128), 0)
    group = lax.broadcasted_iota(jnp.int32, (8, 128), 1) // CAP
    for bit in (1, 2, 4):
        upper_sub = (sub & bit) != 0
        upper_group = (group & bit) != 0
        below = pltpu.roll(pltpu.roll(values, 8 - bit, 0), CAP * bit, 1)
        above = pltpu.roll(pltpu.roll(values, bit, 0), 128 - CAP * bit, 1)
        values = jnp.where(
            upper_sub == upper_group, values, jnp.where(upper_sub, above, below)
        )
    return values


def kernel(
    n_x, n_y, n_z,
    live_hbm, inc_hbm, lame_hbm, shear_hbm, stretch_hbm,
    block_ref, scale_ref,
    live, inc, tail, lame, shear, stretch, alive, weight, number, place, params, send, recv, row, row_recv, hub_recv,
    tail_sem, in_sem, send_sem, recv_sem, cast_sem, here, ready,
):
    n_tiles = send.shape[0]
    my_x, my_y, my_z = lax.axis_index("gx"), lax.axis_index("gy"), lax.axis_index("gz")
    n_xy = n_x * n_y

    last = 4
    main = inc.shape[0] - 2 * CORNERS
    ends = [main // CORNERS * k // last * CORNERS for k in range(last + 1)] + [main + CORNERS]
    tail_load = pltpu.make_async_copy(
        inc_hbm.at[pl.ds(main + CORNERS, CORNERS)], tail, tail_sem
    )
    small = [
        pltpu.make_async_copy(source, target, in_sem.at[k])
        for k, (source, target) in enumerate(
            ((live_hbm, live), (lame_hbm, lame), (shear_hbm, shear), (stretch_hbm, stretch))
        )
    ]
    loads = [
        pltpu.make_async_copy(
            inc_hbm.at[pl.ds(first, end - first)],
            inc.at[pl.ds(first, end - first)],
            in_sem.at[len(small) + k],
        )
        for k, (first, end) in enumerate(zip(ends, ends[1:]))
    ]
    starts = {end // CORNERS: copy for end, copy in zip(ends, loads)}
    for copy in [tail_load] + small + loads:
        copy.start()

    def hops(step, size):
        return min(step, size - step)

    hubs = [(0, 0, LEAD), (0, 0, CAST)]
    hubs += [(i, 0, LEAD) for i in range(1, n_x)] + [(0, j, LEAD) for j in range(1, n_y)]

    def is_at(x, y, z):
        return jnp.logical_and(jnp.logical_and(my_x == x, my_y == y), my_z == z)

    in_corner = jnp.logical_and(my_x == 0, my_y == 0)
    on_edge = jnp.logical_or(my_x == 0, my_y == 0)
    is_lead = my_z == LEAD
    is_early = my_z < EARLY
    is_hub = jnp.logical_or(jnp.logical_and(on_edge, is_lead), is_at(0, 0, CAST))
    plane_steps = sorted(
        ((i, j) for i in range(n_x) for j in range(n_y)),
        key=lambda step: -hops(step[0], n_x) - hops(step[1], n_y),
    )
    line_steps = sorted(range(1, n_z), key=lambda step: -hops(step, n_z))

    barrier = pltpu.get_barrier_semaphore()

    def greet(x, y, z):
        pl.semaphore_signal(
            barrier, inc=1, device_id={"gx": x, "gy": y, "gz": z}, device_id_type=MESH
        )

    @pl.when(is_early)
    def _():
        for step in line_steps:
            greet(my_x, my_y, lax.rem(my_z + step, n_z))

    @pl.when(is_hub)
    def _():
        half = n_z // 2

        @pl.loop(0, half)
        def _(near):
            ahead = lax.rem(my_z + half + near, n_z)
            behind = lax.rem(my_z + jnp.where(near == 0, 0, half - near), n_z)
            for i, j in plane_steps:
                x, y = lax.rem(my_x + i, n_x), lax.rem(my_y + j, n_y)
                greet(x, y, ahead)
                if i or j:
                    greet(x, y, behind)
                else:

                    @pl.when(near > 0)
                    def _():
                        greet(x, y, behind)

    for copy in small:
        copy.wait()
    params[...] = jnp.zeros_like(params)
    first, second = lame[...], shear[...]
    lengths = [stretch[k] for k in range(3)]
    for k, value in enumerate([first, second] + lengths):
        params[:, k * CAP : (k + 1) * CAP] = value
    send[:, 1, :] = params[...]
    inverse = [1.0 / value for value in lengths]
    trace = (
        (lengths[0] * lengths[1] * lengths[2] / 9.0)
        * (first + 4.0 * second)
        * (inverse[0] * inverse[0] + inverse[1] * inverse[1] + inverse[2] * inverse[2])
    )
    diagonal = lax.broadcasted_iota(jnp.int32, (CAP, CAP), 0) == lax.broadcasted_iota(
        jnp.int32, (CAP, CAP), 1
    )
    counts = jnp.broadcast_to(live[...].astype(F32), (n_tiles, n_tiles))
    tile_down = lax.broadcasted_iota(jnp.int32, (n_tiles, n_tiles), 0)
    tile_across = lax.broadcasted_iota(jnp.int32, (n_tiles, n_tiles), 1)
    counts = jnp.sum(jnp.where(tile_down == tile_across, counts, 0.0), axis=1, keepdims=True)
    slot = lax.broadcasted_iota(jnp.int32, (n_tiles, TILE), 1) % CAP
    alive[...] = jnp.where(slot.astype(F32) < counts, 1.0, 0.0)
    trace = trace * alive[:, :CAP]
    for t in range(n_tiles):
        column = jnp.sum(jnp.where(diagonal, trace[t : t + 1, :], 0.0), axis=1, keepdims=True)
        weight[t * CAP : (t + 1) * CAP, :] = jnp.broadcast_to(column, (CAP, TILE))

    down = lax.broadcasted_iota(jnp.int32, (TILE, TILE), 0)
    lane = lax.broadcasted_iota(jnp.int32, (TILE, TILE), 1)
    number[...] = (down + 1).astype(F32).astype(BF16)
    place[...] = jnp.where(lane == (down % CORNERS) * CAP + down // CORNERS, 1.0, 0.0)

    sums = [jnp.zeros((CORNERS, TILE), F32) for _ in range(8)]
    for e in range(n_tiles * CAP):
        if e in starts:
            starts[e].wait()
        if e == n_tiles * CAP - 1:
            tail_load.wait()
            inc[main + CORNERS : main + 2 * CORNERS, :] = tail[...]
        onehot = inc[e * CORNERS : (e + 1) * CORNERS, :].astype(F32)
        sums[e % 8] = sums[e % 8] + onehot * weight[e : e + 1, :]
    while len(sums) > 1:
        sums = [sums[k] + sums[k + 1] for k in range(0, len(sums), 2)]
    partial = jnp.sum(sums[0], axis=0, keepdims=True)
    row[...] = jnp.broadcast_to(jnp.sum(partial, axis=1, keepdims=True), (1, TILE))

    pl.semaphore_wait(
        barrier,
        len(hubs) + EARLY - jnp.where(is_hub, 1, 0) - jnp.where(is_early, 1, 0),
    )

    for x, y, z in hubs:
        source = lax.rem(my_x - x + n_x, n_x) * n_y + lax.rem(my_y - y + n_y, n_y)

        @pl.when(jnp.logical_not(is_at(x, y, z)))
        def _():
            pltpu.make_async_remote_copy(
                src_ref=row,
                dst_ref=hub_recv.at[source * n_z + lax.rem(my_z - z + n_z, n_z)],
                send_sem=send_sem.at[0],
                recv_sem=recv_sem.at[0],
                device_id={"gx": x, "gy": y, "gz": z},
                device_id_type=MESH,
            ).start()

    hub_recv[0] = row[...]

    @pl.when(jnp.logical_not(is_lead))
    def _():
        pl.semaphore_signal(here, inc=1, device_id={"gz": LEAD}, device_id_type=MESH)

    for t in range(n_tiles):
        onehot = inc[t * TILE : (t + 1) * TILE, :].astype(F32).astype(BF16)
        spread = jnp.dot(onehot, number[...], preferred_element_type=F32)
        ids = jnp.sum(spread * place[...], axis=0, keepdims=True)
        send[t, 0:1, :] = ids * alive[t : t + 1, :]

    def send_tile(z):
        @pl.when(my_z != z)
        def _():
            pltpu.make_async_remote_copy(
                src_ref=send.at[z],
                dst_ref=recv.at[lax.rem(my_z - z + n_z, n_z)],
                send_sem=send_sem.at[1],
                recv_sem=recv_sem.at[1],
                device_id={"gz": z},
                device_id_type=MESH,
            ).start()

    for z in range(EARLY):
        send_tile(z)
    recv[0] = send[my_z]

    @pl.when(is_lead)
    def _():
        pl.semaphore_wait(here, n_z - 1)
        for step in line_steps:
            pl.semaphore_signal(
                ready, inc=1, device_id={"gz": (LEAD + step) % n_z}, device_id_type=MESH
            )

    @pl.when(jnp.logical_not(is_lead))
    def _():
        pl.semaphore_wait(ready, 1)

    for z in range(EARLY, n_z):
        send_tile(z)

    def rows(target, count, send_with, recv_with):
        return pltpu.make_async_remote_copy(
            src_ref=target.at[pl.ds(1, count)],
            dst_ref=target.at[pl.ds(1, count)],
            send_sem=send_with,
            recv_sem=recv_with,
            device_id={"gz": lax.rem(my_z + 1, n_z)},
            device_id_type=MESH,
        )

    tiles = rows(recv, n_z - 1, send_sem.at[1], recv_sem.at[1])
    tiles.wait_recv()

    halves = range(n_z // 8)
    ids = jnp.concatenate([swap_groups(recv[8 * h : 8 * h + 8, 0, :]) for h in halves], axis=1)
    material = jnp.concatenate(
        [swap_groups(recv[8 * h : 8 * h + 8, 1, :]) for h in halves], axis=1
    )
    wide = ids.shape[1]
    first, second = material[0:1], material[1:2]
    h = [material[2 + k : 3 + k] for k in range(3)]

    node = (lax.broadcasted_iota(jnp.int32, (TILE, wide), 0) + 1).astype(F32)
    corner = [
        jnp.where(node == ids[p : p + 1], 1.0, 0.0).astype(BF16) for p in range(CORNERS)
    ]
    mode = corner
    for bit in (1, 2, 4):
        mode = [
            mode[k] - mode[k ^ bit] if k & bit else mode[k] + mode[k ^ bit]
            for k in range(CORNERS)
        ]

    def scaled(wave, coefficient):
        wide_row = jnp.broadcast_to(coefficient, (16, wide)).astype(BF16)
        return (wave.reshape(TILE // 16, 16, wide) * wide_row[None]).reshape(TILE, wide)

    def product(left, right):
        return lax.dot_general(
            left, right, (((1,), (1,)), ((), ())), preferred_element_type=F32
        )

    def assemble(pairs):
        high, low, other = [], [], []
        for left, right, coefficient in pairs:
            top = coefficient.astype(BF16).astype(F32)
            high.append(scaled(mode[left], top))
            low.append(scaled(mode[left], coefficient - top))
            other.append(mode[right])
        right = jnp.concatenate(other, axis=1)
        left = jnp.concatenate(
            [jnp.concatenate(high, axis=1), jnp.concatenate(low, axis=1)], axis=0
        )
        result = product(left, right)
        return result[:TILE] + result[TILE:]

    area = [h[1] * h[2] / (16.0 * h[0]), h[0] * h[2] / (16.0 * h[1]), h[0] * h[1] / (16.0 * h[2])]
    strong = first + 2.0 * second
    for i in range(3):
        alpha = [(strong if k == i else second) * area[k] for k in range(3)]
        coefficients = {
            1: alpha[0],
            2: alpha[1],
            4: alpha[2],
            3: (alpha[0] + alpha[1]) / 3.0,
            5: (alpha[0] + alpha[2]) / 3.0,
            6: (alpha[1] + alpha[2]) / 3.0,
            7: (alpha[0] + alpha[1] + alpha[2]) / 9.0,
        }
        block_ref[i, i] = assemble([(m, m, coefficients[m]) for m in ALL_MODES])
    for i, j, k in ((0, 1, 2), (0, 2, 1), (1, 2, 0)):
        a, b, c = 1 << i, 1 << j, 1 << k
        la, mu = h[k] * first / 16.0, h[k] * second / 16.0
        result = assemble(
            [
                (a, b, la),
                (a | c, b | c, la / 3.0),
                (b, a, mu),
                (b | c, a | c, mu / 3.0),
            ]
        )
        block_ref[i, j] = result
        block_ref[j, i] = result.T

    def sum_rows(values, count):
        lanes = min(8, count)
        sums = [values[k] for k in range(lanes)]
        for k in range(lanes, count):
            sums[k % lanes] = sums[k % lanes] + values[k]
        while len(sums) > 1:
            sums = [sums[k] + sums[k + 1] for k in range(0, len(sums), 2)]
        return sums[0]

    from_x, from_y = jnp.minimum(my_x, n_x - my_x), jnp.minimum(my_y, n_y - my_y)
    lead_x = jnp.logical_and(is_lead, jnp.logical_and(my_y == 0, my_x != 0))
    lead_y = jnp.logical_and(is_lead, jnp.logical_and(my_x == 0, my_y != 0))
    lines = [(0, 0, jnp.logical_and(is_hub, jnp.logical_not(is_at(0, 0, LEAD))))]
    lines += [
        (0, j, jnp.logical_and(lead_x, hops(j, n_y) <= from_x)) for j in range(1, n_y)
    ]
    lines += [(i, 0, jnp.logical_and(lead_y, from_y > hops(i, n_x))) for i in range(1, n_x)]

    owned_at_x = {
        i: 1 + sum(hops(j, n_y) <= hops(i, n_x) for j in range(1, n_y)) for i in range(1, n_x)
    }
    owned_at_y = {
        j: 1 + sum(hops(j, n_y) > hops(i, n_x) for i in range(1, n_x)) for j in range(1, n_y)
    }

    @pl.when(is_hub)
    def _():
        rows(hub_recv, n_xy * n_z - 1, send_sem.at[0], recv_sem.at[0]).wait_recv()
        scale = (3.0 * TILE * n_xy * n_z) / sum_rows(hub_recv, n_xy * n_z)
        scale_ref[...] = scale
        row_recv[...] = scale
        @pl.when(jnp.logical_not(is_at(0, 0, LEAD)))
        def _():
            for i, j, casts in lines:

                @pl.when(casts)
                def _():
                    for z in range(n_z):
                        copy = pltpu.make_async_remote_copy(
                            src_ref=row_recv,
                            dst_ref=row_recv,
                            send_sem=cast_sem,
                            recv_sem=recv_sem.at[2],
                            device_id={
                                "gx": lax.rem(my_x + i, n_x),
                                "gy": lax.rem(my_y + j, n_y),
                                "gz": z,
                            },
                            device_id_type=MESH,
                        )
                        if i or j:
                            copy.start()
                        else:
                            first_hub = jnp.logical_and(in_corner, z == LEAD)

                            @pl.when(jnp.logical_not(jnp.logical_or(my_z == z, first_hub)))
                            def _():
                                copy.start()

            for owned in sorted({0} | set(owned_at_x.values()) | set(owned_at_y.values())):
                own = n_z - 1 if owned else n_z - 2
                is_so = is_at(0, 0, CAST) if owned == 0 else False
                for i, count in owned_at_x.items():
                    if count == owned:
                        is_so = jnp.logical_or(is_so, is_at(i, 0, LEAD))
                for j, count in owned_at_y.items():
                    if count == owned:
                        is_so = jnp.logical_or(is_so, is_at(0, j, LEAD))

                @pl.when(is_so)
                def _():
                    rows(hub_recv, max(owned - 1, 0) * n_z + own, cast_sem, recv_sem.at[2]).wait_send()

        rows(hub_recv, len(hubs) - 1, send_sem.at[0], recv_sem.at[0]).wait_send()

    @pl.when(jnp.logical_not(is_hub))
    def _():
        rows(hub_recv, 1, send_sem.at[2], recv_sem.at[2]).wait_recv()
        scale_ref[...] = row_recv[...]
        rows(hub_recv, len(hubs), send_sem.at[0], recv_sem.at[0]).wait_send()

    tiles.wait_send()


def solution(mesh):
    n_x, n_y, n_z = mesh.shape["gx"], mesh.shape["gy"], mesh.shape["gz"]
    n_xy = n_x * n_y

    def on_device(incidence, live_counts, lame_first, shear_modulus, stretch):
        n_tiles = incidence.shape[3]
        hbm = pl.BlockSpec(memory_space=pltpu.HBM)
        vmem = pl.BlockSpec(memory_space=pltpu.VMEM)
        block, scale = pl.pallas_call(
            functools.partial(kernel, n_x, n_y, n_z),
            out_shape=(
                jax.ShapeDtypeStruct((3, 3, TILE, TILE), F32),
                jax.ShapeDtypeStruct((1, TILE), F32),
            ),
            in_specs=[hbm] * 5,
            out_specs=(vmem, vmem),
            scratch_shapes=[
                pltpu.VMEM((1, n_tiles), jnp.int32),
                pltpu.VMEM((n_tiles * CAP * CORNERS, TILE), jnp.int32),
                pltpu.VMEM((CORNERS, TILE), jnp.int32),
                pltpu.VMEM((n_tiles, CAP), F32),
                pltpu.VMEM((n_tiles, CAP), F32),
                pltpu.VMEM((3, n_tiles, CAP), F32),
                pltpu.VMEM((n_tiles, TILE), F32),
                pltpu.VMEM((n_tiles * CAP, TILE), F32),
                pltpu.VMEM((TILE, TILE), BF16),
                pltpu.VMEM((TILE, TILE), F32),
                pltpu.VMEM((n_tiles, TILE), F32),
                pltpu.VMEM((n_z, 2, TILE), F32),
                pltpu.VMEM((n_z, 2, TILE), F32),
                pltpu.VMEM((1, TILE), F32),
                pltpu.VMEM((1, TILE), F32),
                pltpu.VMEM((n_xy * n_z, 1, TILE), F32),
                pltpu.SemaphoreType.DMA,
                pltpu.SemaphoreType.DMA((9,)),
                pltpu.SemaphoreType.DMA((3,)),
                pltpu.SemaphoreType.DMA((3,)),
                pltpu.SemaphoreType.DMA,
                pltpu.SemaphoreType.REGULAR,
                pltpu.SemaphoreType.REGULAR,
            ],
            compiler_params=pltpu.CompilerParams(
                collective_id=0, has_side_effects=True, vmem_limit_bytes=24 << 20
            ),
        )(
            *(
                pltpu.with_memory_space_constraint(value, pltpu.HBM)
                for value in (
                    live_counts.reshape(1, n_tiles),
                    incidence.reshape(n_tiles * CAP * CORNERS, TILE),
                    lame_first.reshape(n_tiles, CAP),
                    shear_modulus.reshape(n_tiles, CAP),
                    stretch.reshape(3, n_tiles, CAP),
                )
            )
        )
        block = block * scale.reshape(1, 1, 1, TILE)
        return block.transpose(0, 2, 1, 3).reshape(1, 1, 1, 3, TILE, 3, TILE)

    return jax.shard_map(
        on_device,
        mesh=mesh,
        in_specs=(
            P("gx", "gy", "gz", None, None, None, None),
            P("gx", "gy", "gz", None),
            P("gx", "gy", "gz", None, None),
            P("gx", "gy", "gz", None, None),
            P(None, "gx", "gy", "gz", None, None),
        ),
        out_specs=P("gx", "gy", "gz", None, None, None, None),
        check_vma=False,
    )
```

```python
import functools

import jax
import jax.numpy as jnp
from jax import lax
from jax.experimental import pallas as pl
from jax.experimental.pallas import tpu as pltpu
from jax.sharding import PartitionSpec as P

MESH = pl.DeviceIdType.MESH
F32, BF16 = jnp.float32, jnp.bfloat16
TILE, CAP, CORNERS = 128, 16, 8

LEAD = 1
CAST = 3
EARLY = 4

ALL_MODES = (1, 2, 4, 3, 5, 6, 7)


def split(value):
    high = value.astype(BF16)
    return high, (value - high.astype(F32)).astype(BF16)


def swap_groups(values):
    sub = lax.broadcasted_iota(jnp.int32, (8, 128), 0)
    group = lax.broadcasted_iota(jnp.int32, (8, 128), 1) // CAP
    for bit in (1, 2, 4):
        upper_sub = (sub & bit) != 0
        upper_group = (group & bit) != 0
        below = pltpu.roll(pltpu.roll(values, 8 - bit, 0), CAP * bit, 1)
        above = pltpu.roll(pltpu.roll(values, bit, 0), 128 - CAP * bit, 1)
        values = jnp.where(
            upper_sub == upper_group, values, jnp.where(upper_sub, above, below)
        )
    return values


def kernel(
    n_x, n_y, n_z,
    live_hbm, inc_hbm, lame_hbm, shear_hbm, stretch_hbm,
    block_ref, scale_ref,
    live, inc, tail, lame, shear, stretch, alive, weight, number, place, params, send, recv, row, row_recv, hub_recv,
    tail_sem, in_sem, send_sem, recv_sem, cast_sem, here, ready,
):
    n_tiles = send.shape[0]
    my_x, my_y, my_z = lax.axis_index("gx"), lax.axis_index("gy"), lax.axis_index("gz")
    n_xy = n_x * n_y

    last = 4
    main = inc.shape[0] - 2 * CORNERS
    ends = [main // CORNERS * k // last * CORNERS for k in range(last + 1)] + [main + CORNERS]
    tail_load = pltpu.make_async_copy(
        inc_hbm.at[pl.ds(main + CORNERS, CORNERS)], tail, tail_sem
    )
    small = [
        pltpu.make_async_copy(source, target, in_sem.at[k])
        for k, (source, target) in enumerate(
            ((live_hbm, live), (lame_hbm, lame), (shear_hbm, shear), (stretch_hbm, stretch))
        )
    ]
    loads = [
        pltpu.make_async_copy(
            inc_hbm.at[pl.ds(first, end - first)],
            inc.at[pl.ds(first, end - first)],
            in_sem.at[len(small) + k],
        )
        for k, (first, end) in enumerate(zip(ends, ends[1:]))
    ]
    starts = {end // CORNERS: copy for end, copy in zip(ends, loads)}
    for copy in [tail_load] + small + loads:
        copy.start()

    def hops(step, size):
        return min(step, size - step)

    hubs = [(0, 0, LEAD), (0, 0, CAST)]
    hubs += [(i, 0, LEAD) for i in range(1, n_x)] + [(0, j, LEAD) for j in range(1, n_y)]

    def is_at(x, y, z):
        return jnp.logical_and(jnp.logical_and(my_x == x, my_y == y), my_z == z)

    in_corner = jnp.logical_and(my_x == 0, my_y == 0)
    on_edge = jnp.logical_or(my_x == 0, my_y == 0)
    is_lead = my_z == LEAD
    is_early = my_z < EARLY
    is_hub = jnp.logical_or(jnp.logical_and(on_edge, is_lead), is_at(0, 0, CAST))
    plane_steps = sorted(
        ((i, j) for i in range(n_x) for j in range(n_y)),
        key=lambda step: -hops(step[0], n_x) - hops(step[1], n_y),
    )
    line_steps = sorted(range(1, n_z), key=lambda step: -hops(step, n_z))

    barrier = pltpu.get_barrier_semaphore()

    def greet(x, y, z):
        pl.semaphore_signal(
            barrier, inc=1, device_id={"gx": x, "gy": y, "gz": z}, device_id_type=MESH
        )

    @pl.when(is_early)
    def _():
        for step in line_steps:
            greet(my_x, my_y, lax.rem(my_z + step, n_z))

    @pl.when(is_hub)
    def _():
        half = n_z // 2

        @pl.loop(0, half)
        def _(near):
            ahead = lax.rem(my_z + half + near, n_z)
            behind = lax.rem(my_z + jnp.where(near == 0, 0, half - near), n_z)
            for i, j in plane_steps:
                x, y = lax.rem(my_x + i, n_x), lax.rem(my_y + j, n_y)
                greet(x, y, ahead)
                if i or j:
                    greet(x, y, behind)
                else:

                    @pl.when(near > 0)
                    def _():
                        greet(x, y, behind)

    for copy in small:
        copy.wait()
    params[...] = jnp.zeros_like(params)
    first, second = lame[...], shear[...]
    lengths = [stretch[k] for k in range(3)]
    for k, value in enumerate([first, second] + lengths):
        params[:, k * CAP : (k + 1) * CAP] = value
    send[:, 1, :] = params[...]
    inverse = [1.0 / value for value in lengths]
    trace = (
        (lengths[0] * lengths[1] * lengths[2] / 9.0)
        * (first + 4.0 * second)
        * (inverse[0] * inverse[0] + inverse[1] * inverse[1] + inverse[2] * inverse[2])
    )
    diagonal = lax.broadcasted_iota(jnp.int32, (CAP, CAP), 0) == lax.broadcasted_iota(
        jnp.int32, (CAP, CAP), 1
    )
    counts = jnp.broadcast_to(live[...].astype(F32), (n_tiles, n_tiles))
    tile_down = lax.broadcasted_iota(jnp.int32, (n_tiles, n_tiles), 0)
    tile_across = lax.broadcasted_iota(jnp.int32, (n_tiles, n_tiles), 1)
    counts = jnp.sum(jnp.where(tile_down == tile_across, counts, 0.0), axis=1, keepdims=True)
    slot = lax.broadcasted_iota(jnp.int32, (n_tiles, TILE), 1) % CAP
    alive[...] = jnp.where(slot.astype(F32) < counts, 1.0, 0.0)
    trace = trace * alive[:, :CAP]
    for t in range(n_tiles):
        column = jnp.sum(jnp.where(diagonal, trace[t : t + 1, :], 0.0), axis=1, keepdims=True)
        weight[t * CAP : (t + 1) * CAP, :] = jnp.broadcast_to(column, (CAP, TILE))

    down = lax.broadcasted_iota(jnp.int32, (TILE, TILE), 0)
    lane = lax.broadcasted_iota(jnp.int32, (TILE, TILE), 1)
    number[...] = (down + 1).astype(F32).astype(BF16)
    place[...] = jnp.where(lane == (down % CORNERS) * CAP + down // CORNERS, 1.0, 0.0)

    sums = [jnp.zeros((CORNERS, TILE), F32) for _ in range(8)]
    for e in range(n_tiles * CAP):
        if e in starts:
            starts[e].wait()
        if e == n_tiles * CAP - 1:
            tail_load.wait()
            inc[main + CORNERS : main + 2 * CORNERS, :] = tail[...]
        onehot = inc[e * CORNERS : (e + 1) * CORNERS, :].astype(F32)
        sums[e % 8] = sums[e % 8] + onehot * weight[e : e + 1, :]
    while len(sums) > 1:
        sums = [sums[k] + sums[k + 1] for k in range(0, len(sums), 2)]
    partial = jnp.sum(sums[0], axis=0, keepdims=True)
    row[...] = jnp.broadcast_to(jnp.sum(partial, axis=1, keepdims=True), (1, TILE))

    pl.semaphore_wait(
        barrier,
        len(hubs) + EARLY - jnp.where(is_hub, 1, 0) - jnp.where(is_early, 1, 0),
    )

    for x, y, z in hubs:
        source = lax.rem(my_x - x + n_x, n_x) * n_y + lax.rem(my_y - y + n_y, n_y)

        @pl.when(jnp.logical_not(is_at(x, y, z)))
        def _():
            pltpu.make_async_remote_copy(
                src_ref=row,
                dst_ref=hub_recv.at[my_z * n_xy + source],
                send_sem=send_sem.at[0],
                recv_sem=recv_sem.at[jnp.where(my_z < n_z // 2, 0, 3)],
                device_id={"gx": x, "gy": y, "gz": z},
                device_id_type=MESH,
            ).start()

    hub_recv[my_z * n_xy] = row[...]

    @pl.when(jnp.logical_not(is_lead))
    def _():
        pl.semaphore_signal(here, inc=1, device_id={"gz": LEAD}, device_id_type=MESH)

    for t in range(n_tiles):
        onehot = inc[t * TILE : (t + 1) * TILE, :].astype(F32).astype(BF16)
        spread = jnp.dot(onehot, number[...], preferred_element_type=F32)
        ids = jnp.sum(spread * place[...], axis=0, keepdims=True)
        send[t, 0:1, :] = ids * alive[t : t + 1, :]

    def send_tile(z):
        @pl.when(my_z != z)
        def _():
            pltpu.make_async_remote_copy(
                src_ref=send.at[z],
                dst_ref=recv.at[lax.rem(my_z - z + n_z, n_z)],
                send_sem=send_sem.at[1],
                recv_sem=recv_sem.at[1],
                device_id={"gz": z},
                device_id_type=MESH,
            ).start()

    for z in range(EARLY):
        send_tile(z)
    recv[0] = send[my_z]

    @pl.when(is_lead)
    def _():
        pl.semaphore_wait(here, n_z - 1)
        for step in line_steps:
            pl.semaphore_signal(
                ready, inc=1, device_id={"gz": (LEAD + step) % n_z}, device_id_type=MESH
            )

    @pl.when(jnp.logical_not(is_lead))
    def _():
        pl.semaphore_wait(ready, 1)

    for z in range(EARLY, n_z):
        send_tile(z)

    def rows(target, count, send_with, recv_with):
        return pltpu.make_async_remote_copy(
            src_ref=target.at[pl.ds(1, count)],
            dst_ref=target.at[pl.ds(1, count)],
            send_sem=send_with,
            recv_sem=recv_with,
            device_id={"gz": lax.rem(my_z + 1, n_z)},
            device_id_type=MESH,
        )

    tiles = rows(recv, n_z - 1, send_sem.at[1], recv_sem.at[1])
    tiles.wait_recv()

    halves = range(n_z // 8)
    ids = jnp.concatenate([swap_groups(recv[8 * h : 8 * h + 8, 0, :]) for h in halves], axis=1)
    material = jnp.concatenate(
        [swap_groups(recv[8 * h : 8 * h + 8, 1, :]) for h in halves], axis=1
    )
    wide = ids.shape[1]
    first, second = material[0:1], material[1:2]
    h = [material[2 + k : 3 + k] for k in range(3)]

    node = (lax.broadcasted_iota(jnp.int32, (TILE, wide), 0) + 1).astype(F32)
    corner = [
        jnp.where(node == ids[p : p + 1], 1.0, 0.0).astype(BF16) for p in range(CORNERS)
    ]
    mode = corner
    for bit in (1, 2, 4):
        mode = [
            mode[k] - mode[k ^ bit] if k & bit else mode[k] + mode[k ^ bit]
            for k in range(CORNERS)
        ]

    def scaled(wave, coefficient):
        wide_row = jnp.broadcast_to(coefficient, (16, wide)).astype(BF16)
        return (wave.reshape(TILE // 16, 16, wide) * wide_row[None]).reshape(TILE, wide)

    def product(left, right):
        return lax.dot_general(
            left, right, (((1,), (1,)), ((), ())), preferred_element_type=F32
        )

    def assemble(pairs):
        high, low, other = [], [], []
        for left, right, coefficient in pairs:
            top = coefficient.astype(BF16).astype(F32)
            high.append(scaled(mode[left], top))
            low.append(scaled(mode[left], coefficient - top))
            other.append(mode[right])
        right = jnp.concatenate(other, axis=1)
        left = jnp.concatenate(
            [jnp.concatenate(high, axis=1), jnp.concatenate(low, axis=1)], axis=0
        )
        result = product(left, right)
        return result[:TILE] + result[TILE:]

    area = [h[1] * h[2] / (16.0 * h[0]), h[0] * h[2] / (16.0 * h[1]), h[0] * h[1] / (16.0 * h[2])]
    strong = first + 2.0 * second
    for i in range(3):
        alpha = [(strong if k == i else second) * area[k] for k in range(3)]
        coefficients = {
            1: alpha[0],
            2: alpha[1],
            4: alpha[2],
            3: (alpha[0] + alpha[1]) / 3.0,
            5: (alpha[0] + alpha[2]) / 3.0,
            6: (alpha[1] + alpha[2]) / 3.0,
            7: (alpha[0] + alpha[1] + alpha[2]) / 9.0,
        }
        block_ref[i, i] = assemble([(m, m, coefficients[m]) for m in ALL_MODES])
    for i, j, k in ((0, 1, 2), (0, 2, 1), (1, 2, 0)):
        a, b, c = 1 << i, 1 << j, 1 << k
        la, mu = h[k] * first / 16.0, h[k] * second / 16.0
        result = assemble(
            [
                (a, b, la),
                (a | c, b | c, la / 3.0),
                (b, a, mu),
                (b | c, a | c, mu / 3.0),
            ]
        )
        block_ref[i, j] = result
        block_ref[j, i] = result.T

    def sum_rows(values, first, end):
        sums = [values[first + k] for k in range(8)]
        for k in range(8, end - first):
            sums[k % 8] = sums[k % 8] + values[first + k]
        while len(sums) > 1:
            sums = [sums[k] + sums[k + 1] for k in range(0, len(sums), 2)]
        return sums[0]

    from_x, from_y = jnp.minimum(my_x, n_x - my_x), jnp.minimum(my_y, n_y - my_y)
    lead_x = jnp.logical_and(is_lead, jnp.logical_and(my_y == 0, my_x != 0))
    lead_y = jnp.logical_and(is_lead, jnp.logical_and(my_x == 0, my_y != 0))
    lines = [(0, 0, jnp.logical_and(is_hub, jnp.logical_not(is_at(0, 0, LEAD))))]
    lines += [
        (0, j, jnp.logical_and(lead_x, hops(j, n_y) <= from_x)) for j in range(1, n_y)
    ]
    lines += [(i, 0, jnp.logical_and(lead_y, from_y > hops(i, n_x))) for i in range(1, n_x)]

    owned_at_x = {
        i: 1 + sum(hops(j, n_y) <= hops(i, n_x) for j in range(1, n_y)) for i in range(1, n_x)
    }
    owned_at_y = {
        j: 1 + sum(hops(j, n_y) > hops(i, n_x) for i in range(1, n_x)) for j in range(1, n_y)
    }

    @pl.when(is_hub)
    def _():
        half = n_xy * n_z // 2
        rows(hub_recv, half - 1, send_sem.at[0], recv_sem.at[0]).wait_recv()
        first_half = sum_rows(hub_recv, 0, half)
        rows(hub_recv, half, send_sem.at[0], recv_sem.at[3]).wait_recv()
        scale = (3.0 * TILE * n_xy * n_z) / (first_half + sum_rows(hub_recv, half, 2 * half))
        scale_ref[...] = scale
        row_recv[...] = scale
        @pl.when(jnp.logical_not(is_at(0, 0, LEAD)))
        def _():
            for i, j, casts in lines:

                @pl.when(casts)
                def _():
                    for z in range(n_z):
                        copy = pltpu.make_async_remote_copy(
                            src_ref=row_recv,
                            dst_ref=row_recv,
                            send_sem=cast_sem,
                            recv_sem=recv_sem.at[2],
                            device_id={
                                "gx": lax.rem(my_x + i, n_x),
                                "gy": lax.rem(my_y + j, n_y),
                                "gz": z,
                            },
                            device_id_type=MESH,
                        )
                        if i or j:
                            copy.start()
                        else:
                            first_hub = jnp.logical_and(in_corner, z == LEAD)

                            @pl.when(jnp.logical_not(jnp.logical_or(my_z == z, first_hub)))
                            def _():
                                copy.start()

            for owned in sorted({0} | set(owned_at_x.values()) | set(owned_at_y.values())):
                own = n_z - 1 if owned else n_z - 2
                is_so = is_at(0, 0, CAST) if owned == 0 else False
                for i, count in owned_at_x.items():
                    if count == owned:
                        is_so = jnp.logical_or(is_so, is_at(i, 0, LEAD))
                for j, count in owned_at_y.items():
                    if count == owned:
                        is_so = jnp.logical_or(is_so, is_at(0, j, LEAD))

                @pl.when(is_so)
                def _():
                    rows(hub_recv, max(owned - 1, 0) * n_z + own, cast_sem, recv_sem.at[2]).wait_send()

        rows(hub_recv, len(hubs) - 1, send_sem.at[0], recv_sem.at[0]).wait_send()

    @pl.when(jnp.logical_not(is_hub))
    def _():
        rows(hub_recv, 1, send_sem.at[2], recv_sem.at[2]).wait_recv()
        scale_ref[...] = row_recv[...]
        rows(hub_recv, len(hubs), send_sem.at[0], recv_sem.at[0]).wait_send()

    tiles.wait_send()


def scale_kernel(block_ref, scale_ref, out_hbm, scaled, sems):
    scale = scale_ref[...]
    copies = []
    for k in range(3):
        part = pl.ds(k * 3 * TILE, 3 * TILE)
        scaled[part, :] = block_ref[part, :] * scale
        copies.append(pltpu.make_async_copy(scaled.at[part], out_hbm.at[part], sems.at[k]))
        copies[k].start()
    for copy in copies:
        copy.wait()


def solution(mesh):
    n_x, n_y, n_z = mesh.shape["gx"], mesh.shape["gy"], mesh.shape["gz"]
    n_xy = n_x * n_y

    def on_device(incidence, live_counts, lame_first, shear_modulus, stretch):
        n_tiles = incidence.shape[3]
        hbm = pl.BlockSpec(memory_space=pltpu.HBM)
        vmem = pl.BlockSpec(memory_space=pltpu.VMEM)
        block, scale = pl.pallas_call(
            functools.partial(kernel, n_x, n_y, n_z),
            out_shape=(
                jax.ShapeDtypeStruct((3, 3, TILE, TILE), F32),
                jax.ShapeDtypeStruct((1, TILE), F32),
            ),
            in_specs=[hbm] * 5,
            out_specs=(vmem, vmem),
            scratch_shapes=[
                pltpu.VMEM((1, n_tiles), jnp.int32),
                pltpu.VMEM((n_tiles * CAP * CORNERS, TILE), jnp.int32),
                pltpu.VMEM((CORNERS, TILE), jnp.int32),
                pltpu.VMEM((n_tiles, CAP), F32),
                pltpu.VMEM((n_tiles, CAP), F32),
                pltpu.VMEM((3, n_tiles, CAP), F32),
                pltpu.VMEM((n_tiles, TILE), F32),
                pltpu.VMEM((n_tiles * CAP, TILE), F32),
                pltpu.VMEM((TILE, TILE), BF16),
                pltpu.VMEM((TILE, TILE), F32),
                pltpu.VMEM((n_tiles, TILE), F32),
                pltpu.VMEM((n_z, 2, TILE), F32),
                pltpu.VMEM((n_z, 2, TILE), F32),
                pltpu.VMEM((1, TILE), F32),
                pltpu.VMEM((1, TILE), F32),
                pltpu.VMEM((n_xy * n_z, 1, TILE), F32),
                pltpu.SemaphoreType.DMA,
                pltpu.SemaphoreType.DMA((9,)),
                pltpu.SemaphoreType.DMA((3,)),
                pltpu.SemaphoreType.DMA((4,)),
                pltpu.SemaphoreType.DMA,
                pltpu.SemaphoreType.REGULAR,
                pltpu.SemaphoreType.REGULAR,
            ],
            compiler_params=pltpu.CompilerParams(
                collective_id=0, has_side_effects=True, vmem_limit_bytes=24 << 20
            ),
        )(
            *(
                pltpu.with_memory_space_constraint(value, pltpu.HBM)
                for value in (
                    live_counts.reshape(1, n_tiles),
                    incidence.reshape(n_tiles * CAP * CORNERS, TILE),
                    lame_first.reshape(n_tiles, CAP),
                    shear_modulus.reshape(n_tiles, CAP),
                    stretch.reshape(3, n_tiles, CAP),
                )
            )
        )
        block = pl.pallas_call(
            scale_kernel,
            out_shape=jax.ShapeDtypeStruct((9 * TILE, TILE), F32),
            in_specs=[vmem, vmem],
            out_specs=hbm,
            scratch_shapes=[pltpu.VMEM((9 * TILE, TILE), F32), pltpu.SemaphoreType.DMA((3,))],
            compiler_params=pltpu.CompilerParams(vmem_limit_bytes=24 << 20),
        )(block.reshape(9 * TILE, TILE), scale)
        block = block.reshape(3, 3, TILE, TILE)
        return block.transpose(0, 2, 1, 3).reshape(1, 1, 1, 3, TILE, 3, TILE)

    return jax.shard_map(
        on_device,
        mesh=mesh,
        in_specs=(
            P("gx", "gy", "gz", None, None, None, None),
            P("gx", "gy", "gz", None),
            P("gx", "gy", "gz", None, None),
            P("gx", "gy", "gz", None, None),
            P(None, "gx", "gy", "gz", None, None),
        ),
        out_specs=P("gx", "gy", "gz", None, None, None, None),
        check_vma=False,
    )
```

```python
import functools

import jax
import jax.numpy as jnp
from jax import lax
from jax.experimental import pallas as pl
from jax.experimental.pallas import tpu as pltpu
from jax.sharding import PartitionSpec as P

MESH = pl.DeviceIdType.MESH
F32, BF16 = jnp.float32, jnp.bfloat16
TILE, CAP, CORNERS = 128, 16, 8

LEAD = 1
CAST = 3
EARLY = 4

ALL_MODES = (1, 2, 4, 3, 5, 6, 7)


def split(value):
    high = value.astype(BF16)
    return high, (value - high.astype(F32)).astype(BF16)


def swap_groups(values):
    sub = lax.broadcasted_iota(jnp.int32, (8, 128), 0)
    group = lax.broadcasted_iota(jnp.int32, (8, 128), 1) // CAP
    for bit in (1, 2, 4):
        upper_sub = (sub & bit) != 0
        upper_group = (group & bit) != 0
        below = pltpu.roll(pltpu.roll(values, 8 - bit, 0), CAP * bit, 1)
        above = pltpu.roll(pltpu.roll(values, bit, 0), 128 - CAP * bit, 1)
        values = jnp.where(
            upper_sub == upper_group, values, jnp.where(upper_sub, above, below)
        )
    return values


def kernel(
    n_x, n_y, n_z,
    live_hbm, inc_hbm, lame_hbm, shear_hbm, stretch_hbm,
    block_ref, scale_ref,
    live, inc, tail, lame, shear, stretch, alive, weight, number, place, params, send, recv, row, row_recv, hub_recv,
    tail_sem, in_sem, send_sem, recv_sem, cast_sem, told,
):
    n_tiles = send.shape[0]
    my_x, my_y, my_z = lax.axis_index("gx"), lax.axis_index("gy"), lax.axis_index("gz")
    n_xy = n_x * n_y

    last = 4
    main = inc.shape[0] - 2 * CORNERS
    ends = [main // CORNERS * k // last * CORNERS for k in range(last + 1)] + [main + CORNERS]
    tail_load = pltpu.make_async_copy(
        inc_hbm.at[pl.ds(main + CORNERS, CORNERS)], tail, tail_sem
    )
    small = [
        pltpu.make_async_copy(source, target, in_sem.at[k])
        for k, (source, target) in enumerate(
            ((live_hbm, live), (lame_hbm, lame), (shear_hbm, shear), (stretch_hbm, stretch))
        )
    ]
    loads = [
        pltpu.make_async_copy(
            inc_hbm.at[pl.ds(first, end - first)],
            inc.at[pl.ds(first, end - first)],
            in_sem.at[len(small) + k],
        )
        for k, (first, end) in enumerate(zip(ends, ends[1:]))
    ]
    starts = {end // CORNERS: copy for end, copy in zip(ends, loads)}
    for copy in [tail_load] + small + loads:
        copy.start()

    def hops(step, size):
        return min(step, size - step)

    hubs = [(0, 0, LEAD), (0, 0, CAST)]
    hubs += [(i, 0, LEAD) for i in range(1, n_x)] + [(0, j, LEAD) for j in range(1, n_y)]

    def is_at(x, y, z):
        return jnp.logical_and(jnp.logical_and(my_x == x, my_y == y), my_z == z)

    in_corner = jnp.logical_and(my_x == 0, my_y == 0)
    on_edge = jnp.logical_or(my_x == 0, my_y == 0)
    is_lead = my_z == LEAD
    is_early = my_z < EARLY
    is_hub = jnp.logical_or(jnp.logical_and(on_edge, is_lead), is_at(0, 0, CAST))
    plane_steps = sorted(
        ((i, j) for i in range(n_x) for j in range(n_y)),
        key=lambda step: -hops(step[0], n_x) - hops(step[1], n_y),
    )
    line_steps = sorted(range(1, n_z), key=lambda step: -hops(step, n_z))

    barrier = pltpu.get_barrier_semaphore()

    def greet(x, y, z):
        pl.semaphore_signal(
            barrier, inc=1, device_id={"gx": x, "gy": y, "gz": z}, device_id_type=MESH
        )

    @pl.when(is_early)
    def _():
        for step in line_steps:
            greet(my_x, my_y, lax.rem(my_z + step, n_z))

    @pl.when(is_hub)
    def _():
        half = n_z // 2

        @pl.loop(0, half)
        def _(near):
            ahead = lax.rem(my_z + half + near, n_z)
            behind = lax.rem(my_z + jnp.where(near == 0, 0, half - near), n_z)
            for i, j in plane_steps:
                x, y = lax.rem(my_x + i, n_x), lax.rem(my_y + j, n_y)
                greet(x, y, ahead)
                if i or j:
                    greet(x, y, behind)
                else:

                    @pl.when(near > 0)
                    def _():
                        greet(x, y, behind)

    for copy in small:
        copy.wait()
    params[...] = jnp.zeros_like(params)
    first, second = lame[...], shear[...]
    lengths = [stretch[k] for k in range(3)]
    for k, value in enumerate([first, second] + lengths):
        params[:, k * CAP : (k + 1) * CAP] = value
    send[:, 1, :] = params[...]
    inverse = [1.0 / value for value in lengths]
    trace = (
        (lengths[0] * lengths[1] * lengths[2] / 9.0)
        * (first + 4.0 * second)
        * (inverse[0] * inverse[0] + inverse[1] * inverse[1] + inverse[2] * inverse[2])
    )
    diagonal = lax.broadcasted_iota(jnp.int32, (CAP, CAP), 0) == lax.broadcasted_iota(
        jnp.int32, (CAP, CAP), 1
    )
    counts = jnp.broadcast_to(live[...].astype(F32), (n_tiles, n_tiles))
    tile_down = lax.broadcasted_iota(jnp.int32, (n_tiles, n_tiles), 0)
    tile_across = lax.broadcasted_iota(jnp.int32, (n_tiles, n_tiles), 1)
    counts = jnp.sum(jnp.where(tile_down == tile_across, counts, 0.0), axis=1, keepdims=True)
    slot = lax.broadcasted_iota(jnp.int32, (n_tiles, TILE), 1) % CAP
    alive[...] = jnp.where(slot.astype(F32) < counts, 1.0, 0.0)
    trace = trace * alive[:, :CAP]
    for t in range(n_tiles):
        column = jnp.sum(jnp.where(diagonal, trace[t : t + 1, :], 0.0), axis=1, keepdims=True)
        weight[t * CAP : (t + 1) * CAP, :] = jnp.broadcast_to(column, (CAP, TILE))

    down = lax.broadcasted_iota(jnp.int32, (TILE, TILE), 0)
    lane = lax.broadcasted_iota(jnp.int32, (TILE, TILE), 1)
    number[...] = (down + 1).astype(F32).astype(BF16)
    place[...] = jnp.where(lane == (down % CORNERS) * CAP + down // CORNERS, 1.0, 0.0)

    sums = [jnp.zeros((CORNERS, TILE), F32) for _ in range(8)]
    for e in range(n_tiles * CAP):
        if e in starts:
            starts[e].wait()
        if e == n_tiles * CAP - 1:
            tail_load.wait()
            inc[main + CORNERS : main + 2 * CORNERS, :] = tail[...]
        onehot = inc[e * CORNERS : (e + 1) * CORNERS, :].astype(F32)
        sums[e % 8] = sums[e % 8] + onehot * weight[e : e + 1, :]
    while len(sums) > 1:
        sums = [sums[k] + sums[k + 1] for k in range(0, len(sums), 2)]
    partial = jnp.sum(sums[0], axis=0, keepdims=True)
    row[...] = jnp.broadcast_to(jnp.sum(partial, axis=1, keepdims=True), (1, TILE))

    pl.semaphore_wait(
        barrier,
        len(hubs) + EARLY - jnp.where(is_hub, 1, 0) - jnp.where(is_early, 1, 0),
    )

    row_group = jnp.where(my_z < n_z // 2, 0, jnp.where(my_z < n_z // 2 + 2, 4, 3))
    for x, y, z in hubs:
        source = lax.rem(my_x - x + n_x, n_x) * n_y + lax.rem(my_y - y + n_y, n_y)

        @pl.when(jnp.logical_not(is_at(x, y, z)))
        def _():
            pltpu.make_async_remote_copy(
                src_ref=row,
                dst_ref=hub_recv.at[my_z * n_xy + source],
                send_sem=send_sem.at[0],
                recv_sem=recv_sem.at[row_group],
                device_id={"gx": x, "gy": y, "gz": z},
                device_id_type=MESH,
            ).start()

    hub_recv[my_z * n_xy] = row[...]

    @pl.when(jnp.logical_not(is_lead))
    def _():
        pl.semaphore_signal(told, inc=1, device_id={"gz": LEAD}, device_id_type=MESH)

    for t in range(n_tiles):
        onehot = inc[t * TILE : (t + 1) * TILE, :].astype(F32).astype(BF16)
        spread = jnp.dot(onehot, number[...], preferred_element_type=F32)
        ids = jnp.sum(spread * place[...], axis=0, keepdims=True)
        send[t, 0:1, :] = ids * alive[t : t + 1, :]

    def send_tile(z):
        @pl.when(my_z != z)
        def _():
            pltpu.make_async_remote_copy(
                src_ref=send.at[z],
                dst_ref=recv.at[lax.rem(my_z - z + n_z, n_z)],
                send_sem=send_sem.at[1],
                recv_sem=recv_sem.at[1],
                device_id={"gz": z},
                device_id_type=MESH,
            ).start()

    for z in range(EARLY):
        send_tile(z)
    recv[0] = send[my_z]

    @pl.when(is_lead)
    def _():
        pl.semaphore_wait(told, n_z - 1)
        for step in line_steps:
            pl.semaphore_signal(
                told, inc=1, device_id={"gz": (LEAD + step) % n_z}, device_id_type=MESH
            )

    @pl.when(jnp.logical_not(is_lead))
    def _():
        pl.semaphore_wait(told, 1)

    for z in range(EARLY, n_z):
        send_tile(z)

    def rows(target, count, send_with, recv_with):
        return pltpu.make_async_remote_copy(
            src_ref=target.at[pl.ds(1, count)],
            dst_ref=target.at[pl.ds(1, count)],
            send_sem=send_with,
            recv_sem=recv_with,
            device_id={"gz": lax.rem(my_z + 1, n_z)},
            device_id_type=MESH,
        )

    tiles = rows(recv, n_z - 1, send_sem.at[1], recv_sem.at[1])
    tiles.wait_recv()

    halves = range(n_z // 8)
    ids = jnp.concatenate([swap_groups(recv[8 * h : 8 * h + 8, 0, :]) for h in halves], axis=1)
    material = jnp.concatenate(
        [swap_groups(recv[8 * h : 8 * h + 8, 1, :]) for h in halves], axis=1
    )
    wide = ids.shape[1]
    first, second = material[0:1], material[1:2]
    h = [material[2 + k : 3 + k] for k in range(3)]

    node = (lax.broadcasted_iota(jnp.int32, (TILE, wide), 0) + 1).astype(F32)
    corner = [
        jnp.where(node == ids[p : p + 1], 1.0, 0.0).astype(BF16) for p in range(CORNERS)
    ]
    mode = corner
    for bit in (1, 2, 4):
        mode = [
            mode[k] - mode[k ^ bit] if k & bit else mode[k] + mode[k ^ bit]
            for k in range(CORNERS)
        ]

    def scaled(wave, coefficient):
        wide_row = jnp.broadcast_to(coefficient, (16, wide)).astype(BF16)
        return (wave.reshape(TILE // 16, 16, wide) * wide_row[None]).reshape(TILE, wide)

    def product(left, right):
        return lax.dot_general(
            left, right, (((1,), (1,)), ((), ())), preferred_element_type=F32
        )

    def assemble(pairs):
        high, low, other = [], [], []
        for left, right, coefficient in pairs:
            top = coefficient.astype(BF16).astype(F32)
            high.append(scaled(mode[left], top))
            low.append(scaled(mode[left], coefficient - top))
            other.append(mode[right])
        right = jnp.concatenate(other, axis=1)
        left = jnp.concatenate(
            [jnp.concatenate(high, axis=1), jnp.concatenate(low, axis=1)], axis=0
        )
        result = product(left, right)
        return result[:TILE] + result[TILE:]

    area = [h[1] * h[2] / (16.0 * h[0]), h[0] * h[2] / (16.0 * h[1]), h[0] * h[1] / (16.0 * h[2])]
    strong = first + 2.0 * second
    for i in range(3):
        alpha = [(strong if k == i else second) * area[k] for k in range(3)]
        coefficients = {
            1: alpha[0],
            2: alpha[1],
            4: alpha[2],
            3: (alpha[0] + alpha[1]) / 3.0,
            5: (alpha[0] + alpha[2]) / 3.0,
            6: (alpha[1] + alpha[2]) / 3.0,
            7: (alpha[0] + alpha[1] + alpha[2]) / 9.0,
        }
        block_ref[i, i] = assemble([(m, m, coefficients[m]) for m in ALL_MODES])
    for i, j, k in ((0, 1, 2), (0, 2, 1), (1, 2, 0)):
        a, b, c = 1 << i, 1 << j, 1 << k
        la, mu = h[k] * first / 16.0, h[k] * second / 16.0
        result = assemble(
            [
                (a, b, la),
                (a | c, b | c, la / 3.0),
                (b, a, mu),
                (b | c, a | c, mu / 3.0),
            ]
        )
        block_ref[i, j] = result
        block_ref[j, i] = result.T

    def sum_rows(values, first, end):
        sums = [values[first + k] for k in range(8)]
        for k in range(8, end - first):
            sums[k % 8] = sums[k % 8] + values[first + k]
        while len(sums) > 1:
            sums = [sums[k] + sums[k + 1] for k in range(0, len(sums), 2)]
        return sums[0]

    from_x, from_y = jnp.minimum(my_x, n_x - my_x), jnp.minimum(my_y, n_y - my_y)
    lead_x = jnp.logical_and(is_lead, jnp.logical_and(my_y == 0, my_x != 0))
    lead_y = jnp.logical_and(is_lead, jnp.logical_and(my_x == 0, my_y != 0))
    lines = [(0, 0, jnp.logical_and(is_hub, jnp.logical_not(is_at(0, 0, LEAD))))]
    lines += [
        (0, j, jnp.logical_and(lead_x, hops(j, n_y) <= from_x)) for j in range(1, n_y)
    ]
    lines += [(i, 0, jnp.logical_and(lead_y, from_y > hops(i, n_x))) for i in range(1, n_x)]

    owned_at_x = {
        i: 1 + sum(hops(j, n_y) <= hops(i, n_x) for j in range(1, n_y)) for i in range(1, n_x)
    }
    owned_at_y = {
        j: 1 + sum(hops(j, n_y) > hops(i, n_x) for i in range(1, n_x)) for j in range(1, n_y)
    }

    @pl.when(is_hub)
    def _():
        half = n_xy * n_z // 2
        rows(hub_recv, half - 1, send_sem.at[0], recv_sem.at[0]).wait_recv()
        first_half = sum_rows(hub_recv, 0, half)
        late = half + 2 * n_xy
        rows(hub_recv, 2 * half - late, send_sem.at[0], recv_sem.at[3]).wait_recv()
        before = first_half + sum_rows(hub_recv, late, 2 * half)
        rows(hub_recv, late - half, send_sem.at[0], recv_sem.at[4]).wait_recv()
        scale = (3.0 * TILE * n_xy * n_z) / (before + sum_rows(hub_recv, half, late))
        scale_ref[...] = scale
        row_recv[...] = scale
        @pl.when(jnp.logical_not(is_at(0, 0, LEAD)))
        def _():
            for i, j, casts in lines:

                @pl.when(casts)
                def _():
                    for z in range(n_z):
                        copy = pltpu.make_async_remote_copy(
                            src_ref=row_recv,
                            dst_ref=row_recv,
                            send_sem=cast_sem,
                            recv_sem=recv_sem.at[2],
                            device_id={
                                "gx": lax.rem(my_x + i, n_x),
                                "gy": lax.rem(my_y + j, n_y),
                                "gz": z,
                            },
                            device_id_type=MESH,
                        )
                        if i or j:
                            copy.start()
                        else:
                            first_hub = jnp.logical_and(in_corner, z == LEAD)

                            @pl.when(jnp.logical_not(jnp.logical_or(my_z == z, first_hub)))
                            def _():
                                copy.start()

            for owned in sorted({0} | set(owned_at_x.values()) | set(owned_at_y.values())):
                own = n_z - 1 if owned else n_z - 2
                is_so = is_at(0, 0, CAST) if owned == 0 else False
                for i, count in owned_at_x.items():
                    if count == owned:
                        is_so = jnp.logical_or(is_so, is_at(i, 0, LEAD))
                for j, count in owned_at_y.items():
                    if count == owned:
                        is_so = jnp.logical_or(is_so, is_at(0, j, LEAD))

                @pl.when(is_so)
                def _():
                    rows(hub_recv, max(owned - 1, 0) * n_z + own, cast_sem, recv_sem.at[2]).wait_send()

        rows(hub_recv, len(hubs) - 1, send_sem.at[0], recv_sem.at[0]).wait_send()

    @pl.when(jnp.logical_not(is_hub))
    def _():
        rows(hub_recv, 1, send_sem.at[2], recv_sem.at[2]).wait_recv()
        scale_ref[...] = row_recv[...]
        rows(hub_recv, len(hubs), send_sem.at[0], recv_sem.at[0]).wait_send()

    tiles.wait_send()


def scale_kernel(block_ref, scale_ref, out_hbm, scaled, sem):
    scale = scale_ref[...]
    for k in range(3):
        part = pl.ds(k * 3 * TILE, 3 * TILE)
        scaled[part, :] = block_ref[part, :] * scale
        pltpu.make_async_copy(scaled.at[part], out_hbm.at[part], sem).start()
    pltpu.make_async_copy(scaled, out_hbm, sem).wait()


def solution(mesh):
    n_x, n_y, n_z = mesh.shape["gx"], mesh.shape["gy"], mesh.shape["gz"]
    n_xy = n_x * n_y

    def on_device(incidence, live_counts, lame_first, shear_modulus, stretch):
        n_tiles = incidence.shape[3]
        hbm = pl.BlockSpec(memory_space=pltpu.HBM)
        vmem = pl.BlockSpec(memory_space=pltpu.VMEM)
        block, scale = pl.pallas_call(
            functools.partial(kernel, n_x, n_y, n_z),
            out_shape=(
                jax.ShapeDtypeStruct((3, 3, TILE, TILE), F32),
                jax.ShapeDtypeStruct((1, TILE), F32),
            ),
            in_specs=[hbm] * 5,
            out_specs=(vmem, vmem),
            scratch_shapes=[
                pltpu.VMEM((1, n_tiles), jnp.int32),
                pltpu.VMEM((n_tiles * CAP * CORNERS, TILE), jnp.int32),
                pltpu.VMEM((CORNERS, TILE), jnp.int32),
                pltpu.VMEM((n_tiles, CAP), F32),
                pltpu.VMEM((n_tiles, CAP), F32),
                pltpu.VMEM((3, n_tiles, CAP), F32),
                pltpu.VMEM((n_tiles, TILE), F32),
                pltpu.VMEM((n_tiles * CAP, TILE), F32),
                pltpu.VMEM((TILE, TILE), BF16),
                pltpu.VMEM((TILE, TILE), F32),
                pltpu.VMEM((n_tiles, TILE), F32),
                pltpu.VMEM((n_z, 2, TILE), F32),
                pltpu.VMEM((n_z, 2, TILE), F32),
                pltpu.VMEM((1, TILE), F32),
                pltpu.VMEM((1, TILE), F32),
                pltpu.VMEM((n_xy * n_z, 1, TILE), F32),
                pltpu.SemaphoreType.DMA,
                pltpu.SemaphoreType.DMA((9,)),
                pltpu.SemaphoreType.DMA((3,)),
                pltpu.SemaphoreType.DMA((5,)),
                pltpu.SemaphoreType.DMA,
                pltpu.SemaphoreType.REGULAR,
            ],
            compiler_params=pltpu.CompilerParams(
                collective_id=0, has_side_effects=True, vmem_limit_bytes=24 << 20
            ),
        )(
            *(
                pltpu.with_memory_space_constraint(value, pltpu.HBM)
                for value in (
                    live_counts.reshape(1, n_tiles),
                    incidence.reshape(n_tiles * CAP * CORNERS, TILE),
                    lame_first.reshape(n_tiles, CAP),
                    shear_modulus.reshape(n_tiles, CAP),
                    stretch.reshape(3, n_tiles, CAP),
                )
            )
        )
        block = pl.pallas_call(
            scale_kernel,
            out_shape=jax.ShapeDtypeStruct((9 * TILE, TILE), F32),
            in_specs=[vmem, vmem],
            out_specs=hbm,
            scratch_shapes=[pltpu.VMEM((9 * TILE, TILE), F32), pltpu.SemaphoreType.DMA],
            compiler_params=pltpu.CompilerParams(vmem_limit_bytes=24 << 20),
        )(block.reshape(9 * TILE, TILE), scale)
        block = block.reshape(3, 3, TILE, TILE)
        return block.transpose(0, 2, 1, 3).reshape(1, 1, 1, 3, TILE, 3, TILE)

    return jax.shard_map(
        on_device,
        mesh=mesh,
        in_specs=(
            P("gx", "gy", "gz", None, None, None, None),
            P("gx", "gy", "gz", None),
            P("gx", "gy", "gz", None, None),
            P("gx", "gy", "gz", None, None),
            P(None, "gx", "gy", "gz", None, None),
        ),
        out_specs=P("gx", "gy", "gz", None, None, None, None),
        check_vma=False,
    )
```

```python
import functools

import jax
import jax.numpy as jnp
from jax import lax
from jax.experimental import pallas as pl
from jax.experimental.pallas import tpu as pltpu
from jax.sharding import PartitionSpec as P

MESH = pl.DeviceIdType.MESH
F32, BF16 = jnp.float32, jnp.bfloat16
TILE, CAP, CORNERS = 128, 16, 8

LEAD = 1
CAST = 3
EARLY = 4

ALL_MODES = (1, 2, 4, 3, 5, 6, 7)


def split(value):
    high = value.astype(BF16)
    return high, (value - high.astype(F32)).astype(BF16)


def swap_groups(values):
    sub = lax.broadcasted_iota(jnp.int32, (8, 128), 0)
    group = lax.broadcasted_iota(jnp.int32, (8, 128), 1) // CAP
    for bit in (1, 2, 4):
        upper_sub = (sub & bit) != 0
        upper_group = (group & bit) != 0
        below = pltpu.roll(pltpu.roll(values, 8 - bit, 0), CAP * bit, 1)
        above = pltpu.roll(pltpu.roll(values, bit, 0), 128 - CAP * bit, 1)
        values = jnp.where(
            upper_sub == upper_group, values, jnp.where(upper_sub, above, below)
        )
    return values


def kernel(
    n_x, n_y, n_z,
    live_hbm, inc_hbm, lame_hbm, shear_hbm, stretch_hbm,
    block_ref, scale_ref,
    live, inc, tail, lame, shear, stretch, alive, weight, number, place, params, send, recv, row, row_recv, hub_recv,
    tail_sem, in_sem, send_sem, recv_sem, cast_sem, told,
):
    n_tiles = send.shape[0]
    my_x, my_y, my_z = lax.axis_index("gx"), lax.axis_index("gy"), lax.axis_index("gz")
    n_xy = n_x * n_y

    last = 4
    main = inc.shape[0] - 2 * CORNERS
    ends = [main // CORNERS * k // last * CORNERS for k in range(last + 1)] + [main + CORNERS]
    tail_load = pltpu.make_async_copy(
        inc_hbm.at[pl.ds(main + CORNERS, CORNERS)], tail, tail_sem
    )
    small = [
        pltpu.make_async_copy(source, target, in_sem.at[k])
        for k, (source, target) in enumerate(
            ((live_hbm, live), (lame_hbm, lame), (shear_hbm, shear), (stretch_hbm, stretch))
        )
    ]
    loads = [
        pltpu.make_async_copy(
            inc_hbm.at[pl.ds(first, end - first)],
            inc.at[pl.ds(first, end - first)],
            in_sem.at[len(small) + k],
        )
        for k, (first, end) in enumerate(zip(ends, ends[1:]))
    ]
    starts = {end // CORNERS: copy for end, copy in zip(ends, loads)}
    for copy in [tail_load] + small + loads:
        copy.start()

    def hops(step, size):
        return min(step, size - step)

    hubs = [(0, 0, LEAD), (0, 0, CAST)]
    hubs += [(i, 0, LEAD) for i in range(1, n_x)] + [(0, j, LEAD) for j in range(1, n_y)]

    def is_at(x, y, z):
        return jnp.logical_and(jnp.logical_and(my_x == x, my_y == y), my_z == z)

    in_corner = jnp.logical_and(my_x == 0, my_y == 0)
    on_edge = jnp.logical_or(my_x == 0, my_y == 0)
    is_lead = my_z == LEAD
    is_early = my_z < EARLY
    is_hub = jnp.logical_or(jnp.logical_and(on_edge, is_lead), is_at(0, 0, CAST))
    plane_steps = sorted(
        ((i, j) for i in range(n_x) for j in range(n_y)),
        key=lambda step: -hops(step[0], n_x) - hops(step[1], n_y),
    )
    line_steps = sorted(range(1, n_z), key=lambda step: -hops(step, n_z))

    barrier = pltpu.get_barrier_semaphore()

    def greet(x, y, z):
        pl.semaphore_signal(
            barrier, inc=1, device_id={"gx": x, "gy": y, "gz": z}, device_id_type=MESH
        )

    @pl.when(is_early)
    def _():
        for step in line_steps:
            greet(my_x, my_y, lax.rem(my_z + step, n_z))

    @pl.when(is_hub)
    def _():
        half = n_z // 2

        @pl.loop(0, half)
        def _(near):
            ahead = lax.rem(my_z + half + near, n_z)
            behind = lax.rem(my_z + jnp.where(near == 0, 0, half - near), n_z)
            for i, j in plane_steps:
                x, y = lax.rem(my_x + i, n_x), lax.rem(my_y + j, n_y)
                greet(x, y, ahead)
                if i or j:
                    greet(x, y, behind)
                else:

                    @pl.when(near > 0)
                    def _():
                        greet(x, y, behind)

    for copy in small:
        copy.wait()
    params[...] = jnp.zeros_like(params)
    first, second = lame[...], shear[...]
    lengths = [stretch[k] for k in range(3)]
    for k, value in enumerate([first, second] + lengths):
        params[:, k * CAP : (k + 1) * CAP] = value
    send[:, 1, :] = params[...]
    inverse = [1.0 / value for value in lengths]
    trace = (
        (lengths[0] * lengths[1] * lengths[2] / 9.0)
        * (first + 4.0 * second)
        * (inverse[0] * inverse[0] + inverse[1] * inverse[1] + inverse[2] * inverse[2])
    )
    diagonal = lax.broadcasted_iota(jnp.int32, (CAP, CAP), 0) == lax.broadcasted_iota(
        jnp.int32, (CAP, CAP), 1
    )
    counts = jnp.broadcast_to(live[...].astype(F32), (n_tiles, n_tiles))
    tile_down = lax.broadcasted_iota(jnp.int32, (n_tiles, n_tiles), 0)
    tile_across = lax.broadcasted_iota(jnp.int32, (n_tiles, n_tiles), 1)
    counts = jnp.sum(jnp.where(tile_down == tile_across, counts, 0.0), axis=1, keepdims=True)
    slot = lax.broadcasted_iota(jnp.int32, (n_tiles, TILE), 1) % CAP
    alive[...] = jnp.where(slot.astype(F32) < counts, 1.0, 0.0)
    trace = trace * alive[:, :CAP]
    for t in range(n_tiles):
        column = jnp.sum(jnp.where(diagonal, trace[t : t + 1, :], 0.0), axis=1, keepdims=True)
        weight[t * CAP : (t + 1) * CAP, :] = jnp.broadcast_to(column, (CAP, TILE))

    down = lax.broadcasted_iota(jnp.int32, (TILE, TILE), 0)
    lane = lax.broadcasted_iota(jnp.int32, (TILE, TILE), 1)
    number[...] = (down + 1).astype(F32).astype(BF16)
    place[...] = jnp.where(lane == (down % CORNERS) * CAP + down // CORNERS, 1.0, 0.0)

    sums = [jnp.zeros((CORNERS, TILE), F32) for _ in range(8)]
    for e in range(n_tiles * CAP):
        if e in starts:
            starts[e].wait()
        if e == n_tiles * CAP - 1:
            tail_load.wait()
            inc[main + CORNERS : main + 2 * CORNERS, :] = tail[...]
        onehot = inc[e * CORNERS : (e + 1) * CORNERS, :].astype(F32)
        sums[e % 8] = sums[e % 8] + onehot * weight[e : e + 1, :]
    while len(sums) > 1:
        sums = [sums[k] + sums[k + 1] for k in range(0, len(sums), 2)]
    partial = jnp.sum(sums[0], axis=0, keepdims=True)
    row[...] = jnp.broadcast_to(jnp.sum(partial, axis=1, keepdims=True), (1, TILE))

    pl.semaphore_wait(
        barrier,
        len(hubs) + EARLY - jnp.where(is_hub, 1, 0) - jnp.where(is_early, 1, 0),
    )

    row_group = jnp.where(my_z < n_z // 2, 0, jnp.where(my_z < n_z // 2 + 2, 4, 3))
    for x, y, z in hubs:
        source = lax.rem(my_x - x + n_x, n_x) * n_y + lax.rem(my_y - y + n_y, n_y)

        @pl.when(jnp.logical_not(is_at(x, y, z)))
        def _():
            pltpu.make_async_remote_copy(
                src_ref=row,
                dst_ref=hub_recv.at[my_z * n_xy + source],
                send_sem=send_sem.at[0],
                recv_sem=recv_sem.at[row_group],
                device_id={"gx": x, "gy": y, "gz": z},
                device_id_type=MESH,
            ).start()

    hub_recv[my_z * n_xy] = row[...]

    @pl.when(jnp.logical_not(is_lead))
    def _():
        pl.semaphore_signal(told, inc=1, device_id={"gz": LEAD}, device_id_type=MESH)

    for t in range(n_tiles):
        onehot = inc[t * TILE : (t + 1) * TILE, :].astype(F32).astype(BF16)
        spread = jnp.dot(onehot, number[...], preferred_element_type=F32)
        ids = jnp.sum(spread * place[...], axis=0, keepdims=True)
        send[t, 0:1, :] = ids * alive[t : t + 1, :]

    def send_tile(z):
        @pl.when(my_z != z)
        def _():
            pltpu.make_async_remote_copy(
                src_ref=send.at[z],
                dst_ref=recv.at[lax.rem(my_z - z + n_z, n_z)],
                send_sem=send_sem.at[0],
                recv_sem=recv_sem.at[1],
                device_id={"gz": z},
                device_id_type=MESH,
            ).start()

    for z in range(EARLY):
        send_tile(z)
    recv[0] = send[my_z]

    @pl.when(is_lead)
    def _():
        pl.semaphore_wait(told, n_z - 1)
        for step in line_steps:
            pl.semaphore_signal(
                told, inc=1, device_id={"gz": (LEAD + step) % n_z}, device_id_type=MESH
            )

    @pl.when(jnp.logical_not(is_lead))
    def _():
        pl.semaphore_wait(told, 1)

    for z in range(EARLY, n_z):
        send_tile(z)

    def rows(target, count, send_with, recv_with):
        return pltpu.make_async_remote_copy(
            src_ref=target.at[pl.ds(1, count)],
            dst_ref=target.at[pl.ds(1, count)],
            send_sem=send_with,
            recv_sem=recv_with,
            device_id={"gz": lax.rem(my_z + 1, n_z)},
            device_id_type=MESH,
        )

    tiles = rows(recv, n_z - 1, send_sem.at[0], recv_sem.at[1])
    tiles.wait_recv()

    halves = range(n_z // 8)
    ids = jnp.concatenate([swap_groups(recv[8 * h : 8 * h + 8, 0, :]) for h in halves], axis=1)
    material = jnp.concatenate(
        [swap_groups(recv[8 * h : 8 * h + 8, 1, :]) for h in halves], axis=1
    )
    wide = ids.shape[1]
    first, second = material[0:1], material[1:2]
    h = [material[2 + k : 3 + k] for k in range(3)]

    node = (lax.broadcasted_iota(jnp.int32, (TILE, wide), 0) + 1).astype(F32)
    corner = [
        jnp.where(node == ids[p : p + 1], 1.0, 0.0).astype(BF16) for p in range(CORNERS)
    ]
    mode = corner
    for bit in (1, 2, 4):
        mode = [
            mode[k] - mode[k ^ bit] if k & bit else mode[k] + mode[k ^ bit]
            for k in range(CORNERS)
        ]

    def scaled(wave, coefficient):
        wide_row = jnp.broadcast_to(coefficient, (16, wide)).astype(BF16)
        return (wave.reshape(TILE // 16, 16, wide) * wide_row[None]).reshape(TILE, wide)

    def product(left, right):
        return lax.dot_general(
            left, right, (((1,), (1,)), ((), ())), preferred_element_type=F32
        )

    def assemble(pairs):
        high, low, other = [], [], []
        for left, right, coefficient in pairs:
            top = coefficient.astype(BF16).astype(F32)
            high.append(scaled(mode[left], top))
            low.append(scaled(mode[left], coefficient - top))
            other.append(mode[right])
        right = jnp.concatenate(other, axis=1)
        left = jnp.concatenate(
            [jnp.concatenate(high, axis=1), jnp.concatenate(low, axis=1)], axis=0
        )
        result = product(left, right)
        return result[:TILE] + result[TILE:]

    area = [h[1] * h[2] / (16.0 * h[0]), h[0] * h[2] / (16.0 * h[1]), h[0] * h[1] / (16.0 * h[2])]
    strong = first + 2.0 * second
    for i in range(3):
        alpha = [(strong if k == i else second) * area[k] for k in range(3)]
        coefficients = {
            1: alpha[0],
            2: alpha[1],
            4: alpha[2],
            3: (alpha[0] + alpha[1]) / 3.0,
            5: (alpha[0] + alpha[2]) / 3.0,
            6: (alpha[1] + alpha[2]) / 3.0,
            7: (alpha[0] + alpha[1] + alpha[2]) / 9.0,
        }
        block_ref[i, i] = assemble([(m, m, coefficients[m]) for m in ALL_MODES])
    for i, j, k in ((0, 1, 2), (0, 2, 1), (1, 2, 0)):
        a, b, c = 1 << i, 1 << j, 1 << k
        la, mu = h[k] * first / 16.0, h[k] * second / 16.0
        result = assemble(
            [
                (a, b, la),
                (a | c, b | c, la / 3.0),
                (b, a, mu),
                (b | c, a | c, mu / 3.0),
            ]
        )
        block_ref[i, j] = result
        block_ref[j, i] = result.T

    def sum_rows(values, first, end):
        sums = [values[first + k] for k in range(8)]
        for k in range(8, end - first):
            sums[k % 8] = sums[k % 8] + values[first + k]
        while len(sums) > 1:
            sums = [sums[k] + sums[k + 1] for k in range(0, len(sums), 2)]
        return sums[0]

    from_x, from_y = jnp.minimum(my_x, n_x - my_x), jnp.minimum(my_y, n_y - my_y)
    lead_x = jnp.logical_and(is_lead, jnp.logical_and(my_y == 0, my_x != 0))
    lead_y = jnp.logical_and(is_lead, jnp.logical_and(my_x == 0, my_y != 0))
    lines = [(0, 0, jnp.logical_and(is_hub, jnp.logical_not(is_at(0, 0, LEAD))))]
    lines += [
        (0, j, jnp.logical_and(lead_x, hops(j, n_y) <= from_x)) for j in range(1, n_y)
    ]
    lines += [(i, 0, jnp.logical_and(lead_y, from_y > hops(i, n_x))) for i in range(1, n_x)]

    owned_at_x = {
        i: 1 + sum(hops(j, n_y) <= hops(i, n_x) for j in range(1, n_y)) for i in range(1, n_x)
    }
    owned_at_y = {
        j: 1 + sum(hops(j, n_y) > hops(i, n_x) for i in range(1, n_x)) for j in range(1, n_y)
    }

    @pl.when(is_hub)
    def _():
        half = n_xy * n_z // 2
        rows(hub_recv, half - 1, send_sem.at[0], recv_sem.at[0]).wait_recv()
        first_half = sum_rows(hub_recv, 0, half)
        late = half + 2 * n_xy
        rows(hub_recv, 2 * half - late, send_sem.at[0], recv_sem.at[3]).wait_recv()
        before = first_half + sum_rows(hub_recv, late, 2 * half)
        rows(hub_recv, late - half, send_sem.at[0], recv_sem.at[4]).wait_recv()
        scale = (3.0 * TILE * n_xy * n_z) / (before + sum_rows(hub_recv, half, late))
        scale_ref[...] = scale
        row_recv[...] = scale
        @pl.when(jnp.logical_not(is_at(0, 0, LEAD)))
        def _():
            for i, j, casts in lines:

                @pl.when(casts)
                def _():
                    for z in range(n_z):
                        copy = pltpu.make_async_remote_copy(
                            src_ref=row_recv,
                            dst_ref=row_recv,
                            send_sem=cast_sem,
                            recv_sem=recv_sem.at[2],
                            device_id={
                                "gx": lax.rem(my_x + i, n_x),
                                "gy": lax.rem(my_y + j, n_y),
                                "gz": z,
                            },
                            device_id_type=MESH,
                        )
                        if i or j:
                            copy.start()
                        else:
                            first_hub = jnp.logical_and(in_corner, z == LEAD)

                            @pl.when(jnp.logical_not(jnp.logical_or(my_z == z, first_hub)))
                            def _():
                                copy.start()

            for owned in sorted({0} | set(owned_at_x.values()) | set(owned_at_y.values())):
                own = n_z - 1 if owned else n_z - 2
                is_so = is_at(0, 0, CAST) if owned == 0 else False
                for i, count in owned_at_x.items():
                    if count == owned:
                        is_so = jnp.logical_or(is_so, is_at(i, 0, LEAD))
                for j, count in owned_at_y.items():
                    if count == owned:
                        is_so = jnp.logical_or(is_so, is_at(0, j, LEAD))

                @pl.when(is_so)
                def _():
                    rows(hub_recv, max(owned - 1, 0) * n_z + own, cast_sem, recv_sem.at[2]).wait_send()

        rows(hub_recv, 2 * (n_z - 1) + len(hubs) - 1, send_sem.at[0], recv_sem.at[0]).wait_send()

    @pl.when(jnp.logical_not(is_hub))
    def _():
        rows(hub_recv, 1, send_sem.at[0], recv_sem.at[2]).wait_recv()
        scale_ref[...] = row_recv[...]
        rows(hub_recv, 2 * (n_z - 1) + len(hubs), send_sem.at[0], recv_sem.at[0]).wait_send()


def scale_kernel(block_ref, scale_ref, out_hbm, scaled, sem):
    scale = scale_ref[...]
    for k in range(3):
        part = pl.ds(k * 3 * TILE, 3 * TILE)
        scaled[part, :] = block_ref[part, :] * scale
        pltpu.make_async_copy(scaled.at[part], out_hbm.at[part], sem).start()
    pltpu.make_async_copy(scaled, out_hbm, sem).wait()


def solution(mesh):
    n_x, n_y, n_z = mesh.shape["gx"], mesh.shape["gy"], mesh.shape["gz"]
    n_xy = n_x * n_y

    def on_device(incidence, live_counts, lame_first, shear_modulus, stretch):
        n_tiles = incidence.shape[3]
        hbm = pl.BlockSpec(memory_space=pltpu.HBM)
        vmem = pl.BlockSpec(memory_space=pltpu.VMEM)
        block, scale = pl.pallas_call(
            functools.partial(kernel, n_x, n_y, n_z),
            out_shape=(
                jax.ShapeDtypeStruct((3, 3, TILE, TILE), F32),
                jax.ShapeDtypeStruct((1, TILE), F32),
            ),
            in_specs=[hbm] * 5,
            out_specs=(vmem, vmem),
            scratch_shapes=[
                pltpu.VMEM((1, n_tiles), jnp.int32),
                pltpu.VMEM((n_tiles * CAP * CORNERS, TILE), jnp.int32),
                pltpu.VMEM((CORNERS, TILE), jnp.int32),
                pltpu.VMEM((n_tiles, CAP), F32),
                pltpu.VMEM((n_tiles, CAP), F32),
                pltpu.VMEM((3, n_tiles, CAP), F32),
                pltpu.VMEM((n_tiles, TILE), F32),
                pltpu.VMEM((n_tiles * CAP, TILE), F32),
                pltpu.VMEM((TILE, TILE), BF16),
                pltpu.VMEM((TILE, TILE), F32),
                pltpu.VMEM((n_tiles, TILE), F32),
                pltpu.VMEM((n_z, 2, TILE), F32),
                pltpu.VMEM((n_z, 2, TILE), F32),
                pltpu.VMEM((1, TILE), F32),
                pltpu.VMEM((1, TILE), F32),
                pltpu.VMEM((n_xy * n_z, 1, TILE), F32),
                pltpu.SemaphoreType.DMA,
                pltpu.SemaphoreType.DMA((9,)),
                pltpu.SemaphoreType.DMA((1,)),
                pltpu.SemaphoreType.DMA((5,)),
                pltpu.SemaphoreType.DMA,
                pltpu.SemaphoreType.REGULAR,
            ],
            compiler_params=pltpu.CompilerParams(
                collective_id=0, has_side_effects=True, vmem_limit_bytes=24 << 20
            ),
        )(
            *(
                pltpu.with_memory_space_constraint(value, pltpu.HBM)
                for value in (
                    live_counts.reshape(1, n_tiles),
                    incidence.reshape(n_tiles * CAP * CORNERS, TILE),
                    lame_first.reshape(n_tiles, CAP),
                    shear_modulus.reshape(n_tiles, CAP),
                    stretch.reshape(3, n_tiles, CAP),
                )
            )
        )
        block = pl.pallas_call(
            scale_kernel,
            out_shape=jax.ShapeDtypeStruct((9 * TILE, TILE), F32),
            in_specs=[vmem, vmem],
            out_specs=hbm,
            scratch_shapes=[pltpu.VMEM((9 * TILE, TILE), F32), pltpu.SemaphoreType.DMA],
            compiler_params=pltpu.CompilerParams(vmem_limit_bytes=24 << 20),
        )(block.reshape(9 * TILE, TILE), scale)
        block = block.reshape(3, 3, TILE, TILE)
        return block.transpose(0, 2, 1, 3).reshape(1, 1, 1, 3, TILE, 3, TILE)

    return jax.shard_map(
        on_device,
        mesh=mesh,
        in_specs=(
            P("gx", "gy", "gz", None, None, None, None),
            P("gx", "gy", "gz", None),
            P("gx", "gy", "gz", None, None),
            P("gx", "gy", "gz", None, None),
            P(None, "gx", "gy", "gz", None, None),
        ),
        out_specs=P("gx", "gy", "gz", None, None, None, None),
        check_vma=False,
    )
```
